256 devices in a mesh: rows: 4 (over y), coarse: 4 (over x_lo, core), fine: 16 (over z, x_hi).
Axes of the slice: x: 4 (x_hi: 2, x_lo: 2; x = x_hi * 2 + x_lo), y: 4, z: 8, core: 2. Of those that a mesh axis runs over, the one named last changes fastest.
Arguments:
- eigvecs: bfloat16 [2048, 32768], P('rows', ('coarse', 'fine')), may hold values from -6 to 6
- perm: int32 [32768], P(('coarse', 'fine')), may hold values from 0 to 511, as said below
- counts: int32 [64], replicated, may hold values from 1 to 256, as said below
- poles: float32 [32768], replicated, may hold values from 0 to 32768, as said below
- weights: float32 [32768], replicated, may hold values from -10 to 10, as said below
- roots: float32 [32768], P(('coarse', 'fine')), may hold values from 0 to 32768, as said below
Outputs:
- merged: bfloat16 [2048, 32768], P('rows', ('coarse', 'fine'))
The draws below stay inside these ranges and needn't reach their ends.
Inputs may be any that keep to these rules, and one draw needn't show every extreme that they name: `perm`: each aligned block of 512 entries is a permutation of 0 to 511. `counts`: at least one device has exactly 256. Every entry of poles lies 0.2 or more away from every entry of roots. `weights`: magnitudes 0.1 or more. `roots`: every entry lies 0.2 or more away from every entry of poles.
All inputs are finite; a program needn't handle non-finite values.
Results may differ from the reference program's by a relative error of at most 0.0027.
Values may be sent and summed in bfloat16 or wider, within the bound.
No kernel may reach another device: no remote copies, remote signals or barrier semaphores. Data moves between devices by JAX's collectives and lax.ppermute only.
A program may use at most 64 MiB of HBM per device.

```python
import jax
import jax.numpy as jnp
from jax import lax

COLS_DEV = 512
UNDEF_MOST = 256
DEVCOLS = 64
NODE = 32768
ROWS = 2048


def draw_perm(key, part):
    keys = jax.random.split(jax.random.fold_in(key, 5), DEVCOLS)
    blocks = jax.vmap(lambda single: jax.random.permutation(single, COLS_DEV))(keys)
    return blocks.reshape(-1).astype(jnp.int32)


def draw_counts(key, part):
    low = max(1, UNDEF_MOST // 8)
    values = jax.random.randint(jax.random.fold_in(key, 7), (DEVCOLS,), low, UNDEF_MOST + 1)
    chosen = jax.random.randint(jax.random.fold_in(key, 9), (), 0, DEVCOLS)
    return values.at[chosen].set(UNDEF_MOST).astype(jnp.int32)


def draw_poles(key, part):
    grid = jax.random.permutation(jax.random.fold_in(key, 11), NODE).astype(jnp.float32)
    jitter = jax.random.uniform(jax.random.fold_in(key, 13), (NODE,), jnp.float32, 0.0, 0.3)
    return grid + jitter


def draw_roots(key, part):
    grid = jax.random.permutation(jax.random.fold_in(key, 23), NODE).astype(jnp.float32)
    jitter = jax.random.uniform(jax.random.fold_in(key, 29), (NODE,), jnp.float32, 0.5, 0.8)
    return grid + jitter


def draw_weights(key, part):
    signs = jnp.where(jax.random.bernoulli(jax.random.fold_in(key, 31), 0.5, (NODE,)), 1.0, -1.0)
    logs = jax.random.uniform(jax.random.fold_in(key, 37), (NODE,), jnp.float32, jnp.log(0.3), jnp.log(3.0))
    return (signs * jnp.exp(logs)).astype(jnp.float32)


def levels(rng, extent, cuts, low, largest):
    def one(axis_at, blocks):
        draws = jax.random.uniform(jax.random.fold_in(jax.random.fold_in(rng, 6), axis_at), (blocks,), jnp.float32, low / len(cuts), largest / len(cuts))
        return jnp.repeat(jnp.exp(draws), extent[axis_at] // blocks).reshape((-1,) + (1,) * (len(extent) - axis_at - 1))

    level = one(*cuts[0])
    for cut in cuts[1:]:
        level = level * one(*cut)
    return level


def gaussian(key, dims, width, bound, cuts=(), kind=jnp.bfloat16):
    drawn = jax.random.normal(key, dims, jnp.float32) * width
    if len(cuts) > 0:
        drawn = levels(key, dims, cuts, -0.22, 0.18) * drawn
    return jnp.clip(drawn, min=-bound, max=bound).astype(kind)


def setup_inputs(seed: int = 0) -> dict:
    seeds = jax.random.split(jax.random.key(seed), 7)
    return {
        "eigvecs": gaussian(seeds[0], (ROWS, NODE), 1.0, 6.0, ((0, 4), (1, 64))),
        "perm": draw_perm(jax.random.fold_in(seeds[6], 71), 0),
        "counts": draw_counts(jax.random.fold_in(seeds[6], 71), 0),
        "poles": draw_poles(jax.random.fold_in(seeds[6], 71), 0),
        "weights": draw_weights(jax.random.fold_in(seeds[6], 71), 0),
        "roots": draw_roots(jax.random.fold_in(seeds[6], 71), 0),
    }


def reference(eigvecs, perm, counts, poles, weights, roots):
    order_total = eigvecs.shape[1]
    device_count = counts.shape[0]
    columns_dev = order_total // device_count
    positions = jnp.arange(order_total, dtype=jnp.int32)
    owners = positions // columns_dev
    gathered_ids = (owners * columns_dev + perm).astype(jnp.int32)
    permuted = jnp.take(eigvecs, gathered_ids, axis=1)
    within = positions % columns_dev
    factor = jnp.where(within < counts[owners], weights, jnp.zeros_like(weights))

    def column_block(device):
        offset = (device * columns_dev).astype(jnp.int32)
        own_roots = lax.dynamic_slice_in_dim(roots, offset, UNDEF_MOST)
        cauchy = factor[:, None] / (poles[:, None] - own_roots[None, :])
        norm = jnp.sqrt(lax.optimization_barrier(jnp.sum(cauchy * cauchy, axis=0)))
        summed = jnp.dot(permuted, cauchy.astype(jnp.bfloat16), preferred_element_type=jnp.float32)
        updated = summed / norm[None, :]
        leading = lax.dynamic_slice_in_dim(permuted, offset, UNDEF_MOST, 1)
        retain = jnp.arange(UNDEF_MOST, dtype=jnp.int32) < counts[device]
        return jnp.where(retain[None, :], updated, leading.astype(jnp.float32)).astype(jnp.bfloat16)
    heads = lax.map(column_block, jnp.arange(device_count, dtype=jnp.int32))
    row_count = eigvecs.shape[0]
    rest = permuted.reshape(row_count, device_count, columns_dev)[:, :, UNDEF_MOST:]
    joined = jnp.concatenate([jnp.transpose(heads, (1, 0, 2)), rest], axis=2)
    return joined.reshape(row_count, order_total)
```

```python
import jax
import jax.numpy as jnp
import numpy as np
from jax import lax
from jax.experimental import pallas as pl
from jax.experimental.pallas import tpu as pltpu
from jax.sharding import Mesh
from jax.sharding import PartitionSpec as P

LIVE = 256
COLS = 512
LANES = 128
ZS = 8
XS = 4
CHUNKS = ((0, 256), (256, 256))
TILE = 64

VM = pl.BlockSpec(memory_space=pltpu.VMEM)
SM = pl.BlockSpec(memory_space=pltpu.SMEM)
F32 = jnp.float32
BF16 = jnp.bfloat16


def params(mib):
    return pltpu.CompilerParams(vmem_limit_bytes=mib << 20)


def cost(flops, size):
    return pl.CostEstimate(flops=flops, transcendentals=0, bytes_accessed=size)


def xshift(a, k):
    pairs = []
    for xl in range(2):
        for xh in range(2):
            x = (2 * xh + xl + k) % XS
            pairs.append((2 * xl + xh, 2 * (x % 2) + x // 2))
    return lax.ppermute(a, ("xl", "xh"), pairs)


def zshift(a, k):
    return lax.ppermute(a, "z", [(i, (i + k) % ZS) for i in range(ZS)])


def cshift(a):
    return lax.ppermute(a, "core", [(0, 1), (1, 0)])


def permute_kernel(e_ref, perm_ref, p_ref, *x_refs):
    source = lax.broadcasted_iota(jnp.int32, (COLS, COLS), 0)
    selector = jnp.where(source == perm_ref[...], 1.0, 0.0).astype(BF16)
    for (start, size), x_ref in zip(CHUNKS, x_refs, strict=True):
        moved = jnp.dot(e_ref[start : start + size, :], selector, preferred_element_type=F32)
        p_ref[start : start + size, :] = moved.astype(BF16)
        x_ref[...] = jnp.transpose(moved[:, :LIVE]).astype(BF16)


def permute(eigvecs, perm):
    return pl.pallas_call(
        permute_kernel,
        in_specs=[VM, VM],
        out_specs=[VM] * (1 + len(CHUNKS)),
        out_shape=[jax.ShapeDtypeStruct((512, COLS), BF16)]
        + [jax.ShapeDtypeStruct((LIVE, size), BF16) for _, size in CHUNKS],
        name="permute",
        compiler_params=params(12),
        cost_estimate=cost(2 * 512**3, 3 << 19),
    )(eigvecs, perm)


def column(row):
    return jnp.transpose(jnp.broadcast_to(row, (8, LIVE)))[:, :1]


def cauchy_kernel(half, me_ref, counts_ref, poles_ref, weights_ref, *refs):
    r_refs, c_ref = refs[:-1], refs[-1]
    me = me_ref[0]
    z = (me // 2) % ZS
    lane = lax.broadcasted_iota(jnp.int32, (1, LANES), 1)
    for d in range(ZS):
        block = me + 2 * ((z + d) % ZS - z)
        live = counts_ref[block]
        for h in range(LIVE // LANES):
            at = 4 * block + h
            pole = poles_ref[pl.ds(at, 1), :]
            factor = jnp.where(lane + h * LANES < live, weights_ref[pl.ds(at, 1), :], 0.0)
            lo = d * LIVE + h * LANES
            for j, r_ref in enumerate(r_refs):
                roots = column(r_ref[:, half * LIVE : (half + 1) * LIVE])
                value = factor / (pole - roots)
                c_ref[j * LIVE : (j + 1) * LIVE, lo : lo + LANES] = value.astype(BF16)


def cauchy(half, me, counts, poles, weights, roots):
    return pl.pallas_call(
        lambda *refs: cauchy_kernel(half, *refs),
        in_specs=[SM, SM, VM, VM] + [VM] * XS,
        out_specs=VM,
        out_shape=pltpu.VMEM((XS * LIVE, ZS * LIVE), BF16),
        name="cauchy",
        compiler_params=params(12),
        cost_estimate=cost(XS * LIVE * ZS * LIVE * 400, 4 << 20),
    )(me, counts, poles, weights, *roots)


def norm_kernel(counts_ref, poles_ref, weights_ref, r_ref, n_ref):
    roots = column(r_ref[...])
    lane = lax.broadcasted_iota(jnp.int32, (1, LANES), 1)
    blocks = counts_ref.shape[0]
    for t in range(LIVE // TILE):
        own = jnp.broadcast_to(roots[t * TILE : (t + 1) * TILE], (TILE, LANES))

        def step(block, total):
            live = counts_ref[block]
            for h in range(LIVE // LANES):
                at = 4 * block + h
                factor = jnp.where(lane + h * LANES < live, weights_ref[pl.ds(at, 1), :], 0.0)
                value = factor / (poles_ref[pl.ds(at, 1), :] - own)
                total = total + value * value
            return total

        total = lax.fori_loop(0, blocks, step, jnp.zeros((TILE, LANES), F32), unroll=4)
        norm = jnp.sqrt(jnp.sum(total, axis=1, keepdims=True))
        n_ref[t * TILE : (t + 1) * TILE, :] = jnp.broadcast_to(norm, (TILE, LANES))


def norms(counts, poles, weights, roots):
    return pl.pallas_call(
        norm_kernel,
        in_specs=[SM, VM, VM, VM],
        out_specs=VM,
        out_shape=jax.ShapeDtypeStruct((LIVE, LANES), F32),
        name="norms",
        compiler_params=params(4),
        cost_estimate=cost(LIVE * 64 * LIVE * 400, 1 << 18),
    )(counts, poles, weights, roots)


def product_kernel(c_ref, *refs):
    x_refs, o_ref = refs[:-1], refs[-1]
    for j in range(XS):
        total = None
        for d, x_ref in enumerate(x_refs):
            piece = jnp.dot(
                c_ref[j * LIVE : (j + 1) * LIVE, d * LIVE : (d + 1) * LIVE],
                x_ref[...],
                preferred_element_type=F32,
            )
            total = piece if total is None else total + piece
        o_ref[j * LIVE : (j + 1) * LIVE, :] = total.astype(o_ref.dtype)


def product(c, pieces, kind):
    size = pieces[0].shape[1]
    return pl.pallas_call(
        product_kernel,
        in_specs=[VM] * (1 + ZS),
        out_specs=VM,
        out_shape=jax.ShapeDtypeStruct((XS * LIVE, size), kind),
        name="product",
        compiler_params=params(12),
        cost_estimate=cost(2 * XS * LIVE * ZS * LIVE * size, 6 << 20),
    )(pltpu.with_memory_space_constraint(c, pltpu.VMEM), *pieces)


def presum_kernel(mine_ref, other_ref, own_ref, *out_refs):
    own_ref[...] = mine_ref[:LIVE, :] + other_ref[:LIVE, :].astype(F32)
    for j, out_ref in enumerate(out_refs):
        part = slice((j + 1) * LIVE, (j + 2) * LIVE)
        out_ref[...] = (mine_ref[part, :] + other_ref[part, :].astype(F32)).astype(BF16)


def presum(mine, other):
    size = mine.shape[1]
    return pl.pallas_call(
        presum_kernel,
        in_specs=[VM] * 2,
        out_specs=[VM] * XS,
        out_shape=[jax.ShapeDtypeStruct((LIVE, size), F32)]
        + [jax.ShapeDtypeStruct((LIVE, size), BF16)] * (XS - 1),
        name="presum",
        compiler_params=params(8),
        cost_estimate=cost(XS * LIVE * size * 2, 2 << 20),
    )(mine, other)


def finish_kernel(count_ref, own_ref, a_ref, b_ref, c_ref, n_ref, p_ref, o_ref):
    total = own_ref[...] + a_ref[...].astype(F32) + b_ref[...].astype(F32) + c_ref[...].astype(F32)
    updated = jnp.transpose(total / n_ref[:, :1])
    within = lax.broadcasted_iota(jnp.int32, (1, LIVE), 1)
    retain = within < count_ref[0]
    o_ref[...] = jnp.where(retain, updated, p_ref[...].astype(F32)).astype(BF16)


def finish(count, own, received, norm, permuted, chunk):
    start, size = CHUNKS[chunk]
    part = pl.BlockSpec((size, LIVE), lambda i: (start // size, 0))
    whole = [pl.BlockSpec((LIVE, size), lambda i: (0, 0))] * XS
    return pl.pallas_call(
        finish_kernel,
        grid=(1,),
        in_specs=[SM] + whole + [pl.BlockSpec((LIVE, LANES), lambda i: (0, 0)), part],
        out_specs=part,
        out_shape=jax.ShapeDtypeStruct(permuted.shape, BF16),
        input_output_aliases={6: 0},
        name="finish",
        compiler_params=params(8),
        cost_estimate=cost(LIVE * size * 8, 1 << 20),
    )(count, own, *received, norm, permuted)


def per_device(eigvecs, perm, counts, poles, weights, roots):
    me = lax.axis_index(("xl", "core", "z", "xh")).astype(jnp.int32).reshape(1)
    count = lax.dynamic_slice(counts, (me[0],), (1,))
    poles = poles.reshape(-1, LANES)
    weights = weights.reshape(-1, LANES)
    permuted, *leading = permute(eigvecs, perm.reshape(1, COLS))

    own_roots = roots[:LIVE].reshape(1, LIVE)
    pair_roots = jnp.concatenate([own_roots, cshift(own_roots)], axis=1)
    all_roots = [pair_roots] + [xshift(pair_roots, -dx) for dx in range(1, XS)]

    gathered = []
    for chunk, lead in enumerate(leading):
        pieces = [None] * ZS
        pieces[0] = lead
        up = down = lead
        for s in range(1, ZS // 2):
            up, down = zshift(up, 1), zshift(down, -1)
            pieces[ZS - s], pieces[s] = up, down
        pieces[ZS // 2] = zshift(up, 1) if chunk % 2 == 0 else zshift(down, -1)
        gathered.append(pieces)

    c_other = cauchy(1, me, counts, poles, weights, all_roots)
    c_mine = cauchy(0, me, counts, poles, weights, all_roots)
    norm = norms(counts, poles, weights, own_roots)

    out = permuted
    for chunk, pieces in enumerate(gathered):
        other = cshift(product(c_other, pieces, BF16))
        mine = product(c_mine, pieces, F32)
        own, *sent = presum(mine, other)
        received = [xshift(part, dx + 1) for dx, part in enumerate(sent)]
        out = finish(count, own, received, norm, out, chunk)
    return out


def solution(mesh):
    fine_mesh = Mesh(mesh.devices.reshape(4, 2, 2, 8, 2), ("rows", "xl", "core", "z", "xh"))
    columns = ("xl", "core", "z", "xh")
    return jax.shard_map(
        per_device,
        mesh=fine_mesh,
        in_specs=(P("rows", columns), P(columns), P(), P(), P(), P(columns)),
        out_specs=P("rows", columns),
        check_vma=False,
    )
```

```python
import jax
import jax.numpy as jnp
from jax import lax
from jax.experimental import pallas as pl
from jax.experimental.pallas import tpu as pltpu
from jax.sharding import Mesh
from jax.sharding import PartitionSpec as P

LIVE = 256
COLS = 512
LANES = 128
ZS = 8
XS = 4
CHUNKS = ((0, 256), (256, 256))
TILE = 128

VM = pl.BlockSpec(memory_space=pltpu.VMEM)
HB = pl.BlockSpec(memory_space=pltpu.HBM)
SM = pl.BlockSpec(memory_space=pltpu.SMEM)
F32 = jnp.float32
BF16 = jnp.bfloat16


def params(mib):
    return pltpu.CompilerParams(vmem_limit_bytes=mib << 20)


def cost(flops, size):
    return pl.CostEstimate(flops=1, transcendentals=0, bytes_accessed=1)


def xflip(a, mask):
    partner = 2 * (mask % 2) + mask // 2
    return lax.ppermute(a, ("xl", "xh"), [(i, i ^ partner) for i in range(XS)])


def zshift(a, k):
    return lax.ppermute(a, "z", [(i, (i + k) % ZS) for i in range(ZS)])


def cshift(a):
    return lax.ppermute(a, "core", [(0, 1), (1, 0)])


def hold(a, *others):
    return lax.optimization_barrier((a, *others))[0]


def in_hbm(a):
    return pltpu.with_memory_space_constraint(a, pltpu.HBM)


def permute_kernel(e_hbm, perm_ref, lead_ref, rest_ref, *refs):
    x_refs, e_ref, sem = refs[: len(CHUNKS)], refs[-2], refs[-1]
    copies = []
    for i, (start, size) in enumerate(CHUNKS):
        part = pl.ds(start, size)
        copies.append(pltpu.make_async_copy(e_hbm.at[part, :], e_ref.at[part, :], sem.at[i]))
        copies[-1].start()
    source = lax.broadcasted_iota(jnp.int32, (COLS, COLS), 0)
    selector = jnp.where(source == perm_ref[...], 1.0, 0.0).astype(BF16)
    for copy, (start, size), x_ref in zip(copies, CHUNKS, x_refs, strict=True):
        copy.wait()
        rows = slice(start, start + size)
        moved = jnp.dot(e_ref[rows, :], selector, preferred_element_type=F32)
        x_ref[...] = jnp.transpose(moved[:, :LIVE]).astype(BF16)
        lead_ref[rows, :] = moved[:, :LIVE].astype(BF16)
        rest_ref[rows, :] = moved[:, LIVE:].astype(BF16)


def permute(eigvecs, perm):
    rows = eigvecs.shape[0]
    return pl.pallas_call(
        permute_kernel,
        in_specs=[HB, VM],
        out_specs=[VM] * (2 + len(CHUNKS)),
        out_shape=[pltpu.VMEM((rows, LIVE), BF16), pltpu.VMEM((rows, COLS - LIVE), BF16)]
        + [pltpu.VMEM((LIVE, size), BF16) for _, size in CHUNKS],
        scratch_shapes=[pltpu.VMEM(eigvecs.shape, BF16), pltpu.SemaphoreType.DMA((len(CHUNKS),))],
        name="permute",
        compiler_params=params(8),
        cost_estimate=cost(2 * 512 * 512 * COLS, 1 << 20),
    )(eigvecs, perm)


def table_kernel(counts_ref, poles_hbm, weights_hbm, p_ref, f_ref, poles_ref, weights_ref, sem):
    first = pltpu.make_async_copy(poles_hbm, poles_ref, sem.at[0])
    second = pltpu.make_async_copy(weights_hbm, weights_ref, sem.at[1])
    first.start()
    second.start()
    first.wait()
    second.wait()
    span, keep = COLS // LANES, LIVE // LANES
    at = lax.broadcasted_iota(jnp.int32, (keep, LANES), 0) * LANES
    at = at + lax.broadcasted_iota(jnp.int32, (keep, LANES), 1)
    for block in range(counts_ref.shape[0]):
        rows = slice(keep * block, keep * (block + 1))
        here = slice(span * block, span * block + keep)
        p_ref[rows, :] = poles_ref[here, :]
        f_ref[rows, :] = jnp.where(at < counts_ref[block], weights_ref[here, :], 0.0)


def tables(counts, poles, weights):
    shape = (counts.shape[0] * LIVE // LANES, LANES)
    return pl.pallas_call(
        table_kernel,
        in_specs=[SM, HB, HB],
        out_specs=[VM, VM],
        out_shape=[pltpu.VMEM(shape, F32)] * 2,
        scratch_shapes=[pltpu.VMEM(poles.shape, F32)] * 2 + [pltpu.SemaphoreType.DMA((2,))],
        name="tables",
        compiler_params=params(4),
        cost_estimate=cost(1 << 29, 1 << 19),
    )(counts, poles, weights)


def column(row):
    return jnp.transpose(jnp.broadcast_to(row, (8, LIVE)))[:, :1]


def cauchy_kernel(half, me_ref, poles_ref, factors_ref, r_ref, c_ref):
    me = me_ref[0]
    z = (me // 2) % ZS
    tiles = LIVE // LANES
    for j in range(XS):
        b = 2 * j + half
        roots = column(r_ref[:, b * LIVE : (b + 1) * LIVE])
        for t in range(LIVE // TILE):
            own = jnp.broadcast_to(roots[t * TILE : (t + 1) * TILE], (TILE, LANES))
            rows = slice(j * LIVE + t * TILE, j * LIVE + (t + 1) * TILE)
            for d in range(ZS):
                block = me + 2 * ((z + d) % ZS - z)
                for h in range(tiles):
                    at = pl.ds(tiles * block + h, 1)
                    value = factors_ref[at, :] / (poles_ref[at, :] - own)
                    lo = (tiles * d + h) * LANES
                    c_ref[rows, lo : lo + LANES] = value.astype(BF16)


def cauchy(half, me, poles, factors, roots):
    return pl.pallas_call(
        lambda *refs: cauchy_kernel(half, *refs),
        in_specs=[SM, VM, VM, VM],
        out_specs=VM,
        out_shape=pltpu.VMEM((XS * LIVE, ZS * LIVE), BF16),
        name="cauchy",
        compiler_params=params(8),
        cost_estimate=cost(1 << 31, 4 << 20),
    )(me, poles, factors, roots)


def norm_kernel(lo, size, poles_ref, factors_ref, r_ref, n_ref):
    roots = column(r_ref[...])[lo : lo + size]
    own = jnp.broadcast_to(roots, (size, LANES))
    group = 16

    def step(g, total):
        for u in range(group):
            at = pl.ds(g * group + u, 1)
            value = factors_ref[at, :] / (poles_ref[at, :] - own)
            total = total + value * value
        return total

    total = lax.fori_loop(0, poles_ref.shape[0] // group, step, jnp.zeros((size, LANES), F32))
    norm = jnp.sqrt(jnp.sum(total, axis=1, keepdims=True))
    n_ref[...] = jnp.broadcast_to(norm, (size, LANES))


def norms(lo, size, poles, factors, roots):
    return pl.pallas_call(
        lambda *refs: norm_kernel(lo, size, *refs),
        in_specs=[VM, VM, VM],
        out_specs=VM,
        out_shape=pltpu.VMEM((size, LANES), F32),
        name="norms",
        compiler_params=params(4),
        cost_estimate=cost(1 << 31, 1 << 18),
    )(poles, factors, roots)


def product_kernel(c_ref, *refs):
    x_refs, o_ref = refs[:-1], refs[-1]
    for j in range(XS):
        total = None
        for d, x_ref in enumerate(x_refs):
            piece = jnp.dot(
                c_ref[j * LIVE : (j + 1) * LIVE, d * LIVE : (d + 1) * LIVE],
                x_ref[...],
                preferred_element_type=F32,
            )
            total = piece if total is None else total + piece
        o_ref[j * LIVE : (j + 1) * LIVE, :] = total.astype(o_ref.dtype)


def product(c, pieces, kind):
    size = pieces[0].shape[1]
    return pl.pallas_call(
        product_kernel,
        in_specs=[VM] * (1 + ZS),
        out_specs=VM,
        out_shape=pltpu.VMEM((XS * LIVE, size), kind),
        name="product",
        compiler_params=params(8),
        cost_estimate=cost(2 * XS * LIVE * ZS * LIVE * size, 6 << 20),
    )(c, *pieces)


def presum_kernel(mine_ref, other_ref, own_ref, *out_refs):
    own_ref[...] = mine_ref[:LIVE, :] + other_ref[:LIVE, :].astype(F32)
    for j, out_ref in enumerate(out_refs):
        part = slice((j + 1) * LIVE, (j + 2) * LIVE)
        out_ref[...] = (mine_ref[part, :] + other_ref[part, :].astype(F32)).astype(BF16)


def presum(mine, other):
    size = mine.shape[1]
    return pl.pallas_call(
        presum_kernel,
        in_specs=[VM] * 2,
        out_specs=[VM] * XS,
        out_shape=[pltpu.VMEM((LIVE, size), F32)] + [pltpu.VMEM((LIVE, size), BF16)] * (XS - 1),
        name="presum",
        compiler_params=params(4),
        cost_estimate=cost(XS * LIVE * size * 2, 2 << 20),
    )(mine, other)


def finish_kernel(chunk, me_ref, counts_ref, own_ref, a_ref, b_ref, c_ref, n0_ref, n1_ref, lead_ref, *refs):
    start, size = CHUNKS[chunk]
    o_hbm, buffer, sem = refs[-3:]
    copies = []
    if chunk == 0:
        rest = o_hbm.at[:, pl.ds(LIVE, COLS - LIVE)]
        copies.append(pltpu.make_async_copy(refs[0], rest, sem.at[1]))
        copies[-1].start()
    total = own_ref[...] + a_ref[...].astype(F32) + b_ref[...].astype(F32) + c_ref[...].astype(F32)
    norm = jnp.concatenate([n0_ref[:, :1], n1_ref[:, :1]], axis=0)
    updated = jnp.transpose(total / norm)
    within = lax.broadcasted_iota(jnp.int32, (1, LIVE), 1)
    retain = within < counts_ref[me_ref[0]]
    lead = lead_ref[start : start + size, :]
    buffer[...] = jnp.where(retain, updated, lead.astype(F32)).astype(BF16)
    copies.append(pltpu.make_async_copy(buffer, o_hbm.at[pl.ds(start, size), pl.ds(0, LIVE)], sem.at[0]))
    copies[-1].start()
    for copy in copies:
        copy.wait()


def finish(me, counts, own, received, norm, lead, last, chunk):
    size = CHUNKS[chunk][1]
    return pl.pallas_call(
        lambda *refs: finish_kernel(chunk, *refs),
        in_specs=[SM, SM] + [VM] * (XS + 3) + [HB if chunk else VM],
        out_specs=HB,
        out_shape=jax.ShapeDtypeStruct((lead.shape[0], COLS), BF16),
        scratch_shapes=[pltpu.VMEM((size, LIVE), BF16), pltpu.SemaphoreType.DMA((2,))],
        input_output_aliases={2 + XS + 3: 0} if chunk else {},
        name="finish",
        compiler_params=params(4),
        cost_estimate=cost(LIVE * size * 8, 1 << 20),
    )(me, counts, own, *received, *norm, lead, last)


def per_device(eigvecs, perm, counts, poles, weights, roots):
    me = lax.axis_index(("xl", "core", "z", "xh")).astype(jnp.int32).reshape(1)

    own = roots.reshape(1, COLS)
    other = cshift(own)
    lead, rest, xa, xb = permute(in_hbm(eigvecs), perm.reshape(1, COLS))
    own_roots = hold(own, xa)[:, :LIVE]
    near = jnp.concatenate([own_roots, other[:, :LIVE]], axis=1)

    a_up, a_down = [xa], [xa]
    b_up, b_down = [xb], [xb]

    def advance(up, down, *others):
        up.append(zshift(hold(up[-1], *others), 1))
        down.append(zshift(hold(down[-1], *others), -1))

    advance(a_up, a_down)
    pair = jnp.concatenate([near, xflip(near, 1)], axis=1)
    advance(b_up, b_down, pair)
    all_roots = jnp.concatenate([pair, xflip(pair, 2)], axis=1)
    pole_table, factors = tables(
        hold(counts, xa), in_hbm(poles.reshape(-1, LANES)), in_hbm(weights.reshape(-1, LANES))
    )
    advance(a_up, a_down, all_roots, factors)
    c_other = cauchy(1, me, pole_table, factors, hold(all_roots, a_up[1], a_down[1]))
    advance(b_up, b_down, c_other)
    c_mine = cauchy(0, me, pole_table, factors, hold(all_roots, b_up[1], b_down[1]))
    advance(a_up, a_down, c_mine)
    advance(b_up, b_down)
    a_last = zshift(a_up[3], 1)
    b_last = zshift(b_down[3], -1)

    def order(up, down, last):
        return [up[0], down[1], down[2], down[3], last, up[3], up[2], up[1]]

    half = LIVE // 2
    a_all, b_all = order(a_up, a_down, a_last), order(b_up, b_down, b_last)
    a_other = cshift(product(c_other, a_all, BF16))
    a_mine = product(c_mine, a_all, F32)
    b_all[0] = hold(b_all[0], a_mine)
    b_other = cshift(product(c_other, b_all, BF16))
    a_own, *a_sent = presum(a_mine, a_other)
    a_recv = [xflip(part, i + 1) for i, part in enumerate(a_sent)]
    b_all[0] = hold(b_all[0], a_own)
    b_mine = product(c_mine, b_all, F32)
    b_own, *b_sent = presum(b_mine, b_other)
    b_recv = [xflip(part, i + 1) for i, part in enumerate(b_sent)]
    norm0 = norms(0, half, hold(pole_table, a_own, b_mine), factors, own_roots)
    norm1 = norms(half, half, hold(pole_table, b_own), factors, own_roots)
    norm = (norm0, norm1)
    out = finish(me, counts, a_own, a_recv, norm, lead, rest, 0)
    return finish(me, counts, b_own, b_recv, norm, lead, out, 1)


def solution(mesh):
    fine_mesh = Mesh(mesh.devices.reshape(4, 2, 2, 8, 2), ("rows", "xl", "core", "z", "xh"))
    columns = ("xl", "core", "z", "xh")
    return jax.shard_map(
        per_device,
        mesh=fine_mesh,
        in_specs=(P("rows", columns), P(columns), P(), P(), P(), P(columns)),
        out_specs=P("rows", columns),
        check_vma=False,
    )
```

```python
import jax
import jax.numpy as jnp
from jax import lax
from jax.experimental import pallas as pl
from jax.experimental.pallas import tpu as pltpu
from jax.sharding import Mesh
from jax.sharding import PartitionSpec as P

LIVE = 256
COLS = 512
LANES = 128
TILES = LIVE // LANES
ZS = 8
XS = 4
TILE = 128
OTHER = range(7)
MINE = range(9)

VM = pl.BlockSpec(memory_space=pltpu.VMEM)
HB = pl.BlockSpec(memory_space=pltpu.HBM)
SM = pl.BlockSpec(memory_space=pltpu.SMEM)
F32 = jnp.float32
BF16 = jnp.bfloat16


def params(mib):
    return pltpu.CompilerParams(vmem_limit_bytes=mib << 20)


TINY = pl.CostEstimate(flops=1, transcendentals=0, bytes_accessed=1)
LONG = pl.CostEstimate(flops=10**10, transcendentals=0, bytes_accessed=1)


def xflip(a, mask):
    partner = 2 * (mask % 2) + mask // 2
    return lax.ppermute(a, ("xl", "xh"), [(i, i ^ partner) for i in range(XS)])


def around(a, way):
    up = [(z, (z + way) % ZS) for z in range(ZS)]
    down = [(ZS + z, ZS + (z - way) % ZS) for z in range(ZS)]
    return lax.ppermute(a, ("core", "z"), up + down)


def cshift(a):
    return lax.ppermute(a, "core", [(0, 1), (1, 0)])


def hold(a, *others):
    return lax.optimization_barrier((a, *others))[0]


def in_hbm(a):
    return pltpu.with_memory_space_constraint(a, pltpu.HBM)


def permute_kernel(e_hbm, perm_ref, x_ref, lead_ref, rest_ref, e_ref, sem):
    rows = e_ref.shape[0]
    half = rows // 2
    copies = []
    for i in range(2):
        part = pl.ds(i * half, half)
        copies.append(pltpu.make_async_copy(e_hbm.at[part, :], e_ref.at[part, :], sem.at[i]))
        copies[-1].start()
    source = lax.broadcasted_iota(jnp.int32, (COLS, COLS), 0)
    selector = jnp.where(source == perm_ref[...], 1.0, 0.0).astype(BF16)
    for i, copy in enumerate(copies):
        copy.wait()
        part = slice(i * half, (i + 1) * half)
        moved = jnp.dot(e_ref[part, :], selector, preferred_element_type=F32)
        x_ref[:, part] = jnp.transpose(moved[:, :LIVE]).astype(BF16)
        lead_ref[part, :] = moved[:, :LIVE].astype(BF16)
        rest_ref[part, :] = moved[:, LIVE:].astype(BF16)


def permute(eigvecs, perm):
    rows = eigvecs.shape[0]
    return pl.pallas_call(
        permute_kernel,
        in_specs=[HB, VM],
        out_specs=[VM] * 3,
        out_shape=[
            pltpu.VMEM((LIVE, rows), BF16),
            pltpu.VMEM((rows, LIVE), BF16),
            pltpu.VMEM((rows, COLS - LIVE), BF16),
        ],
        scratch_shapes=[pltpu.VMEM(eigvecs.shape, BF16), pltpu.SemaphoreType.DMA((2,))],
        name="permute",
        compiler_params=params(8),
        cost_estimate=TINY,
    )(eigvecs, perm)


def table_kernel(counts_ref, poles_hbm, weights_hbm, p_ref, f_ref, poles_ref, weights_ref, sem):
    first = pltpu.make_async_copy(poles_hbm, poles_ref, sem.at[0])
    second = pltpu.make_async_copy(weights_hbm, weights_ref, sem.at[1])
    first.start()
    second.start()
    first.wait()
    second.wait()
    span, keep = COLS // LANES, LIVE // LANES
    at = lax.broadcasted_iota(jnp.int32, (keep, LANES), 0) * LANES
    at = at + lax.broadcasted_iota(jnp.int32, (keep, LANES), 1)
    for block in range(counts_ref.shape[0]):
        rows = slice(keep * block, keep * (block + 1))
        here = slice(span * block, span * block + keep)
        p_ref[rows, :] = poles_ref[here, :]
        f_ref[rows, :] = jnp.where(at < counts_ref[block], weights_ref[here, :], 0.0)


def tables(counts, poles, weights):
    shape = (counts.shape[0] * LIVE // LANES, LANES)
    return pl.pallas_call(
        table_kernel,
        in_specs=[SM, HB, HB],
        out_specs=[VM, VM],
        out_shape=[pltpu.VMEM(shape, F32)] * 2,
        scratch_shapes=[pltpu.VMEM(poles.shape, F32)] * 2 + [pltpu.SemaphoreType.DMA((2,))],
        name="tables",
        compiler_params=params(4),
        cost_estimate=TINY,
    )(counts, poles, weights)


def column(row):
    return jnp.transpose(jnp.broadcast_to(row, (8, LIVE)))[:, :1]


def cauchy_kernel(fc, pieces, me_ref, poles_ref, factors_ref, r_ref, c_ref):
    me = me_ref[0]
    xl, core, z, xh = me // 32, (me // 16) % 2, (me // 2) % ZS, me % 2
    step = 1 - 2 * core
    for j in range(XS):
        row = 4 * (xl ^ (j % 2)) + 2 * (core ^ fc) + (xh ^ (j // 2))
        roots = column(r_ref[pl.ds(row, 1), :LIVE])
        for t in range(LIVE // TILE):
            own = jnp.broadcast_to(roots[t * TILE : (t + 1) * TILE], (TILE, LANES))
            rows = slice(j * LIVE + t * TILE, j * LIVE + (t + 1) * TILE)
            for i, d in enumerate(pieces):
                away = (d + 1) // 2
                ring = (z + 4) % ZS if d >= 7 else (z + (1 - 2 * (d % 2)) * step * away + ZS) % ZS
                block = me + 2 * (ring - z)
                if d == 8:
                    block = block + 16 * step
                for h in range(TILES):
                    at = pl.ds(TILES * block + h, 1)
                    value = factors_ref[at, :] / (poles_ref[at, :] - own)
                    lo = (TILES * i + h) * LANES
                    c_ref[rows, lo : lo + LANES] = value.astype(BF16)


def cauchy(fc, pieces, me, poles, factors, roots):
    return pl.pallas_call(
        lambda *refs: cauchy_kernel(fc, pieces, *refs),
        in_specs=[SM, VM, VM, VM],
        out_specs=VM,
        out_shape=pltpu.VMEM((XS * LIVE, len(pieces) * LIVE), BF16),
        name="cauchy",
        compiler_params=params(8),
        cost_estimate=TINY,
    )(me, poles, factors, roots)


def norm_kernel(poles_ref, factors_ref, r_ref, rest_ref, n_ref, o_hbm, sem):
    copy = pltpu.make_async_copy(rest_ref, o_hbm.at[:, pl.ds(LIVE, COLS - LIVE)], sem.at[0])
    copy.start()
    roots = column(r_ref[:, :LIVE])
    group = 16
    for t in range(LIVE // TILE):
        own = jnp.broadcast_to(roots[t * TILE : (t + 1) * TILE], (TILE, LANES))

        def step(g, total):
            for u in range(group):
                at = pl.ds(g * group + u, 1)
                value = factors_ref[at, :] / (poles_ref[at, :] - own)
                total = total + value * value
            return total

        total = lax.fori_loop(0, poles_ref.shape[0] // group, step, jnp.zeros((TILE, LANES), F32))
        norm = jnp.sqrt(jnp.sum(total, axis=1, keepdims=True))
        n_ref[t * TILE : (t + 1) * TILE, :] = jnp.broadcast_to(norm, (TILE, LANES))
    copy.wait()


def norms(poles, factors, roots, rest):
    return pl.pallas_call(
        norm_kernel,
        in_specs=[VM] * 4,
        out_specs=[VM, HB],
        out_shape=[
            pltpu.VMEM((LIVE, LANES), F32),
            jax.ShapeDtypeStruct((rest.shape[0], COLS), BF16),
        ],
        scratch_shapes=[pltpu.SemaphoreType.DMA((1,))],
        name="norms",
        compiler_params=params(4),
        cost_estimate=TINY,
    )(poles, factors, roots, rest)


def product(c_ref, j, first, x_refs):
    total = None
    for i, x_ref in enumerate(x_refs):
        lo = (first + i) * LIVE
        part = c_ref[j * LIVE : (j + 1) * LIVE, lo : lo + LIVE]
        piece = jnp.dot(part, x_ref[...], preferred_element_type=F32)
        total = piece if total is None else total + piece
    return total


def stage_kernel(first, count, c_mine, c_other, *refs):
    x_refs, refs = refs[:count], refs[count:]
    sums, outs = refs[:-2], refs[-2:]
    for i, c_ref in enumerate((c_mine, c_other)):
        for j in range(XS):
            rows = slice(j * LIVE, (j + 1) * LIVE)
            total = product(c_ref, j, first, x_refs)
            if sums:
                total = total + sums[i][rows, :]
            outs[i][rows, :] = total.astype(outs[i].dtype)


def stage(first, c_mine, c_other, pieces, sums, last):
    shape = (XS * LIVE, pieces[0].shape[1])
    return pl.pallas_call(
        lambda *refs: stage_kernel(first, len(pieces), *refs),
        in_specs=[VM] * (2 + len(pieces) + len(sums)),
        out_specs=[VM] * 2,
        out_shape=[pltpu.VMEM(shape, F32), pltpu.VMEM(shape, BF16 if last else F32)],
        name="stage",
        compiler_params=params(8),
        cost_estimate=TINY,
    )(c_mine, c_other, *pieces, *sums)


def opposite_kernel(c_ref, x_ref, sum_ref, o_ref):
    for j in range(XS):
        rows = slice(j * LIVE, (j + 1) * LIVE)
        o_ref[rows, :] = sum_ref[rows, :] + product(c_ref, j, 7, (x_ref,))


def add_opposite(c_mine, piece, mine):
    return pl.pallas_call(
        opposite_kernel,
        in_specs=[VM] * 3,
        out_specs=VM,
        out_shape=pltpu.VMEM(mine.shape, F32),
        name="add_opposite",
        compiler_params=params(8),
        cost_estimate=LONG,
    )(c_mine, piece, mine)


def total_kernel(c_ref, x_ref, mine_ref, other_ref, own_ref, *out_refs):
    for j, out_ref in enumerate((own_ref, *out_refs)):
        rows = slice(j * LIVE, (j + 1) * LIVE)
        total = product(c_ref, j, 8, (x_ref,))
        total = total + mine_ref[rows, :] + other_ref[rows, :].astype(F32)
        out_ref[...] = total.astype(out_ref.dtype)


def totals(c_mine, sibling, mine, other):
    shape = (LIVE, mine.shape[1])
    return pl.pallas_call(
        total_kernel,
        in_specs=[VM] * 4,
        out_specs=[VM] * XS,
        out_shape=[pltpu.VMEM(shape, F32)] + [pltpu.VMEM(shape, BF16)] * (XS - 1),
        name="totals",
        compiler_params=params(8),
        cost_estimate=TINY,
    )(c_mine, sibling, mine, other)


def finish_kernel(me_ref, counts_ref, own_ref, a_ref, b_ref, c_ref, n_ref, lead_ref, _, o_hbm, buffer, sem):
    within = lax.broadcasted_iota(jnp.int32, (1, LIVE), 1)
    retain = within < counts_ref[me_ref[0]]
    norm = n_ref[:, :1]
    half = buffer.shape[0] // 2
    copies = []
    for i in range(2):
        part = slice(i * half, (i + 1) * half)
        total = own_ref[:, part] + a_ref[:, part].astype(F32)
        total = total + b_ref[:, part].astype(F32) + c_ref[:, part].astype(F32)
        updated = jnp.transpose(total / norm)
        lead = lead_ref[part, :].astype(F32)
        buffer[part, :] = jnp.where(retain, updated, lead).astype(BF16)
        rows = pl.ds(i * half, half)
        copies.append(
            pltpu.make_async_copy(buffer.at[rows, :], o_hbm.at[rows, pl.ds(0, LIVE)], sem.at[i])
        )
        copies[-1].start()
    for copy in copies:
        copy.wait()


def finish(me, counts, own, received, norm, lead, out):
    return pl.pallas_call(
        finish_kernel,
        in_specs=[SM, SM] + [VM] * (XS + 2) + [HB],
        out_specs=HB,
        out_shape=jax.ShapeDtypeStruct(out.shape, BF16),
        scratch_shapes=[pltpu.VMEM(lead.shape, BF16), pltpu.SemaphoreType.DMA((2,))],
        input_output_aliases={4 + XS: 0},
        name="finish",
        compiler_params=params(4),
        cost_estimate=TINY,
    )(me, counts, own, *received, norm, lead, out)


def per_device(eigvecs, perm, counts, poles, weights, roots):
    me = lax.axis_index(("xl", "core", "z", "xh")).astype(jnp.int32).reshape(1)
    roots = roots.reshape(1, COLS)
    all_roots = lax.all_gather(roots, ("xl", "core", "xh"), axis=0, tiled=True)

    own, lead, rest = permute(in_hbm(eigvecs), perm.reshape(1, COLS))
    table, factors = tables(
        hold(counts, own), in_hbm(poles.reshape(-1, LANES)), in_hbm(weights.reshape(-1, LANES))
    )
    p1 = around(own, 1)
    p2 = around(own, -1)
    p3 = around(hold(p1, factors), 1)
    p4 = around(p2, -1)
    c_other = cauchy(1, OTHER, me, table, factors, hold(all_roots, p2))
    p5 = around(hold(p3, c_other), 1)
    c_mine = cauchy(0, MINE, me, table, factors, hold(all_roots, p3, c_other))
    p6 = around(hold(p4, c_mine), -1)
    sums = stage(0, c_mine, c_other, (own, p1, p2, p3, p4), (), False)
    p7 = around(hold(p5, sums[0]), 1)
    mine, other = stage(5, c_mine, c_other, (p5, p6), sums, True)
    other = cshift(other)
    sibling = cshift(p7)
    mine = add_opposite(c_mine, p7, mine)
    own_sum, *sent = totals(c_mine, sibling, mine, other)
    received = [xflip(part, i + 1) for i, part in enumerate(sent)]
    norm, out = norms(table, factors, hold(roots, own_sum), rest)
    return finish(me, counts, own_sum, received, norm, lead, out)


def solution(mesh):
    fine_mesh = Mesh(mesh.devices.reshape(4, 2, 2, 8, 2), ("rows", "xl", "core", "z", "xh"))
    columns = ("xl", "core", "z", "xh")
    return jax.shard_map(
        per_device,
        mesh=fine_mesh,
        in_specs=(P("rows", columns), P(columns), P(), P(), P(), P(columns)),
        out_specs=P("rows", columns),
        check_vma=False,
    )
```

```python
import jax
import jax.numpy as jnp
from jax import lax
from jax.experimental import pallas as pl
from jax.experimental.pallas import tpu as pltpu
from jax.sharding import Mesh
from jax.sharding import PartitionSpec as P

LIVE = 256
COLS = 512
LANES = 128
TILES = LIVE // LANES
ZS = 8
XS = 4
TILE = 128
OTHER = range(7)
MINE = range(9)

VM = pl.BlockSpec(memory_space=pltpu.VMEM)
HB = pl.BlockSpec(memory_space=pltpu.HBM)
SM = pl.BlockSpec(memory_space=pltpu.SMEM)
F32 = jnp.float32
BF16 = jnp.bfloat16


def params(mib):
    return pltpu.CompilerParams(vmem_limit_bytes=mib << 20)


TINY = pl.CostEstimate(flops=1, transcendentals=0, bytes_accessed=1)
LONG = pl.CostEstimate(flops=10**10, transcendentals=0, bytes_accessed=1)


def xflip(a, mask):
    partner = 2 * (mask % 2) + mask // 2
    return lax.ppermute(a, ("xl", "xh"), [(i, i ^ partner) for i in range(XS)])


def neighbours(a, first):
    pairs = []
    for i in range(2 * XS):
        xl, core, xh = i // 4, (i // 2) % 2, i % 2
        flip = core if first else 1 - core
        pairs.append((i, 4 * (1 - xl) + 2 * core + (xh ^ flip)))
    return lax.ppermute(a, ("xl", "core", "xh"), pairs)


def around(a, way):
    up = [(z, (z + way) % ZS) for z in range(ZS)]
    down = [(ZS + z, ZS + (z - way) % ZS) for z in range(ZS)]
    return lax.ppermute(a, ("core", "z"), up + down)


def cshift(a):
    return lax.ppermute(a, "core", [(0, 1), (1, 0)])


def hold(a, *others):
    return lax.optimization_barrier((a, *others))[0]


def in_hbm(a):
    return pltpu.with_memory_space_constraint(a, pltpu.HBM)


def permute_kernel(e_hbm, perm_ref, x_ref, lead_ref, rest_ref, e_ref, sem):
    rows = e_ref.shape[0]
    half = rows // 2
    copies = []
    for i in range(2):
        part = pl.ds(i * half, half)
        copies.append(pltpu.make_async_copy(e_hbm.at[part, :], e_ref.at[part, :], sem.at[i]))
        copies[-1].start()
    source = lax.broadcasted_iota(jnp.int32, (COLS, COLS), 0)
    selector = jnp.where(source == perm_ref[...], 1.0, 0.0).astype(BF16)
    for i, copy in enumerate(copies):
        copy.wait()
        part = slice(i * half, (i + 1) * half)
        moved = jnp.dot(e_ref[part, :], selector, preferred_element_type=F32)
        x_ref[:, part] = jnp.transpose(moved[:, :LIVE]).astype(BF16)
        lead_ref[part, :] = moved[:, :LIVE].astype(BF16)
        rest_ref[part, :] = moved[:, LIVE:].astype(BF16)


def permute(eigvecs, perm):
    rows = eigvecs.shape[0]
    return pl.pallas_call(
        permute_kernel,
        in_specs=[HB, VM],
        out_specs=[VM] * 3,
        out_shape=[
            pltpu.VMEM((LIVE, rows), BF16),
            pltpu.VMEM((rows, LIVE), BF16),
            pltpu.VMEM((rows, COLS - LIVE), BF16),
        ],
        scratch_shapes=[pltpu.VMEM(eigvecs.shape, BF16), pltpu.SemaphoreType.DMA((2,))],
        name="permute",
        compiler_params=params(8),
        cost_estimate=TINY,
    )(eigvecs, perm)


def table_kernel(counts_ref, poles_hbm, weights_hbm, p_ref, f_ref, poles_ref, weights_ref, sem):
    first = pltpu.make_async_copy(poles_hbm, poles_ref, sem.at[0])
    second = pltpu.make_async_copy(weights_hbm, weights_ref, sem.at[1])
    first.start()
    second.start()
    first.wait()
    second.wait()
    span, keep = COLS // LANES, LIVE // LANES
    at = lax.broadcasted_iota(jnp.int32, (keep, LANES), 0) * LANES
    at = at + lax.broadcasted_iota(jnp.int32, (keep, LANES), 1)
    for block in range(counts_ref.shape[0]):
        rows = slice(keep * block, keep * (block + 1))
        here = slice(span * block, span * block + keep)
        p_ref[rows, :] = poles_ref[here, :]
        f_ref[rows, :] = jnp.where(at < counts_ref[block], weights_ref[here, :], 0.0)


def tables(counts, poles, weights):
    shape = (counts.shape[0] * LIVE // LANES, LANES)
    return pl.pallas_call(
        table_kernel,
        in_specs=[SM, HB, HB],
        out_specs=[VM, VM],
        out_shape=[pltpu.VMEM(shape, F32)] * 2,
        scratch_shapes=[pltpu.VMEM(poles.shape, F32)] * 2 + [pltpu.SemaphoreType.DMA((2,))],
        name="tables",
        compiler_params=params(4),
        cost_estimate=TINY,
    )(counts, poles, weights)


def column(row):
    return jnp.transpose(jnp.broadcast_to(row, (8, LIVE)))[:, :1]


def cauchy_kernel(fc, pieces, me_ref, poles_ref, factors_ref, r_ref, c_ref):
    me = me_ref[0]
    core, z = (me // 16) % 2, (me // 2) % ZS
    step = 1 - 2 * core
    for j in range(XS):
        mask = 2 - (1 - 2 * fc) * step * (2 - j) if j % 2 else j
        lo = pl.multiple_of((2 * mask + fc) * LIVE, LIVE)
        roots = column(r_ref[:, pl.ds(lo, LIVE)])
        for t in range(LIVE // TILE):
            own = jnp.broadcast_to(roots[t * TILE : (t + 1) * TILE], (TILE, LANES))
            rows = slice(j * LIVE + t * TILE, j * LIVE + (t + 1) * TILE)
            for i, d in enumerate(pieces):
                away = (d + 1) // 2
                ring = (z + 4) % ZS if d >= 7 else (z + (1 - 2 * (d % 2)) * step * away + ZS) % ZS
                block = me + 2 * (ring - z)
                if d == 8:
                    block = block + 16 * step
                for h in range(TILES):
                    at = pl.ds(TILES * block + h, 1)
                    value = factors_ref[at, :] / (poles_ref[at, :] - own)
                    lo = (TILES * i + h) * LANES
                    c_ref[rows, lo : lo + LANES] = value.astype(BF16)


def cauchy(fc, pieces, me, poles, factors, roots):
    return pl.pallas_call(
        lambda *refs: cauchy_kernel(fc, pieces, *refs),
        in_specs=[SM, VM, VM, VM],
        out_specs=VM,
        out_shape=pltpu.VMEM((XS * LIVE, len(pieces) * LIVE), BF16),
        name="cauchy",
        compiler_params=params(8),
        cost_estimate=TINY,
    )(me, poles, factors, roots)


def norm_kernel(poles_ref, factors_ref, r_ref, rest_ref, n_ref, o_hbm, sem):
    copy = pltpu.make_async_copy(rest_ref, o_hbm.at[:, pl.ds(LIVE, COLS - LIVE)], sem.at[0])
    copy.start()
    roots = column(r_ref[:, :LIVE])
    group = 16
    for t in range(LIVE // TILE):
        own = jnp.broadcast_to(roots[t * TILE : (t + 1) * TILE], (TILE, LANES))

        def step(g, total):
            for u in range(group):
                at = pl.ds(g * group + u, 1)
                value = factors_ref[at, :] / (poles_ref[at, :] - own)
                total = total + value * value
            return total

        total = lax.fori_loop(0, poles_ref.shape[0] // group, step, jnp.zeros((TILE, LANES), F32))
        norm = jnp.sqrt(jnp.sum(total, axis=1, keepdims=True))
        n_ref[t * TILE : (t + 1) * TILE, :] = jnp.broadcast_to(norm, (TILE, LANES))
    copy.wait()


def norms(poles, factors, roots, rest):
    return pl.pallas_call(
        norm_kernel,
        in_specs=[VM] * 4,
        out_specs=[VM, HB],
        out_shape=[
            pltpu.VMEM((LIVE, LANES), F32),
            jax.ShapeDtypeStruct((rest.shape[0], COLS), BF16),
        ],
        scratch_shapes=[pltpu.SemaphoreType.DMA((1,))],
        name="norms",
        compiler_params=params(4),
        cost_estimate=TINY,
    )(poles, factors, roots, rest)


def product(c_ref, j, first, x_refs):
    total = None
    for i, x_ref in enumerate(x_refs):
        lo = (first + i) * LIVE
        part = c_ref[j * LIVE : (j + 1) * LIVE, lo : lo + LIVE]
        piece = jnp.dot(part, x_ref[...], preferred_element_type=F32)
        total = piece if total is None else total + piece
    return total


def stage_kernel(first, count, c_mine, c_other, *refs):
    x_refs, refs = refs[:count], refs[count:]
    sums, outs = refs[:-2], refs[-2:]
    for i, c_ref in enumerate((c_mine, c_other)):
        for j in range(XS):
            rows = slice(j * LIVE, (j + 1) * LIVE)
            total = product(c_ref, j, first, x_refs)
            if sums:
                total = total + sums[i][rows, :]
            outs[i][rows, :] = total.astype(outs[i].dtype)


def stage(first, c_mine, c_other, pieces, sums, last):
    shape = (XS * LIVE, pieces[0].shape[1])
    return pl.pallas_call(
        lambda *refs: stage_kernel(first, len(pieces), *refs),
        in_specs=[VM] * (2 + len(pieces) + len(sums)),
        out_specs=[VM] * 2,
        out_shape=[pltpu.VMEM(shape, F32), pltpu.VMEM(shape, BF16 if last else F32)],
        name="stage",
        compiler_params=params(8),
        cost_estimate=TINY,
    )(c_mine, c_other, *pieces, *sums)


def opposite_kernel(c_ref, x_ref, sum_ref, o_ref):
    for j in range(XS):
        rows = slice(j * LIVE, (j + 1) * LIVE)
        o_ref[rows, :] = sum_ref[rows, :] + product(c_ref, j, 7, (x_ref,))


def add_opposite(c_mine, piece, mine):
    return pl.pallas_call(
        opposite_kernel,
        in_specs=[VM] * 3,
        out_specs=VM,
        out_shape=pltpu.VMEM(mine.shape, F32),
        name="add_opposite",
        compiler_params=params(8),
        cost_estimate=LONG,
    )(c_mine, piece, mine)


def total_kernel(c_ref, x_ref, mine_ref, other_ref, own_ref, two_ref, last_ref):
    outs = (own_ref, two_ref.at[:LIVE, :], two_ref.at[LIVE:, :], last_ref)
    for j in (1, 2, 3, 0):
        rows = slice(j * LIVE, (j + 1) * LIVE)
        total = product(c_ref, j, 8, (x_ref,))
        total = total + mine_ref[rows, :] + other_ref[rows, :].astype(F32)
        outs[j][...] = total.astype(outs[j].dtype)


def totals(c_mine, sibling, mine, other):
    rows = mine.shape[1]
    return pl.pallas_call(
        total_kernel,
        in_specs=[VM] * 4,
        out_specs=[VM] * 3,
        out_shape=[
            pltpu.VMEM((LIVE, rows), F32),
            pltpu.VMEM((2 * LIVE, rows), BF16),
            pltpu.VMEM((LIVE, rows), F32),
        ],
        name="totals",
        compiler_params=params(8),
        cost_estimate=TINY,
    )(c_mine, sibling, mine, other)


def relay_kernel(mine_ref, got_ref, o_ref):
    o_ref[...] = (mine_ref[...] + got_ref[LIVE:, :].astype(F32)).astype(BF16)


def relay(mine, got):
    return pl.pallas_call(
        relay_kernel,
        in_specs=[VM] * 2,
        out_specs=VM,
        out_shape=pltpu.VMEM(mine.shape, BF16),
        name="relay",
        compiler_params=params(4),
        cost_estimate=TINY,
    )(mine, got)


def finish_kernel(me_ref, counts_ref, own_ref, a_ref, b_ref, n_ref, lead_ref, _, o_hbm, buffer, sem):
    within = lax.broadcasted_iota(jnp.int32, (1, LIVE), 1)
    retain = within < counts_ref[me_ref[0]]
    norm = n_ref[:, :1]
    half = buffer.shape[0] // 2
    copies = []
    for i in range(2):
        part = slice(i * half, (i + 1) * half)
        total = own_ref[:, part] + a_ref[:LIVE, part].astype(F32) + b_ref[:, part].astype(F32)
        updated = jnp.transpose(total / norm)
        lead = lead_ref[part, :].astype(F32)
        buffer[part, :] = jnp.where(retain, updated, lead).astype(BF16)
        rows = pl.ds(i * half, half)
        copies.append(
            pltpu.make_async_copy(buffer.at[rows, :], o_hbm.at[rows, pl.ds(0, LIVE)], sem.at[i])
        )
        copies[-1].start()
    for copy in copies:
        copy.wait()


def finish(me, counts, own, near, far, norm, lead, out):
    return pl.pallas_call(
        finish_kernel,
        in_specs=[SM, SM] + [VM] * 5 + [HB],
        out_specs=HB,
        out_shape=jax.ShapeDtypeStruct(out.shape, BF16),
        scratch_shapes=[pltpu.VMEM(lead.shape, BF16), pltpu.SemaphoreType.DMA((2,))],
        input_output_aliases={7: 0},
        name="finish",
        compiler_params=params(4),
        cost_estimate=TINY,
    )(me, counts, own, near, far, norm, lead, out)


def per_device(eigvecs, perm, counts, poles, weights, roots):
    me = lax.axis_index(("xl", "core", "z", "xh")).astype(jnp.int32).reshape(1)
    roots = roots.reshape(1, COLS)
    other_roots = cshift(roots)

    own, lead, rest = permute(in_hbm(eigvecs), perm.reshape(1, COLS))
    table, factors = tables(
        hold(counts, own), in_hbm(poles.reshape(-1, LANES)), in_hbm(weights.reshape(-1, LANES))
    )
    p1 = around(own, 1)
    p2 = around(own, -1)
    own_roots = hold(roots, factors)[:, :LIVE]
    near = jnp.concatenate([own_roots, other_roots[:, :LIVE]], axis=1)
    pair = jnp.concatenate([near, xflip(near, 1)], axis=1)
    p3 = around(hold(p1, near), 1)
    far = xflip(hold(pair, p1), 2)
    p4 = around(hold(p2, pair), -1)
    all_roots = jnp.concatenate([pair, far], axis=1)
    c_other = cauchy(1, OTHER, me, table, factors, hold(all_roots, p2))
    p5 = around(hold(p3, c_other), 1)
    c_mine = cauchy(0, MINE, me, table, factors, hold(all_roots, p3, c_other))
    p6 = around(hold(p4, c_mine), -1)
    sums = stage(0, c_mine, c_other, (own, p1, p2, p3, p4), (), False)
    p7 = around(hold(p5, sums[0]), 1)
    mine, other = stage(5, c_mine, c_other, (p5, p6), sums, True)
    other = cshift(other)
    sibling = cshift(p7)
    mine = add_opposite(c_mine, p7, mine)
    own_sum, two, last = totals(c_mine, sibling, mine, other)
    got = neighbours(two, True)
    norm, out = norms(table, factors, hold(roots, own_sum), rest)
    final = neighbours(relay(hold(last, norm), got), False)
    return finish(me, counts, own_sum, got, final, norm, lead, out)


def solution(mesh):
    fine_mesh = Mesh(mesh.devices.reshape(4, 2, 2, 8, 2), ("rows", "xl", "core", "z", "xh"))
    columns = ("xl", "core", "z", "xh")
    return jax.shard_map(
        per_device,
        mesh=fine_mesh,
        in_specs=(P("rows", columns), P(columns), P(), P(), P(), P(columns)),
        out_specs=P("rows", columns),
        check_vma=False,
    )
```

```python
import jax
import jax.numpy as jnp
from jax import lax
from jax.experimental import pallas as pl
from jax.experimental.pallas import tpu as pltpu
from jax.sharding import Mesh
from jax.sharding import PartitionSpec as P

LIVE = 256
COLS = 512
LANES = 128
TILES = LIVE // LANES
ZS = 8
XS = 4
TILE = 128
AWAY = (0, 1, -1, 2, -2, 3, -3, 4, 4)
OTHER = range(7)
MINE = range(9)

VM = pl.BlockSpec(memory_space=pltpu.VMEM)
HB = pl.BlockSpec(memory_space=pltpu.HBM)
SM = pl.BlockSpec(memory_space=pltpu.SMEM)
F32 = jnp.float32
BF16 = jnp.bfloat16


def params(mib):
    return pltpu.CompilerParams(vmem_limit_bytes=mib << 20)


TINY = pl.CostEstimate(flops=1, transcendentals=0, bytes_accessed=1)
LONG = pl.CostEstimate(flops=10**10, transcendentals=0, bytes_accessed=1)


def xshift(a, k):
    pairs = []
    for i in range(XS):
        xl, xh = i // 2, i % 2
        x = (2 * xh + xl + k) % XS
        pairs.append((i, 2 * (x % 2) + x // 2))
    return lax.ppermute(a, ("xl", "xh"), pairs)


def around(a, way):
    up = [(z, (z + way) % ZS) for z in range(ZS)]
    down = [(ZS + z, ZS + (z - way) % ZS) for z in range(ZS)]
    return lax.ppermute(a, ("core", "z"), up + down)


def cshift(a):
    return lax.ppermute(a, "core", [(0, 1), (1, 0)])


def hold(a, *others):
    return lax.optimization_barrier((a, *others))[0]


def in_hbm(a):
    return pltpu.with_memory_space_constraint(a, pltpu.HBM)


def permute_kernel(e_hbm, perm_hbm, x_ref, lead_ref, rest_ref, e_ref, perm_ref, sem):
    rows = e_ref.shape[0]
    half = rows // 2
    order = pltpu.make_async_copy(perm_hbm, perm_ref, sem.at[2])
    order.start()
    copies = []
    for i in range(2):
        part = pl.ds(i * half, half)
        copies.append(pltpu.make_async_copy(e_hbm.at[part, :], e_ref.at[part, :], sem.at[i]))
        copies[-1].start()
    order.wait()
    source = lax.broadcasted_iota(jnp.int32, (COLS, COLS), 0)
    selector = jnp.where(source == perm_ref[...], 1.0, 0.0).astype(BF16)
    for i, copy in enumerate(copies):
        copy.wait()
        part = slice(i * half, (i + 1) * half)
        moved = jnp.dot(e_ref[part, :], selector, preferred_element_type=F32)
        x_ref[:, part] = jnp.transpose(moved[:, :LIVE]).astype(BF16)
        lead_ref[part, :] = moved[:, :LIVE].astype(BF16)
        rest_ref[part, :] = moved[:, LIVE:].astype(BF16)


def permute(eigvecs, perm):
    rows = eigvecs.shape[0]
    return pl.pallas_call(
        permute_kernel,
        in_specs=[HB, HB],
        out_specs=[VM] * 3,
        out_shape=[
            pltpu.VMEM((LIVE, rows), BF16),
            pltpu.VMEM((rows, LIVE), BF16),
            pltpu.VMEM((rows, COLS - LIVE), BF16),
        ],
        scratch_shapes=[
            pltpu.VMEM(eigvecs.shape, BF16),
            pltpu.VMEM(perm.shape, jnp.int32),
            pltpu.SemaphoreType.DMA((3,)),
        ],
        name="permute",
        compiler_params=params(8),
        cost_estimate=TINY,
    )(eigvecs, perm)


def table_kernel(counts_hbm, poles_hbm, weights_hbm, p_ref, f_ref, poles_ref, weights_ref, counts_ref, sem):
    first = pltpu.make_async_copy(poles_hbm, poles_ref, sem.at[0])
    second = pltpu.make_async_copy(weights_hbm, weights_ref, sem.at[1])
    third = pltpu.make_async_copy(counts_hbm, counts_ref, sem.at[2])
    third.start()
    first.start()
    second.start()
    third.wait()
    first.wait()
    second.wait()
    span, keep = COLS // LANES, LIVE // LANES
    at = lax.broadcasted_iota(jnp.int32, (keep, LANES), 0) * LANES
    at = at + lax.broadcasted_iota(jnp.int32, (keep, LANES), 1)
    for block in range(counts_ref.shape[0]):
        rows = slice(keep * block, keep * (block + 1))
        here = slice(span * block, span * block + keep)
        p_ref[rows, :] = poles_ref[here, :]
        f_ref[rows, :] = jnp.where(at < counts_ref[block], weights_ref[here, :], 0.0)


def tables(counts, poles, weights):
    shape = (counts.shape[0] * LIVE // LANES, LANES)
    return pl.pallas_call(
        table_kernel,
        in_specs=[HB, HB, HB],
        out_specs=[VM, VM],
        out_shape=[pltpu.VMEM(shape, F32)] * 2,
        scratch_shapes=[pltpu.VMEM(poles.shape, F32)] * 2
        + [pltpu.SMEM(counts.shape, jnp.int32), pltpu.SemaphoreType.DMA((3,))],
        name="tables",
        compiler_params=params(4),
        cost_estimate=TINY,
    )(counts, poles, weights)


def column(row):
    return jnp.transpose(jnp.broadcast_to(row, (8, LIVE)))[:, :1]


def cauchy_kernel(fc, pieces, me_ref, poles_ref, factors_ref, near_ref, far_ref, c_ref):
    me = me_ref[0]
    core, z = (me // 16) % 2, (me // 2) % ZS
    step = 1 - 2 * core
    for j in range(XS):
        lo = (2 * (j % 2) + fc) * COLS
        roots = column((far_ref if j // 2 else near_ref)[:, lo : lo + LIVE])
        for t in range(LIVE // TILE):
            own = jnp.broadcast_to(roots[t * TILE : (t + 1) * TILE], (TILE, LANES))
            rows = slice(j * LIVE + t * TILE, j * LIVE + (t + 1) * TILE)
            for i, d in enumerate(pieces):
                ring = (z - step * AWAY[d] + ZS) % ZS
                block = me + 2 * (ring - z)
                if d == 8:
                    block = block + 16 * step
                for h in range(TILES):
                    at = pl.ds(TILES * block + h, 1)
                    value = factors_ref[at, :] / (poles_ref[at, :] - own)
                    lo = (TILES * i + h) * LANES
                    c_ref[rows, lo : lo + LANES] = value.astype(BF16)


def cauchy(fc, pieces, me, poles, factors, near, far):
    return pl.pallas_call(
        lambda *refs: cauchy_kernel(fc, pieces, *refs),
        in_specs=[SM, VM, VM, VM, VM],
        out_specs=VM,
        out_shape=pltpu.VMEM((XS * LIVE, len(pieces) * LIVE), BF16),
        name="cauchy",
        compiler_params=params(8),
        cost_estimate=TINY,
    )(me, poles, factors, near, far)


def norm_kernel(poles_ref, factors_ref, r_ref, rest_ref, n_ref, o_hbm, sem):
    copy = pltpu.make_async_copy(rest_ref, o_hbm.at[:, pl.ds(LIVE, COLS - LIVE)], sem.at[0])
    copy.start()
    roots = column(r_ref[:, :LIVE])
    group = 16
    for t in range(LIVE // TILE):
        own = jnp.broadcast_to(roots[t * TILE : (t + 1) * TILE], (TILE, LANES))

        def step(g, total):
            for u in range(group):
                at = pl.ds(g * group + u, 1)
                value = factors_ref[at, :] / (poles_ref[at, :] - own)
                total = total + value * value
            return total

        total = lax.fori_loop(0, poles_ref.shape[0] // group, step, jnp.zeros((TILE, LANES), F32))
        norm = jnp.sqrt(jnp.sum(total, axis=1, keepdims=True))
        n_ref[t * TILE : (t + 1) * TILE, :] = jnp.broadcast_to(norm, (TILE, LANES))
    copy.wait()


def norms(poles, factors, roots, rest):
    return pl.pallas_call(
        norm_kernel,
        in_specs=[VM] * 4,
        out_specs=[VM, HB],
        out_shape=[
            pltpu.VMEM((LIVE, LANES), F32),
            jax.ShapeDtypeStruct((rest.shape[0], COLS), BF16),
        ],
        scratch_shapes=[pltpu.SemaphoreType.DMA((1,))],
        name="norms",
        compiler_params=params(4),
        cost_estimate=TINY,
    )(poles, factors, roots, rest)


def product(c_ref, j, first, x_refs):
    total = None
    for i, x_ref in enumerate(x_refs):
        lo = (first + i) * LIVE
        part = c_ref[j * LIVE : (j + 1) * LIVE, lo : lo + LIVE]
        piece = jnp.dot(part, x_ref[...], preferred_element_type=F32)
        total = piece if total is None else total + piece
    return total


def stage_kernel(first, count, c_mine, c_other, *refs):
    x_refs, refs = refs[:count], refs[count:]
    sums, outs = refs[:-2], refs[-2:]
    for i, c_ref in enumerate((c_mine, c_other)):
        for j in range(XS):
            rows = slice(j * LIVE, (j + 1) * LIVE)
            total = product(c_ref, j, first, x_refs)
            if sums:
                total = total + sums[i][rows, :]
            outs[i][rows, :] = total.astype(outs[i].dtype)


def stage(first, c_mine, c_other, pieces, sums, last):
    shape = (XS * LIVE, pieces[0].shape[1])
    return pl.pallas_call(
        lambda *refs: stage_kernel(first, len(pieces), *refs),
        in_specs=[VM] * (2 + len(pieces) + len(sums)),
        out_specs=[VM] * 2,
        out_shape=[pltpu.VMEM(shape, F32), pltpu.VMEM(shape, BF16 if last else F32)],
        name="stage",
        compiler_params=params(8),
        cost_estimate=TINY,
    )(c_mine, c_other, *pieces, *sums)


def opposite_kernel(c_ref, x_ref, sum_ref, o_ref):
    for j in range(XS):
        rows = slice(j * LIVE, (j + 1) * LIVE)
        o_ref[rows, :] = sum_ref[rows, :] + product(c_ref, j, 7, (x_ref,))


def add_opposite(c_mine, piece, mine):
    return pl.pallas_call(
        opposite_kernel,
        in_specs=[VM] * 3,
        out_specs=VM,
        out_shape=pltpu.VMEM(mine.shape, F32),
        name="add_opposite",
        compiler_params=params(8),
        cost_estimate=LONG,
    )(c_mine, piece, mine)


def total_kernel(c_ref, x_ref, mine_ref, other_ref, own_ref, *out_refs):
    for j, out_ref in enumerate((own_ref, *out_refs)):
        rows = slice(j * LIVE, (j + 1) * LIVE)
        total = product(c_ref, j, 8, (x_ref,))
        total = total + mine_ref[rows, :] + other_ref[rows, :].astype(F32)
        out_ref[...] = total.astype(out_ref.dtype)


def totals(c_mine, sibling, mine, other):
    shape = (LIVE, mine.shape[1])
    return pl.pallas_call(
        total_kernel,
        in_specs=[VM] * 4,
        out_specs=[VM] * XS,
        out_shape=[pltpu.VMEM(shape, F32)] + [pltpu.VMEM(shape, BF16)] * (XS - 1),
        name="totals",
        compiler_params=params(8),
        cost_estimate=TINY,
    )(c_mine, sibling, mine, other)


def finish_kernel(me_ref, counts_ref, own_ref, a_ref, b_ref, c_ref, n_ref, lead_ref, _, o_hbm, buffer, sem):
    within = lax.broadcasted_iota(jnp.int32, (1, LIVE), 1)
    retain = within < counts_ref[me_ref[0]]
    norm = n_ref[:, :1]
    half = buffer.shape[0] // 2
    copies = []
    for i in range(2):
        part = slice(i * half, (i + 1) * half)
        total = own_ref[:, part] + a_ref[:, part].astype(F32)
        total = total + b_ref[:, part].astype(F32) + c_ref[:, part].astype(F32)
        updated = jnp.transpose(total / norm)
        lead = lead_ref[part, :].astype(F32)
        buffer[part, :] = jnp.where(retain, updated, lead).astype(BF16)
        rows = pl.ds(i * half, half)
        copies.append(
            pltpu.make_async_copy(buffer.at[rows, :], o_hbm.at[rows, pl.ds(0, LIVE)], sem.at[i])
        )
        copies[-1].start()
    for copy in copies:
        copy.wait()


def finish(me, counts, own, received, norm, lead, out):
    return pl.pallas_call(
        finish_kernel,
        in_specs=[SM, SM] + [VM] * (XS + 2) + [HB],
        out_specs=HB,
        out_shape=jax.ShapeDtypeStruct(out.shape, BF16),
        scratch_shapes=[pltpu.VMEM(lead.shape, BF16), pltpu.SemaphoreType.DMA((2,))],
        input_output_aliases={4 + XS: 0},
        name="finish",
        compiler_params=params(4),
        cost_estimate=TINY,
    )(me, counts, own, *received, norm, lead, out)


def per_device(eigvecs, perm, counts, poles, weights, roots):
    me = lax.axis_index(("xl", "core", "z", "xh")).astype(jnp.int32).reshape(1)
    roots = roots.reshape(1, COLS)
    other_roots = cshift(roots)

    own, lead, rest = permute(in_hbm(eigvecs), in_hbm(perm.reshape(1, COLS)))
    table, factors = tables(
        hold(in_hbm(counts), own), in_hbm(poles.reshape(-1, LANES)), in_hbm(weights.reshape(-1, LANES))
    )
    p3 = around(own, 2)
    p4 = around(own, -2)
    p1 = around(own, 1)
    p2 = around(own, -1)
    near = jnp.concatenate([hold(roots, factors), other_roots], axis=1)
    pair = jnp.concatenate([near, xshift(near, -1)], axis=1)
    far = xshift(pair, -2)
    p5 = around(p3, 1)
    p6 = around(p4, -1)
    p7 = around(p3, 2)
    c_other = cauchy(1, OTHER, me, table, factors, pair, hold(far, p3, p4))
    c_mine = cauchy(0, MINE, me, table, factors, pair, hold(far, c_other))

    sums = stage(0, c_mine, c_other, (own, p1, p2, p3, p4), (), False)
    mine, other = stage(5, c_mine, c_other, (p5, p6), sums, True)
    other = cshift(other)
    sibling = cshift(p7)
    mine = add_opposite(c_mine, p7, mine)
    own_sum, *sent = totals(c_mine, sibling, mine, other)
    received = [xshift(part, k) for k, part in zip((1, 2, -1), sent, strict=True)]
    norm, out = norms(table, factors, hold(roots, own_sum), rest)
    return finish(me, counts, own_sum, received, norm, lead, out)


def solution(mesh):
    fine_mesh = Mesh(mesh.devices.reshape(4, 2, 2, 8, 2), ("rows", "xl", "core", "z", "xh"))
    columns = ("xl", "core", "z", "xh")
    return jax.shard_map(
        per_device,
        mesh=fine_mesh,
        in_specs=(P("rows", columns), P(columns), P(), P(), P(), P(columns)),
        out_specs=P("rows", columns),
        check_vma=False,
    )
```

```python
import jax
import jax.numpy as jnp
from jax import lax
from jax.experimental import pallas as pl
from jax.experimental.pallas import tpu as pltpu
from jax.sharding import Mesh
from jax.sharding import PartitionSpec as P

LIVE = 256
COLS = 512
LANES = 128
TILES = LIVE // LANES
ZS = 8
XS = 4
TILE = 128
AWAY = (0, 1, -1, 2, -2, 3, -3, 4, 4)
OTHER = range(7)
MINE = range(9)

VM = pl.BlockSpec(memory_space=pltpu.VMEM)
HB = pl.BlockSpec(memory_space=pltpu.HBM)
SM = pl.BlockSpec(memory_space=pltpu.SMEM)
F32 = jnp.float32
BF16 = jnp.bfloat16


def params(mib):
    return pltpu.CompilerParams(vmem_limit_bytes=mib << 20)


TINY = pl.CostEstimate(flops=1, transcendentals=0, bytes_accessed=1)
LONG = pl.CostEstimate(flops=10**10, transcendentals=0, bytes_accessed=1)


def xshift(a, k):
    pairs = []
    for i in range(XS):
        xl, xh = i // 2, i % 2
        x = (2 * xh + xl + k) % XS
        pairs.append((i, 2 * (x % 2) + x // 2))
    return lax.ppermute(a, ("xl", "xh"), pairs)


def around(a, way):
    up = [(z, (z + way) % ZS) for z in range(ZS)]
    down = [(ZS + z, ZS + (z - way) % ZS) for z in range(ZS)]
    return lax.ppermute(a, ("core", "z"), up + down)


def cshift(a):
    return lax.ppermute(a, "core", [(0, 1), (1, 0)])


def hold(a, *others):
    return lax.optimization_barrier((a, *others))[0]


def in_hbm(a):
    return pltpu.with_memory_space_constraint(a, pltpu.HBM)


def permute_kernel(e_hbm, perm_hbm, x_ref, lead_ref, rest_ref, e_ref, perm_ref, sem):
    rows = e_ref.shape[0]
    half = rows // 2
    order = pltpu.make_async_copy(perm_hbm, perm_ref, sem.at[2])
    order.start()
    copies = []
    for i in range(2):
        part = pl.ds(i * half, half)
        copies.append(pltpu.make_async_copy(e_hbm.at[part, :], e_ref.at[part, :], sem.at[i]))
        copies[-1].start()
    order.wait()
    source = lax.broadcasted_iota(jnp.int32, (COLS, COLS), 0)
    selector = jnp.where(source == perm_ref[...], 1.0, 0.0).astype(BF16)
    for i, copy in enumerate(copies):
        copy.wait()
        part = slice(i * half, (i + 1) * half)
        moved = jnp.dot(e_ref[part, :], selector, preferred_element_type=F32)
        x_ref[:, part] = jnp.transpose(moved[:, :LIVE]).astype(BF16)
        lead_ref[part, :] = moved[:, :LIVE].astype(BF16)
        rest_ref[part, :] = moved[:, LIVE:].astype(BF16)


def permute(eigvecs, perm):
    rows = eigvecs.shape[0]
    return pl.pallas_call(
        permute_kernel,
        in_specs=[HB, HB],
        out_specs=[VM] * 3,
        out_shape=[
            pltpu.VMEM((LIVE, rows), BF16),
            pltpu.VMEM((rows, LIVE), BF16),
            pltpu.VMEM((rows, COLS - LIVE), BF16),
        ],
        scratch_shapes=[
            pltpu.VMEM(eigvecs.shape, BF16),
            pltpu.VMEM(perm.shape, jnp.int32),
            pltpu.SemaphoreType.DMA((3,)),
        ],
        name="permute",
        compiler_params=params(8),
        cost_estimate=TINY,
    )(eigvecs, perm)


def table_kernel(
    counts_hbm, poles_hbm, weights_hbm, roots_hbm, sibling_ref, p_ref, f_ref, near_ref, poles_ref, weights_ref, counts_ref, sem
):
    first = pltpu.make_async_copy(poles_hbm, poles_ref, sem.at[0])
    second = pltpu.make_async_copy(weights_hbm, weights_ref, sem.at[1])
    third = pltpu.make_async_copy(counts_hbm, counts_ref, sem.at[2])
    fourth = pltpu.make_async_copy(roots_hbm, near_ref.at[:, pl.ds(0, COLS)], sem.at[3])
    third.start()
    fourth.start()
    first.start()
    second.start()
    third.wait()
    first.wait()
    second.wait()
    span, keep = COLS // LANES, LIVE // LANES
    at = lax.broadcasted_iota(jnp.int32, (keep, LANES), 0) * LANES
    at = at + lax.broadcasted_iota(jnp.int32, (keep, LANES), 1)
    for block in range(counts_ref.shape[0]):
        rows = slice(keep * block, keep * (block + 1))
        here = slice(span * block, span * block + keep)
        p_ref[rows, :] = poles_ref[here, :]
        f_ref[rows, :] = jnp.where(at < counts_ref[block], weights_ref[here, :], 0.0)
    near_ref[:, COLS:] = sibling_ref[...]
    fourth.wait()


def tables(counts, poles, weights, roots, sibling):
    shape = (counts.shape[0] * LIVE // LANES, LANES)
    return pl.pallas_call(
        table_kernel,
        in_specs=[HB, HB, HB, HB, VM],
        out_specs=[VM, VM, VM],
        out_shape=[pltpu.VMEM(shape, F32)] * 2 + [pltpu.VMEM((1, 2 * COLS), F32)],
        scratch_shapes=[pltpu.VMEM(poles.shape, F32)] * 2
        + [pltpu.SMEM(counts.shape, jnp.int32), pltpu.SemaphoreType.DMA((4,))],
        name="tables",
        compiler_params=params(4),
        cost_estimate=TINY,
    )(counts, poles, weights, roots, sibling)


def column(row):
    return jnp.transpose(jnp.broadcast_to(row, (8, LIVE)))[:, :1]


def cauchy_kernel(fc, pieces, me_ref, poles_ref, factors_ref, *refs):
    r_refs, c_ref = refs[:-1], refs[-1]
    me = me_ref[0]
    core, z = (me // 16) % 2, (me // 2) % ZS
    step = 1 - 2 * core
    for j in range(XS):
        roots = column(r_refs[j][:, fc * COLS : fc * COLS + LIVE])
        for t in range(LIVE // TILE):
            own = jnp.broadcast_to(roots[t * TILE : (t + 1) * TILE], (TILE, LANES))
            rows = slice(j * LIVE + t * TILE, j * LIVE + (t + 1) * TILE)
            for i, d in enumerate(pieces):
                ring = (z - step * AWAY[d] + ZS) % ZS
                block = me + 2 * (ring - z)
                if d == 8:
                    block = block + 16 * step
                for h in range(TILES):
                    at = pl.ds(TILES * block + h, 1)
                    value = factors_ref[at, :] / (poles_ref[at, :] - own)
                    lo = (TILES * i + h) * LANES
                    c_ref[rows, lo : lo + LANES] = value.astype(BF16)


def cauchy(fc, pieces, me, poles, factors, roots):
    return pl.pallas_call(
        lambda *refs: cauchy_kernel(fc, pieces, *refs),
        in_specs=[SM] + [VM] * (2 + XS),
        out_specs=VM,
        out_shape=pltpu.VMEM((XS * LIVE, len(pieces) * LIVE), BF16),
        name="cauchy",
        compiler_params=params(8),
        cost_estimate=TINY,
    )(me, poles, factors, *roots)


def norm_kernel(poles_ref, factors_ref, r_ref, rest_ref, n_ref, o_hbm, sem):
    copy = pltpu.make_async_copy(rest_ref, o_hbm.at[:, pl.ds(LIVE, COLS - LIVE)], sem.at[0])
    copy.start()
    roots = column(r_ref[:, :LIVE])
    group = 16
    for t in range(LIVE // TILE):
        own = jnp.broadcast_to(roots[t * TILE : (t + 1) * TILE], (TILE, LANES))

        def step(g, total):
            for u in range(group):
                at = pl.ds(g * group + u, 1)
                value = factors_ref[at, :] / (poles_ref[at, :] - own)
                total = total + value * value
            return total

        total = lax.fori_loop(0, poles_ref.shape[0] // group, step, jnp.zeros((TILE, LANES), F32))
        norm = jnp.sqrt(jnp.sum(total, axis=1, keepdims=True))
        n_ref[t * TILE : (t + 1) * TILE, :] = jnp.broadcast_to(norm, (TILE, LANES))
    copy.wait()


def norms(poles, factors, roots, rest):
    return pl.pallas_call(
        norm_kernel,
        in_specs=[VM] * 4,
        out_specs=[VM, HB],
        out_shape=[
            pltpu.VMEM((LIVE, LANES), F32),
            jax.ShapeDtypeStruct((rest.shape[0], COLS), BF16),
        ],
        scratch_shapes=[pltpu.SemaphoreType.DMA((1,))],
        name="norms",
        compiler_params=params(4),
        cost_estimate=TINY,
    )(poles, factors, roots, rest)


def product(c_ref, j, first, x_refs):
    total = None
    for i, x_ref in enumerate(x_refs):
        lo = (first + i) * LIVE
        part = c_ref[j * LIVE : (j + 1) * LIVE, lo : lo + LIVE]
        piece = jnp.dot(part, x_ref[...], preferred_element_type=F32)
        total = piece if total is None else total + piece
    return total


def stage_kernel(first, count, c_mine, c_other, *refs):
    x_refs, refs = refs[:count], refs[count:]
    sums, outs = refs[:-2], refs[-2:]
    for i, c_ref in enumerate((c_mine, c_other)):
        for j in range(XS):
            rows = slice(j * LIVE, (j + 1) * LIVE)
            total = product(c_ref, j, first, x_refs)
            if sums:
                total = total + sums[i][rows, :]
            outs[i][rows, :] = total.astype(outs[i].dtype)


def stage(first, c_mine, c_other, pieces, sums, last):
    shape = (XS * LIVE, pieces[0].shape[1])
    return pl.pallas_call(
        lambda *refs: stage_kernel(first, len(pieces), *refs),
        in_specs=[VM] * (2 + len(pieces) + len(sums)),
        out_specs=[VM] * 2,
        out_shape=[pltpu.VMEM(shape, F32), pltpu.VMEM(shape, BF16 if last else F32)],
        name="stage",
        compiler_params=params(8),
        cost_estimate=TINY,
    )(c_mine, c_other, *pieces, *sums)


def opposite_kernel(c_ref, x_ref, sum_ref, o_ref):
    for j in range(XS):
        rows = slice(j * LIVE, (j + 1) * LIVE)
        o_ref[rows, :] = sum_ref[rows, :] + product(c_ref, j, 7, (x_ref,))


def add_opposite(c_mine, piece, mine):
    return pl.pallas_call(
        opposite_kernel,
        in_specs=[VM] * 3,
        out_specs=VM,
        out_shape=pltpu.VMEM(mine.shape, F32),
        name="add_opposite",
        compiler_params=params(8),
        cost_estimate=LONG,
    )(c_mine, piece, mine)


def total_kernel(c_ref, x_ref, mine_ref, other_ref, own_ref, *out_refs):
    for j, out_ref in enumerate((own_ref, *out_refs)):
        rows = slice(j * LIVE, (j + 1) * LIVE)
        total = product(c_ref, j, 8, (x_ref,))
        total = total + mine_ref[rows, :] + other_ref[rows, :].astype(F32)
        out_ref[...] = total.astype(out_ref.dtype)


def totals(c_mine, sibling, mine, other):
    shape = (LIVE, mine.shape[1])
    return pl.pallas_call(
        total_kernel,
        in_specs=[VM] * 4,
        out_specs=[VM] * XS,
        out_shape=[pltpu.VMEM(shape, F32)] + [pltpu.VMEM(shape, BF16)] * (XS - 1),
        name="totals",
        compiler_params=params(8),
        cost_estimate=TINY,
    )(c_mine, sibling, mine, other)


def finish_kernel(me_ref, counts_ref, own_ref, a_ref, b_ref, c_ref, n_ref, lead_ref, _, o_hbm, buffer, sem):
    within = lax.broadcasted_iota(jnp.int32, (1, LIVE), 1)
    retain = within < counts_ref[me_ref[0]]
    norm = n_ref[:, :1]
    half = buffer.shape[0] // 2
    copies = []
    for i in range(2):
        part = slice(i * half, (i + 1) * half)
        total = own_ref[:, part] + a_ref[:, part].astype(F32)
        total = total + b_ref[:, part].astype(F32) + c_ref[:, part].astype(F32)
        updated = jnp.transpose(total / norm)
        lead = lead_ref[part, :].astype(F32)
        buffer[part, :] = jnp.where(retain, updated, lead).astype(BF16)
        rows = pl.ds(i * half, half)
        copies.append(
            pltpu.make_async_copy(buffer.at[rows, :], o_hbm.at[rows, pl.ds(0, LIVE)], sem.at[i])
        )
        copies[-1].start()
    for copy in copies:
        copy.wait()


def finish(me, counts, own, received, norm, lead, out):
    return pl.pallas_call(
        finish_kernel,
        in_specs=[SM, SM] + [VM] * (XS + 2) + [HB],
        out_specs=HB,
        out_shape=jax.ShapeDtypeStruct(out.shape, BF16),
        scratch_shapes=[pltpu.VMEM(lead.shape, BF16), pltpu.SemaphoreType.DMA((2,))],
        input_output_aliases={4 + XS: 0},
        name="finish",
        compiler_params=params(4),
        cost_estimate=TINY,
    )(me, counts, own, *received, norm, lead, out)


def per_device(eigvecs, perm, counts, poles, weights, roots):
    me = lax.axis_index(("xl", "core", "z", "xh")).astype(jnp.int32).reshape(1)
    roots = roots.reshape(1, COLS)
    other_roots = cshift(roots)

    own, lead, rest = permute(in_hbm(eigvecs), in_hbm(perm.reshape(1, COLS)))
    table, factors, near = tables(
        hold(in_hbm(counts), own),
        in_hbm(poles.reshape(-1, LANES)),
        in_hbm(weights.reshape(-1, LANES)),
        in_hbm(roots),
        other_roots,
    )
    p3 = around(own, 2)
    p4 = around(own, -2)
    p1 = around(own, 1)
    p2 = around(own, -1)
    far = [xshift(near, k) for k in (-1, -2, 1)]
    c_other = cauchy(1, OTHER, me, table, factors, [near, *far])
    p5 = around(hold(p3, c_other), 1)
    p7 = around(hold(p3, c_other), 2)
    p6 = around(p4, -1)
    c_mine = cauchy(0, MINE, me, table, factors, [hold(near, p3, p4), *far])

    sums = stage(0, c_mine, c_other, (own, p1, p2, p3, p4), (), False)
    mine, other = stage(5, c_mine, c_other, (p5, p6), sums, True)
    other = cshift(other)
    sibling = cshift(p7)
    mine = add_opposite(c_mine, p7, mine)
    own_sum, *sent = totals(c_mine, sibling, mine, other)
    received = [xshift(part, k) for k, part in zip((1, 2, -1), sent, strict=True)]
    norm, out = norms(table, factors, hold(roots, own_sum), rest)
    return finish(me, counts, own_sum, received, norm, lead, out)


def solution(mesh):
    fine_mesh = Mesh(mesh.devices.reshape(4, 2, 2, 8, 2), ("rows", "xl", "core", "z", "xh"))
    columns = ("xl", "core", "z", "xh")
    return jax.shard_map(
        per_device,
        mesh=fine_mesh,
        in_specs=(P("rows", columns), P(columns), P(), P(), P(), P(columns)),
        out_specs=P("rows", columns),
        check_vma=False,
    )
```

```python
import jax
import jax.numpy as jnp
from jax import lax
from jax.experimental import pallas as pl
from jax.experimental.pallas import tpu as pltpu
from jax.sharding import Mesh
from jax.sharding import PartitionSpec as P

LIVE = 256
COLS = 512
LANES = 128
TILES = LIVE // LANES
ZS = 8
XS = 4
TILE = 128
AWAY = (0, 1, -1, 2, -2, 3, -3, 4, 4)
OTHER = range(7)
MINE = range(9)

VM = pl.BlockSpec(memory_space=pltpu.VMEM)
HB = pl.BlockSpec(memory_space=pltpu.HBM)
SM = pl.BlockSpec(memory_space=pltpu.SMEM)
F32 = jnp.float32
BF16 = jnp.bfloat16


def params(mib):
    return pltpu.CompilerParams(vmem_limit_bytes=mib << 20)


TINY = pl.CostEstimate(flops=1, transcendentals=0, bytes_accessed=1)
LONG = pl.CostEstimate(flops=10**10, transcendentals=0, bytes_accessed=1)


def xshift(a, k):
    pairs = []
    for i in range(XS):
        xl, xh = i // 2, i % 2
        x = (2 * xh + xl + k) % XS
        pairs.append((i, 2 * (x % 2) + x // 2))
    return lax.ppermute(a, ("xl", "xh"), pairs)


def around(a, way):
    up = [(z, (z + way) % ZS) for z in range(ZS)]
    down = [(ZS + z, ZS + (z - way) % ZS) for z in range(ZS)]
    return lax.ppermute(a, ("core", "z"), up + down)


def cshift(a):
    return lax.ppermute(a, "core", [(0, 1), (1, 0)])


def hold(a, *others):
    return lax.optimization_barrier((a, *others))[0]


def in_hbm(a):
    return pltpu.with_memory_space_constraint(a, pltpu.HBM)


def permute_kernel(e_hbm, perm_hbm, x_ref, lead_ref, rest_ref, e_ref, perm_ref, sem):
    rows = e_ref.shape[0]
    half = rows // 2
    order = pltpu.make_async_copy(perm_hbm, perm_ref, sem.at[2])
    order.start()
    copies = []
    for i in range(2):
        part = pl.ds(i * half, half)
        copies.append(pltpu.make_async_copy(e_hbm.at[part, :], e_ref.at[part, :], sem.at[i]))
        copies[-1].start()
    order.wait()
    source = lax.broadcasted_iota(jnp.int32, (COLS, COLS), 0)
    selector = jnp.where(source == perm_ref[...], 1.0, 0.0).astype(BF16)
    for i, copy in enumerate(copies):
        copy.wait()
        part = slice(i * half, (i + 1) * half)
        moved = jnp.dot(e_ref[part, :], selector, preferred_element_type=F32)
        x_ref[:, part] = jnp.transpose(moved[:, :LIVE]).astype(BF16)
        lead_ref[part, :] = moved[:, :LIVE].astype(BF16)
        rest_ref[part, :] = moved[:, LIVE:].astype(BF16)


def permute(eigvecs, perm):
    rows = eigvecs.shape[0]
    return pl.pallas_call(
        permute_kernel,
        in_specs=[HB, HB],
        out_specs=[VM] * 3,
        out_shape=[
            pltpu.VMEM((LIVE, rows), BF16),
            pltpu.VMEM((rows, LIVE), BF16),
            pltpu.VMEM((rows, COLS - LIVE), BF16),
        ],
        scratch_shapes=[
            pltpu.VMEM(eigvecs.shape, BF16),
            pltpu.VMEM(perm.shape, jnp.int32),
            pltpu.SemaphoreType.DMA((3,)),
        ],
        name="permute",
        compiler_params=params(8),
        cost_estimate=TINY,
    )(eigvecs, perm)


def table_kernel(
    counts_hbm, poles_hbm, weights_hbm, roots_hbm, sibling_ref, p_ref, f_ref, near_ref, poles_ref, weights_ref, counts_ref, sem
):
    first = pltpu.make_async_copy(poles_hbm, poles_ref, sem.at[0])
    second = pltpu.make_async_copy(weights_hbm, weights_ref, sem.at[1])
    third = pltpu.make_async_copy(counts_hbm, counts_ref, sem.at[2])
    fourth = pltpu.make_async_copy(roots_hbm, near_ref.at[:, pl.ds(0, COLS)], sem.at[3])
    third.start()
    fourth.start()
    first.start()
    second.start()
    third.wait()
    first.wait()
    second.wait()
    span, keep = COLS // LANES, LIVE // LANES
    at = lax.broadcasted_iota(jnp.int32, (keep, LANES), 0) * LANES
    at = at + lax.broadcasted_iota(jnp.int32, (keep, LANES), 1)
    for block in range(counts_ref.shape[0]):
        rows = slice(keep * block, keep * (block + 1))
        here = slice(span * block, span * block + keep)
        p_ref[rows, :] = poles_ref[here, :]
        f_ref[rows, :] = jnp.where(at < counts_ref[block], weights_ref[here, :], 0.0)
    near_ref[:, COLS:] = sibling_ref[...]
    fourth.wait()


def tables(counts, poles, weights, roots, sibling):
    shape = (counts.shape[0] * LIVE // LANES, LANES)
    return pl.pallas_call(
        table_kernel,
        in_specs=[HB, HB, HB, HB, VM],
        out_specs=[VM, VM, VM],
        out_shape=[pltpu.VMEM(shape, F32)] * 2 + [pltpu.VMEM((1, 2 * COLS), F32)],
        scratch_shapes=[pltpu.VMEM(poles.shape, F32)] * 2
        + [pltpu.SMEM(counts.shape, jnp.int32), pltpu.SemaphoreType.DMA((4,))],
        name="tables",
        compiler_params=params(4),
        cost_estimate=TINY,
    )(counts, poles, weights, roots, sibling)


def column(row):
    return jnp.transpose(jnp.broadcast_to(row, (8, LIVE)))[:, :1]


def cauchy_kernel(fc, pieces, me_ref, poles_ref, factors_ref, *refs):
    r_refs, c_ref = refs[:-1], refs[-1]
    me = me_ref[0]
    core, z = (me // 16) % 2, (me // 2) % ZS
    step = 1 - 2 * core
    for j in range(XS):
        roots = column(r_refs[j][:, fc * COLS : fc * COLS + LIVE])
        for t in range(LIVE // TILE):
            own = jnp.broadcast_to(roots[t * TILE : (t + 1) * TILE], (TILE, LANES))
            rows = slice(j * LIVE + t * TILE, j * LIVE + (t + 1) * TILE)
            for i, d in enumerate(pieces):
                ring = (z - step * AWAY[d] + ZS) % ZS
                block = me + 2 * (ring - z)
                if d == 8:
                    block = block + 16 * step
                for h in range(TILES):
                    at = pl.ds(TILES * block + h, 1)
                    value = factors_ref[at, :] / (poles_ref[at, :] - own)
                    lo = (TILES * i + h) * LANES
                    c_ref[rows, lo : lo + LANES] = value.astype(BF16)


def cauchy(fc, pieces, me, poles, factors, roots):
    return pl.pallas_call(
        lambda *refs: cauchy_kernel(fc, pieces, *refs),
        in_specs=[SM] + [VM] * (2 + XS),
        out_specs=VM,
        out_shape=pltpu.VMEM((XS * LIVE, len(pieces) * LIVE), BF16),
        name="cauchy",
        compiler_params=params(8),
        cost_estimate=TINY,
    )(me, poles, factors, *roots)


def norm_kernel(poles_ref, factors_ref, r_ref, rest_ref, n_ref, o_hbm, sem):
    copy = pltpu.make_async_copy(rest_ref, o_hbm.at[:, pl.ds(LIVE, COLS - LIVE)], sem.at[0])
    copy.start()
    roots = column(r_ref[:, :LIVE])
    group = 16
    for t in range(LIVE // TILE):
        own = jnp.broadcast_to(roots[t * TILE : (t + 1) * TILE], (TILE, LANES))

        def step(g, total):
            for u in range(group):
                at = pl.ds(g * group + u, 1)
                value = factors_ref[at, :] / (poles_ref[at, :] - own)
                total = total + value * value
            return total

        total = lax.fori_loop(0, poles_ref.shape[0] // group, step, jnp.zeros((TILE, LANES), F32))
        norm = jnp.sqrt(jnp.sum(total, axis=1, keepdims=True))
        n_ref[t * TILE : (t + 1) * TILE, :] = jnp.broadcast_to(norm, (TILE, LANES))
    copy.wait()


def norms(poles, factors, roots, rest):
    return pl.pallas_call(
        norm_kernel,
        in_specs=[VM] * 4,
        out_specs=[VM, HB],
        out_shape=[
            pltpu.VMEM((LIVE, LANES), F32),
            jax.ShapeDtypeStruct((rest.shape[0], COLS), BF16),
        ],
        scratch_shapes=[pltpu.SemaphoreType.DMA((1,))],
        name="norms",
        compiler_params=params(4),
        cost_estimate=TINY,
    )(poles, factors, roots, rest)


def product(c_ref, j, first, x_refs):
    total = None
    for i, x_ref in enumerate(x_refs):
        lo = (first + i) * LIVE
        part = c_ref[j * LIVE : (j + 1) * LIVE, lo : lo + LIVE]
        piece = jnp.dot(part, x_ref[...], preferred_element_type=F32)
        total = piece if total is None else total + piece
    return total


def stage_kernel(first, count, c_mine, c_other, *refs):
    x_refs, refs = refs[:count], refs[count:]
    sums, outs = refs[:-2], refs[-2:]
    for i, c_ref in enumerate((c_mine, c_other)):
        for j in range(XS):
            rows = slice(j * LIVE, (j + 1) * LIVE)
            total = product(c_ref, j, first, x_refs)
            if sums:
                total = total + sums[i][rows, :]
            outs[i][rows, :] = total.astype(outs[i].dtype)


def stage(first, c_mine, c_other, pieces, sums, last):
    shape = (XS * LIVE, pieces[0].shape[1])
    return pl.pallas_call(
        lambda *refs: stage_kernel(first, len(pieces), *refs),
        in_specs=[VM] * (2 + len(pieces) + len(sums)),
        out_specs=[VM] * 2,
        out_shape=[pltpu.VMEM(shape, F32), pltpu.VMEM(shape, BF16 if last else F32)],
        name="stage",
        compiler_params=params(8),
        cost_estimate=TINY,
    )(c_mine, c_other, *pieces, *sums)


def opposite_kernel(c_ref, x_ref, sum_ref, o_ref):
    for j in range(XS):
        rows = slice(j * LIVE, (j + 1) * LIVE)
        o_ref[rows, :] = sum_ref[rows, :] + product(c_ref, j, 7, (x_ref,))


def add_opposite(c_mine, piece, mine):
    return pl.pallas_call(
        opposite_kernel,
        in_specs=[VM] * 3,
        out_specs=VM,
        out_shape=pltpu.VMEM(mine.shape, F32),
        name="add_opposite",
        compiler_params=params(8),
        cost_estimate=LONG,
    )(c_mine, piece, mine)


def total_kernel(c_ref, x_ref, mine_ref, other_ref, own_ref, *out_refs):
    for j, out_ref in enumerate((own_ref, *out_refs)):
        rows = slice(j * LIVE, (j + 1) * LIVE)
        total = product(c_ref, j, 8, (x_ref,))
        total = total + mine_ref[rows, :] + other_ref[rows, :].astype(F32)
        out_ref[...] = total.astype(out_ref.dtype)


def totals(c_mine, sibling, mine, other):
    shape = (LIVE, mine.shape[1])
    return pl.pallas_call(
        total_kernel,
        in_specs=[VM] * 4,
        out_specs=[VM] * XS,
        out_shape=[pltpu.VMEM(shape, F32)] + [pltpu.VMEM(shape, BF16)] * (XS - 1),
        name="totals",
        compiler_params=params(8),
        cost_estimate=TINY,
    )(c_mine, sibling, mine, other)


def finish_kernel(me_ref, counts_ref, own_ref, a_ref, b_ref, c_ref, n_ref, lead_ref, _, o_hbm, buffer, sem):
    within = lax.broadcasted_iota(jnp.int32, (1, LIVE), 1)
    retain = within < counts_ref[me_ref[0]]
    norm = n_ref[:, :1]
    half = buffer.shape[0] // 2
    copies = []
    for i in range(2):
        part = slice(i * half, (i + 1) * half)
        total = own_ref[:, part] + a_ref[:, part].astype(F32)
        total = total + b_ref[:, part].astype(F32) + c_ref[:, part].astype(F32)
        updated = jnp.transpose(total / norm)
        lead = lead_ref[part, :].astype(F32)
        buffer[part, :] = jnp.where(retain, updated, lead).astype(BF16)
        rows = pl.ds(i * half, half)
        copies.append(
            pltpu.make_async_copy(buffer.at[rows, :], o_hbm.at[rows, pl.ds(0, LIVE)], sem.at[i])
        )
        copies[-1].start()
    for copy in copies:
        copy.wait()


def finish(me, counts, own, received, norm, lead, out):
    return pl.pallas_call(
        finish_kernel,
        in_specs=[SM, SM] + [VM] * (XS + 2) + [HB],
        out_specs=HB,
        out_shape=jax.ShapeDtypeStruct(out.shape, BF16),
        scratch_shapes=[pltpu.VMEM(lead.shape, BF16), pltpu.SemaphoreType.DMA((2,))],
        input_output_aliases={4 + XS: 0},
        name="finish",
        compiler_params=params(4),
        cost_estimate=TINY,
    )(me, counts, own, *received, norm, lead, out)


def per_device(eigvecs, perm, counts, poles, weights, roots):
    me = lax.axis_index(("xl", "core", "z", "xh")).astype(jnp.int32).reshape(1)
    roots = roots.reshape(1, COLS)
    other_roots = cshift(roots)

    own, lead, rest = permute(in_hbm(eigvecs), in_hbm(perm.reshape(1, COLS)))
    table, factors, near = tables(
        hold(in_hbm(counts), own),
        in_hbm(poles.reshape(-1, LANES)),
        in_hbm(weights.reshape(-1, LANES)),
        in_hbm(roots),
        other_roots,
    )
    p3 = around(own, 2)
    p2 = around(own, -1)
    p1 = around(own, 1)
    far = [xshift(near, k) for k in (-1, -2, 1)]
    p4 = around(hold(p2, far[0]), -1)
    c_other = cauchy(1, OTHER, me, table, factors, [hold(near, p2), *far])
    p5 = around(hold(p3, c_other), 1)
    c_mine = cauchy(0, MINE, me, table, factors, [hold(near, p3, c_other), *far])
    p6 = around(hold(p4, c_mine), -1)
    sums = stage(0, c_mine, c_other, (own, p1, p2, p3), (), False)
    p7 = around(hold(p5, sums[0]), 1)
    sums = stage(4, c_mine, c_other, (p4, p5), sums, False)
    mine, other = stage(6, c_mine, c_other, (p6,), sums, True)
    other = cshift(other)
    sibling = cshift(p7)
    mine = add_opposite(c_mine, p7, mine)
    own_sum, *sent = totals(c_mine, sibling, mine, other)
    received = [xshift(sent[i], k) for i, k in ((1, 2), (0, 1), (2, -1))]
    norm, out = norms(table, factors, hold(roots, own_sum), rest)
    return finish(me, counts, own_sum, received, norm, lead, out)


def solution(mesh):
    fine_mesh = Mesh(mesh.devices.reshape(4, 2, 2, 8, 2), ("rows", "xl", "core", "z", "xh"))
    columns = ("xl", "core", "z", "xh")
    return jax.shard_map(
        per_device,
        mesh=fine_mesh,
        in_specs=(P("rows", columns), P(columns), P(), P(), P(), P(columns)),
        out_specs=P("rows", columns),
        check_vma=False,
    )
```

```python
import jax
import jax.numpy as jnp
from jax import lax
from jax.experimental import pallas as pl
from jax.experimental.pallas import tpu as pltpu
from jax.sharding import Mesh
from jax.sharding import PartitionSpec as P

LIVE = 256
COLS = 512
LANES = 128
TILES = LIVE // LANES
ZS = 8
XS = 4
TILE = 128
AWAY = (0, 1, -1, 2, -2, 3, -3, 4, 4)
OTHER = range(7)
MINE = range(9)

VM = pl.BlockSpec(memory_space=pltpu.VMEM)
HB = pl.BlockSpec(memory_space=pltpu.HBM)
SM = pl.BlockSpec(memory_space=pltpu.SMEM)
F32 = jnp.float32
BF16 = jnp.bfloat16


def params(mib):
    return pltpu.CompilerParams(vmem_limit_bytes=mib << 20)


TINY = pl.CostEstimate(flops=1, transcendentals=0, bytes_accessed=1)
LONG = pl.CostEstimate(flops=10**10, transcendentals=0, bytes_accessed=1)


def xshift(a, k):
    pairs = []
    for i in range(XS):
        xl, xh = i // 2, i % 2
        x = (2 * xh + xl + k) % XS
        pairs.append((i, 2 * (x % 2) + x // 2))
    return lax.ppermute(a, ("xl", "xh"), pairs)


def around(a, way):
    up = [(z, (z + way) % ZS) for z in range(ZS)]
    down = [(ZS + z, ZS + (z - way) % ZS) for z in range(ZS)]
    return lax.ppermute(a, ("core", "z"), up + down)


def cshift(a):
    return lax.ppermute(a, "core", [(0, 1), (1, 0)])


def hold(a, *others):
    return lax.optimization_barrier((a, *others))[0]


def in_hbm(a):
    return pltpu.with_memory_space_constraint(a, pltpu.HBM)


def permute_kernel(e_hbm, perm_hbm, x_ref, lead_ref, rest_ref, e_ref, perm_ref, sem):
    rows = e_ref.shape[0]
    half = rows // 2
    order = pltpu.make_async_copy(perm_hbm, perm_ref, sem.at[2])
    order.start()
    copies = []
    for i in range(2):
        part = pl.ds(i * half, half)
        copies.append(pltpu.make_async_copy(e_hbm.at[part, :], e_ref.at[part, :], sem.at[i]))
        copies[-1].start()
    order.wait()
    source = lax.broadcasted_iota(jnp.int32, (COLS, COLS), 0)
    selector = jnp.where(source == perm_ref[...], 1.0, 0.0).astype(BF16)
    for i, copy in enumerate(copies):
        copy.wait()
        part = slice(i * half, (i + 1) * half)
        moved = jnp.dot(e_ref[part, :], selector, preferred_element_type=F32)
        x_ref[:, part] = jnp.transpose(moved[:, :LIVE]).astype(BF16)
        lead_ref[part, :] = moved[:, :LIVE].astype(BF16)
        rest_ref[part, :] = moved[:, LIVE:].astype(BF16)


def permute(eigvecs, perm):
    rows = eigvecs.shape[0]
    return pl.pallas_call(
        permute_kernel,
        in_specs=[HB, HB],
        out_specs=[VM] * 3,
        out_shape=[
            pltpu.VMEM((LIVE, rows), BF16),
            pltpu.VMEM((rows, LIVE), BF16),
            pltpu.VMEM((rows, COLS - LIVE), BF16),
        ],
        scratch_shapes=[
            pltpu.VMEM(eigvecs.shape, BF16),
            pltpu.VMEM(perm.shape, jnp.int32),
            pltpu.SemaphoreType.DMA((3,)),
        ],
        name="permute",
        compiler_params=params(8),
        cost_estimate=TINY,
    )(eigvecs, perm)


def table_kernel(counts_hbm, poles_hbm, weights_hbm, p_ref, f_ref, poles_ref, weights_ref, counts_ref, sem):
    first = pltpu.make_async_copy(poles_hbm, poles_ref, sem.at[0])
    second = pltpu.make_async_copy(weights_hbm, weights_ref, sem.at[1])
    third = pltpu.make_async_copy(counts_hbm, counts_ref, sem.at[2])
    third.start()
    first.start()
    second.start()
    third.wait()
    first.wait()
    second.wait()
    span, keep = COLS // LANES, LIVE // LANES
    at = lax.broadcasted_iota(jnp.int32, (keep, LANES), 0) * LANES
    at = at + lax.broadcasted_iota(jnp.int32, (keep, LANES), 1)
    for block in range(counts_ref.shape[0]):
        rows = slice(keep * block, keep * (block + 1))
        here = slice(span * block, span * block + keep)
        p_ref[rows, :] = poles_ref[here, :]
        f_ref[rows, :] = jnp.where(at < counts_ref[block], weights_ref[here, :], 0.0)


def tables(counts, poles, weights):
    shape = (counts.shape[0] * LIVE // LANES, LANES)
    return pl.pallas_call(
        table_kernel,
        in_specs=[HB, HB, HB],
        out_specs=[VM, VM],
        out_shape=[pltpu.VMEM(shape, F32)] * 2,
        scratch_shapes=[pltpu.VMEM(poles.shape, F32)] * 2
        + [pltpu.SMEM(counts.shape, jnp.int32), pltpu.SemaphoreType.DMA((3,))],
        name="tables",
        compiler_params=params(4),
        cost_estimate=TINY,
    )(counts, poles, weights)


def join_kernel(a_ref, b_ref, o_ref):
    o_ref[:, :COLS] = a_ref[...]
    o_ref[:, COLS:] = b_ref[...]


def join(a, b):
    return pl.pallas_call(
        join_kernel,
        in_specs=[VM, VM],
        out_specs=VM,
        out_shape=pltpu.VMEM((1, 2 * COLS), F32),
        name="join",
        compiler_params=params(4),
        cost_estimate=TINY,
    )(a, b)


def column(row):
    return jnp.transpose(jnp.broadcast_to(row, (8, LIVE)))[:, :1]


def cauchy_kernel(fc, pieces, me_ref, poles_ref, factors_ref, *refs):
    r_refs, c_ref = refs[:-1], refs[-1]
    me = me_ref[0]
    core, z = (me // 16) % 2, (me // 2) % ZS
    step = 1 - 2 * core
    for j in range(XS):
        roots = column(r_refs[j][:, fc * COLS : fc * COLS + LIVE])
        for t in range(LIVE // TILE):
            own = jnp.broadcast_to(roots[t * TILE : (t + 1) * TILE], (TILE, LANES))
            rows = slice(j * LIVE + t * TILE, j * LIVE + (t + 1) * TILE)
            for i, d in enumerate(pieces):
                ring = (z - step * AWAY[d] + ZS) % ZS
                block = me + 2 * (ring - z)
                if d == 8:
                    block = block + 16 * step
                for h in range(TILES):
                    at = pl.ds(TILES * block + h, 1)
                    value = factors_ref[at, :] / (poles_ref[at, :] - own)
                    lo = (TILES * i + h) * LANES
                    c_ref[rows, lo : lo + LANES] = value.astype(BF16)


def cauchy(fc, pieces, me, poles, factors, roots):
    return pl.pallas_call(
        lambda *refs: cauchy_kernel(fc, pieces, *refs),
        in_specs=[SM] + [VM] * (2 + XS),
        out_specs=VM,
        out_shape=pltpu.VMEM((XS * LIVE, len(pieces) * LIVE), BF16),
        name="cauchy",
        compiler_params=params(8),
        cost_estimate=TINY,
    )(me, poles, factors, *roots)


def norm_kernel(poles_ref, factors_ref, r_ref, rest_ref, n_ref, o_hbm, sem):
    copy = pltpu.make_async_copy(rest_ref, o_hbm.at[:, pl.ds(LIVE, COLS - LIVE)], sem.at[0])
    copy.start()
    roots = column(r_ref[:, :LIVE])
    group = 16
    for t in range(LIVE // TILE):
        own = jnp.broadcast_to(roots[t * TILE : (t + 1) * TILE], (TILE, LANES))

        def step(g, total):
            for u in range(group):
                at = pl.ds(g * group + u, 1)
                value = factors_ref[at, :] / (poles_ref[at, :] - own)
                total = total + value * value
            return total

        total = lax.fori_loop(0, poles_ref.shape[0] // group, step, jnp.zeros((TILE, LANES), F32))
        norm = jnp.sqrt(jnp.sum(total, axis=1, keepdims=True))
        n_ref[t * TILE : (t + 1) * TILE, :] = jnp.broadcast_to(norm, (TILE, LANES))
    copy.wait()


def norms(poles, factors, roots, rest):
    return pl.pallas_call(
        norm_kernel,
        in_specs=[VM] * 4,
        out_specs=[VM, HB],
        out_shape=[
            pltpu.VMEM((LIVE, LANES), F32),
            jax.ShapeDtypeStruct((rest.shape[0], COLS), BF16),
        ],
        scratch_shapes=[pltpu.SemaphoreType.DMA((1,))],
        name="norms",
        compiler_params=params(4),
        cost_estimate=TINY,
    )(poles, factors, roots, rest)


def product(c_ref, j, first, x_refs):
    total = None
    for i, x_ref in enumerate(x_refs):
        lo = (first + i) * LIVE
        part = c_ref[j * LIVE : (j + 1) * LIVE, lo : lo + LIVE]
        piece = jnp.dot(part, x_ref[...], preferred_element_type=F32)
        total = piece if total is None else total + piece
    return total


def stage_kernel(first, count, c_mine, c_other, *refs):
    x_refs, refs = refs[:count], refs[count:]
    sums, outs = refs[:-2], refs[-2:]
    for i, c_ref in enumerate((c_mine, c_other)):
        for j in range(XS):
            rows = slice(j * LIVE, (j + 1) * LIVE)
            total = product(c_ref, j, first, x_refs)
            if sums:
                total = total + sums[i][rows, :]
            outs[i][rows, :] = total.astype(outs[i].dtype)


def stage(first, c_mine, c_other, pieces, sums, last):
    shape = (XS * LIVE, pieces[0].shape[1])
    return pl.pallas_call(
        lambda *refs: stage_kernel(first, len(pieces), *refs),
        in_specs=[VM] * (2 + len(pieces) + len(sums)),
        out_specs=[VM] * 2,
        out_shape=[pltpu.VMEM(shape, F32), pltpu.VMEM(shape, BF16 if last else F32)],
        name="stage",
        compiler_params=params(8),
        cost_estimate=TINY,
    )(c_mine, c_other, *pieces, *sums)


def opposite_kernel(c_ref, x_ref, sum_ref, o_ref):
    for j in range(XS):
        rows = slice(j * LIVE, (j + 1) * LIVE)
        o_ref[rows, :] = sum_ref[rows, :] + product(c_ref, j, 7, (x_ref,))


def add_opposite(c_mine, piece, mine):
    return pl.pallas_call(
        opposite_kernel,
        in_specs=[VM] * 3,
        out_specs=VM,
        out_shape=pltpu.VMEM(mine.shape, F32),
        name="add_opposite",
        compiler_params=params(8),
        cost_estimate=LONG,
    )(c_mine, piece, mine)


def total_kernel(c_ref, x_ref, mine_ref, other_ref, own_ref, *out_refs):
    for j, out_ref in enumerate((own_ref, *out_refs)):
        rows = slice(j * LIVE, (j + 1) * LIVE)
        total = product(c_ref, j, 8, (x_ref,))
        total = total + mine_ref[rows, :] + other_ref[rows, :].astype(F32)
        out_ref[...] = total.astype(out_ref.dtype)


def totals(c_mine, sibling, mine, other):
    shape = (LIVE, mine.shape[1])
    return pl.pallas_call(
        total_kernel,
        in_specs=[VM] * 4,
        out_specs=[VM] * XS,
        out_shape=[pltpu.VMEM(shape, F32)] + [pltpu.VMEM(shape, BF16)] * (XS - 1),
        name="totals",
        compiler_params=params(8),
        cost_estimate=TINY,
    )(c_mine, sibling, mine, other)


def finish_kernel(me_ref, counts_ref, own_ref, a_ref, b_ref, c_ref, n_ref, lead_ref, _, o_hbm, buffer, sem):
    within = lax.broadcasted_iota(jnp.int32, (1, LIVE), 1)
    retain = within < counts_ref[me_ref[0]]
    norm = n_ref[:, :1]
    half = buffer.shape[0] // 2
    copies = []
    for i in range(2):
        part = slice(i * half, (i + 1) * half)
        total = own_ref[:, part] + a_ref[:, part].astype(F32)
        total = total + b_ref[:, part].astype(F32) + c_ref[:, part].astype(F32)
        updated = jnp.transpose(total / norm)
        lead = lead_ref[part, :].astype(F32)
        buffer[part, :] = jnp.where(retain, updated, lead).astype(BF16)
        rows = pl.ds(i * half, half)
        copies.append(
            pltpu.make_async_copy(buffer.at[rows, :], o_hbm.at[rows, pl.ds(0, LIVE)], sem.at[i])
        )
        copies[-1].start()
    for copy in copies:
        copy.wait()


def finish(me, counts, own, received, norm, lead, out):
    return pl.pallas_call(
        finish_kernel,
        in_specs=[SM, SM] + [VM] * (XS + 2) + [HB],
        out_specs=HB,
        out_shape=jax.ShapeDtypeStruct(out.shape, BF16),
        scratch_shapes=[pltpu.VMEM(lead.shape, BF16), pltpu.SemaphoreType.DMA((2,))],
        input_output_aliases={4 + XS: 0},
        name="finish",
        compiler_params=params(4),
        cost_estimate=TINY,
    )(me, counts, own, *received, norm, lead, out)


def per_device(eigvecs, perm, counts, poles, weights, roots):
    me = lax.axis_index(("xl", "core", "z", "xh")).astype(jnp.int32).reshape(1)
    roots = roots.reshape(1, COLS)
    other_roots = cshift(roots)

    own, lead, rest = permute(in_hbm(eigvecs), in_hbm(perm.reshape(1, COLS)))
    p3 = around(own, 2)
    p2 = around(own, -1)
    p1 = around(own, 1)
    near = join(roots, hold(other_roots, own))
    far = [xshift(near, k) for k in (-1, -2, 1)]
    table, factors = tables(
        hold(in_hbm(counts), near), in_hbm(poles.reshape(-1, LANES)), in_hbm(weights.reshape(-1, LANES))
    )
    p4 = around(hold(p2, factors, *far), -1)
    p5 = around(hold(p3, *far), 1)
    c_other = cauchy(1, OTHER, me, table, factors, [hold(near, p3), *far])
    c_mine = cauchy(0, MINE, me, table, factors, [hold(near, c_other), *far])
    p6 = around(hold(p4, c_other), -1)
    p7 = around(hold(p5, c_mine), 1)
    sums = stage(0, c_mine, c_other, (hold(own, p5), p1, p2, p3), (), False)
    sums = stage(4, c_mine, c_other, (p4, p5), sums, False)
    mine, other = stage(6, c_mine, c_other, (p6,), sums, True)
    other = cshift(other)
    sibling = cshift(p7)
    mine = add_opposite(c_mine, p7, mine)
    own_sum, *sent = totals(c_mine, sibling, mine, other)
    received = [xshift(sent[i], k) for i, k in ((1, 2), (0, 1), (2, -1))]
    norm, out = norms(table, factors, hold(roots, own_sum), rest)
    return finish(me, counts, own_sum, received, norm, lead, out)


def solution(mesh):
    fine_mesh = Mesh(mesh.devices.reshape(4, 2, 2, 8, 2), ("rows", "xl", "core", "z", "xh"))
    columns = ("xl", "core", "z", "xh")
    return jax.shard_map(
        per_device,
        mesh=fine_mesh,
        in_specs=(P("rows", columns), P(columns), P(), P(), P(), P(columns)),
        out_specs=P("rows", columns),
        check_vma=False,
    )
```

```python
import jax
import jax.numpy as jnp
from jax import lax
from jax.experimental import pallas as pl
from jax.experimental.pallas import tpu as pltpu
from jax.sharding import Mesh
from jax.sharding import PartitionSpec as P

LIVE = 256
COLS = 512
LANES = 128
TILES = LIVE // LANES
ZS = 8
XS = 4
TILE = 128
AWAY = (0, -1, 2, 1, -2, 3, -3, 4, 4)
OTHER = range(7)
MINE = range(9)

VM = pl.BlockSpec(memory_space=pltpu.VMEM)
HB = pl.BlockSpec(memory_space=pltpu.HBM)
SM = pl.BlockSpec(memory_space=pltpu.SMEM)
F32 = jnp.float32
BF16 = jnp.bfloat16


def params(mib):
    return pltpu.CompilerParams(vmem_limit_bytes=mib << 20)


TINY = pl.CostEstimate(flops=1, transcendentals=0, bytes_accessed=1)
LONG = pl.CostEstimate(flops=10**10, transcendentals=0, bytes_accessed=1)


def xshift(a, k):
    pairs = []
    for i in range(XS):
        xl, xh = i // 2, i % 2
        x = (2 * xh + xl + k) % XS
        pairs.append((i, 2 * (x % 2) + x // 2))
    return lax.ppermute(a, ("xl", "xh"), pairs)


def around(a, way):
    up = [(z, (z + way) % ZS) for z in range(ZS)]
    down = [(ZS + z, ZS + (z - way) % ZS) for z in range(ZS)]
    return lax.ppermute(a, ("core", "z"), up + down)


def cshift(a):
    return lax.ppermute(a, "core", [(0, 1), (1, 0)])


def hold(a, *others):
    return lax.optimization_barrier((a, *others))[0]


def in_hbm(a):
    return pltpu.with_memory_space_constraint(a, pltpu.HBM)


def permute_kernel(e_hbm, perm_hbm, x_ref, lead_ref, rest_ref, e_ref, perm_ref, sem):
    rows = e_ref.shape[0]
    half = rows // 2
    order = pltpu.make_async_copy(perm_hbm, perm_ref, sem.at[2])
    order.start()
    copies = []
    for i in range(2):
        part = pl.ds(i * half, half)
        copies.append(pltpu.make_async_copy(e_hbm.at[part, :], e_ref.at[part, :], sem.at[i]))
        copies[-1].start()
    order.wait()
    source = lax.broadcasted_iota(jnp.int32, (COLS, COLS), 0)
    selector = jnp.where(source == perm_ref[...], 1.0, 0.0).astype(BF16)
    for i, copy in enumerate(copies):
        copy.wait()
        part = slice(i * half, (i + 1) * half)
        moved = jnp.dot(e_ref[part, :], selector, preferred_element_type=F32)
        x_ref[:, part] = jnp.transpose(moved[:, :LIVE]).astype(BF16)
        lead_ref[part, :] = moved[:, :LIVE].astype(BF16)
        rest_ref[part, :] = moved[:, LIVE:].astype(BF16)


def permute(eigvecs, perm):
    rows = eigvecs.shape[0]
    return pl.pallas_call(
        permute_kernel,
        in_specs=[HB, HB],
        out_specs=[VM] * 3,
        out_shape=[
            pltpu.VMEM((LIVE, rows), BF16),
            pltpu.VMEM((rows, LIVE), BF16),
            pltpu.VMEM((rows, COLS - LIVE), BF16),
        ],
        scratch_shapes=[
            pltpu.VMEM(eigvecs.shape, BF16),
            pltpu.VMEM(perm.shape, jnp.int32),
            pltpu.SemaphoreType.DMA((3,)),
        ],
        name="permute",
        compiler_params=params(8),
        cost_estimate=TINY,
    )(eigvecs, perm)


def table_kernel(counts_hbm, poles_hbm, weights_hbm, p_ref, f_ref, poles_ref, weights_ref, counts_ref, sem):
    first = pltpu.make_async_copy(poles_hbm, poles_ref, sem.at[0])
    second = pltpu.make_async_copy(weights_hbm, weights_ref, sem.at[1])
    third = pltpu.make_async_copy(counts_hbm, counts_ref, sem.at[2])
    third.start()
    first.start()
    second.start()
    third.wait()
    first.wait()
    second.wait()
    span, keep = COLS // LANES, LIVE // LANES
    at = lax.broadcasted_iota(jnp.int32, (keep, LANES), 0) * LANES
    at = at + lax.broadcasted_iota(jnp.int32, (keep, LANES), 1)
    for block in range(counts_ref.shape[0]):
        rows = slice(keep * block, keep * (block + 1))
        here = slice(span * block, span * block + keep)
        p_ref[rows, :] = poles_ref[here, :]
        f_ref[rows, :] = jnp.where(at < counts_ref[block], weights_ref[here, :], 0.0)


def tables(counts, poles, weights):
    shape = (counts.shape[0] * LIVE // LANES, LANES)
    return pl.pallas_call(
        table_kernel,
        in_specs=[HB, HB, HB],
        out_specs=[VM, VM],
        out_shape=[pltpu.VMEM(shape, F32)] * 2,
        scratch_shapes=[pltpu.VMEM(poles.shape, F32)] * 2
        + [pltpu.SMEM(counts.shape, jnp.int32), pltpu.SemaphoreType.DMA((3,))],
        name="tables",
        compiler_params=params(4),
        cost_estimate=TINY,
    )(counts, poles, weights)


def join_kernel(a_ref, b_ref, o_ref):
    o_ref[:, :COLS] = a_ref[...]
    o_ref[:, COLS:] = b_ref[...]


def join(a, b):
    return pl.pallas_call(
        join_kernel,
        in_specs=[VM, VM],
        out_specs=VM,
        out_shape=pltpu.VMEM((1, 2 * COLS), F32),
        name="join",
        compiler_params=params(4),
        cost_estimate=TINY,
    )(a, b)


def column(row):
    return jnp.transpose(jnp.broadcast_to(row, (8, LIVE)))[:, :1]


def cauchy_kernel(fc, pieces, me_ref, poles_ref, factors_ref, *refs):
    r_refs, c_ref = refs[:-1], refs[-1]
    me = me_ref[0]
    core, z = (me // 16) % 2, (me // 2) % ZS
    step = 1 - 2 * core
    for j in range(XS):
        roots = column(r_refs[j][:, fc * COLS : fc * COLS + LIVE])
        for t in range(LIVE // TILE):
            own = jnp.broadcast_to(roots[t * TILE : (t + 1) * TILE], (TILE, LANES))
            rows = slice(j * LIVE + t * TILE, j * LIVE + (t + 1) * TILE)
            for i, d in enumerate(pieces):
                ring = (z - step * AWAY[d] + ZS) % ZS
                block = me + 2 * (ring - z)
                if d == 8:
                    block = block + 16 * step
                for h in range(TILES):
                    at = pl.ds(TILES * block + h, 1)
                    value = factors_ref[at, :] / (poles_ref[at, :] - own)
                    lo = (TILES * i + h) * LANES
                    c_ref[rows, lo : lo + LANES] = value.astype(BF16)


def cauchy(fc, pieces, me, poles, factors, roots):
    return pl.pallas_call(
        lambda *refs: cauchy_kernel(fc, pieces, *refs),
        in_specs=[SM] + [VM] * (2 + XS),
        out_specs=VM,
        out_shape=pltpu.VMEM((XS * LIVE, len(pieces) * LIVE), BF16),
        name="cauchy",
        compiler_params=params(8),
        cost_estimate=TINY,
    )(me, poles, factors, *roots)


def norm_kernel(poles_ref, factors_ref, r_ref, rest_ref, n_ref, o_hbm, sem):
    copy = pltpu.make_async_copy(rest_ref, o_hbm.at[:, pl.ds(LIVE, COLS - LIVE)], sem.at[0])
    copy.start()
    roots = column(r_ref[:, :LIVE])
    group = 16
    for t in range(LIVE // TILE):
        own = jnp.broadcast_to(roots[t * TILE : (t + 1) * TILE], (TILE, LANES))

        def step(g, total):
            for u in range(group):
                at = pl.ds(g * group + u, 1)
                value = factors_ref[at, :] / (poles_ref[at, :] - own)
                total = total + value * value
            return total

        total = lax.fori_loop(0, poles_ref.shape[0] // group, step, jnp.zeros((TILE, LANES), F32))
        norm = jnp.sqrt(jnp.sum(total, axis=1, keepdims=True))
        n_ref[t * TILE : (t + 1) * TILE, :] = jnp.broadcast_to(norm, (TILE, LANES))
    copy.wait()


def norms(poles, factors, roots, rest):
    return pl.pallas_call(
        norm_kernel,
        in_specs=[VM] * 4,
        out_specs=[VM, HB],
        out_shape=[
            pltpu.VMEM((LIVE, LANES), F32),
            jax.ShapeDtypeStruct((rest.shape[0], COLS), BF16),
        ],
        scratch_shapes=[pltpu.SemaphoreType.DMA((1,))],
        name="norms",
        compiler_params=params(4),
        cost_estimate=TINY,
    )(poles, factors, roots, rest)


def product(c_ref, j, first, x_refs):
    total = None
    for i, x_ref in enumerate(x_refs):
        lo = (first + i) * LIVE
        part = c_ref[j * LIVE : (j + 1) * LIVE, lo : lo + LIVE]
        piece = jnp.dot(part, x_ref[...], preferred_element_type=F32)
        total = piece if total is None else total + piece
    return total


def stage_kernel(first, count, c_mine, c_other, *refs):
    x_refs, refs = refs[:count], refs[count:]
    sums, outs = refs[:-2], refs[-2:]
    for i, c_ref in enumerate((c_mine, c_other)):
        for j in range(XS):
            rows = slice(j * LIVE, (j + 1) * LIVE)
            total = product(c_ref, j, first, x_refs)
            if sums:
                total = total + sums[i][rows, :]
            outs[i][rows, :] = total.astype(outs[i].dtype)


def stage(first, c_mine, c_other, pieces, sums, last):
    shape = (XS * LIVE, pieces[0].shape[1])
    return pl.pallas_call(
        lambda *refs: stage_kernel(first, len(pieces), *refs),
        in_specs=[VM] * (2 + len(pieces) + len(sums)),
        out_specs=[VM] * 2,
        out_shape=[pltpu.VMEM(shape, F32), pltpu.VMEM(shape, BF16 if last else F32)],
        name="stage",
        compiler_params=params(8),
        cost_estimate=TINY,
    )(c_mine, c_other, *pieces, *sums)


def opposite_kernel(c_ref, x_ref, sum_ref, o_ref):
    for j in range(XS):
        rows = slice(j * LIVE, (j + 1) * LIVE)
        o_ref[rows, :] = sum_ref[rows, :] + product(c_ref, j, 7, (x_ref,))


def add_opposite(c_mine, piece, mine):
    return pl.pallas_call(
        opposite_kernel,
        in_specs=[VM] * 3,
        out_specs=VM,
        out_shape=pltpu.VMEM(mine.shape, F32),
        name="add_opposite",
        compiler_params=params(8),
        cost_estimate=LONG,
    )(c_mine, piece, mine)


def total_kernel(c_ref, x_ref, mine_ref, other_ref, own_ref, *out_refs):
    for j, out_ref in enumerate((own_ref, *out_refs)):
        rows = slice(j * LIVE, (j + 1) * LIVE)
        total = product(c_ref, j, 8, (x_ref,))
        total = total + mine_ref[rows, :] + other_ref[rows, :].astype(F32)
        out_ref[...] = total.astype(out_ref.dtype)


def totals(c_mine, sibling, mine, other):
    shape = (LIVE, mine.shape[1])
    return pl.pallas_call(
        total_kernel,
        in_specs=[VM] * 4,
        out_specs=[VM] * XS,
        out_shape=[pltpu.VMEM(shape, F32)] + [pltpu.VMEM(shape, BF16)] * (XS - 1),
        name="totals",
        compiler_params=params(8),
        cost_estimate=TINY,
    )(c_mine, sibling, mine, other)


def finish_kernel(me_ref, counts_ref, own_ref, a_ref, b_ref, c_ref, n_ref, lead_ref, _, o_hbm, buffer, sem):
    within = lax.broadcasted_iota(jnp.int32, (1, LIVE), 1)
    retain = within < counts_ref[me_ref[0]]
    norm = n_ref[:, :1]
    half = buffer.shape[0] // 2
    copies = []
    for i in range(2):
        part = slice(i * half, (i + 1) * half)
        total = own_ref[:, part] + a_ref[:, part].astype(F32)
        total = total + b_ref[:, part].astype(F32) + c_ref[:, part].astype(F32)
        updated = jnp.transpose(total / norm)
        lead = lead_ref[part, :].astype(F32)
        buffer[part, :] = jnp.where(retain, updated, lead).astype(BF16)
        rows = pl.ds(i * half, half)
        copies.append(
            pltpu.make_async_copy(buffer.at[rows, :], o_hbm.at[rows, pl.ds(0, LIVE)], sem.at[i])
        )
        copies[-1].start()
    for copy in copies:
        copy.wait()


def finish(me, counts, own, received, norm, lead, out):
    return pl.pallas_call(
        finish_kernel,
        in_specs=[SM, SM] + [VM] * (XS + 2) + [HB],
        out_specs=HB,
        out_shape=jax.ShapeDtypeStruct(out.shape, BF16),
        scratch_shapes=[pltpu.VMEM(lead.shape, BF16), pltpu.SemaphoreType.DMA((2,))],
        input_output_aliases={4 + XS: 0},
        name="finish",
        compiler_params=params(4),
        cost_estimate=TINY,
    )(me, counts, own, *received, norm, lead, out)


def per_device(eigvecs, perm, counts, poles, weights, roots):
    me = lax.axis_index(("xl", "core", "z", "xh")).astype(jnp.int32).reshape(1)
    roots = roots.reshape(1, COLS)
    other_roots = cshift(roots)

    own, lead, rest = permute(in_hbm(eigvecs), in_hbm(perm.reshape(1, COLS)))
    p3 = around(own, 2)
    p2 = around(own, -1)
    p1 = around(own, 1)
    near = join(roots, hold(other_roots, own))
    far = [xshift(near, k) for k in (-1, -2, 1)]
    table, factors = tables(
        hold(in_hbm(counts), near), in_hbm(poles.reshape(-1, LANES)), in_hbm(weights.reshape(-1, LANES))
    )
    p4 = around(hold(p2, factors, *far), -1)
    p5 = around(hold(p3, *far), 1)
    c_other = cauchy(1, OTHER, me, table, factors, [hold(near, p3), *far])
    c_mine = cauchy(0, MINE, me, table, factors, [hold(near, c_other), *far])
    p6 = around(hold(p4, c_mine), -1)
    sums = stage(0, c_mine, c_other, (own, p2, p3), (), False)
    p7 = around(hold(p5, sums[0]), 1)
    sums = stage(3, c_mine, c_other, (p1, p4, p5), sums, False)
    mine, other = stage(6, c_mine, c_other, (p6,), sums, True)
    other = cshift(other)
    sibling = cshift(p7)
    mine = add_opposite(c_mine, p7, mine)
    own_sum, *sent = totals(c_mine, sibling, mine, other)
    received = [xshift(sent[i], k) for i, k in ((1, 2), (0, 1), (2, -1))]
    norm, out = norms(table, factors, hold(roots, own_sum), rest)
    return finish(me, counts, own_sum, received, norm, lead, out)


def solution(mesh):
    fine_mesh = Mesh(mesh.devices.reshape(4, 2, 2, 8, 2), ("rows", "xl", "core", "z", "xh"))
    columns = ("xl", "core", "z", "xh")
    return jax.shard_map(
        per_device,
        mesh=fine_mesh,
        in_specs=(P("rows", columns), P(columns), P(), P(), P(), P(columns)),
        out_specs=P("rows", columns),
        check_vma=False,
    )
```

```python
import jax
import jax.numpy as jnp
from jax import lax
from jax.experimental import pallas as pl
from jax.experimental.pallas import tpu as pltpu
from jax.sharding import Mesh
from jax.sharding import PartitionSpec as P

LIVE = 256
COLS = 512
LANES = 128
TILES = LIVE // LANES
ZS = 8
XS = 4
TILE = 128
AWAY = (0, -1, 2, 1, -2, 3, -3, 4, 3, 4)
OTHER = range(6)
MINE = range(10)

VM = pl.BlockSpec(memory_space=pltpu.VMEM)
HB = pl.BlockSpec(memory_space=pltpu.HBM)
SM = pl.BlockSpec(memory_space=pltpu.SMEM)
F32 = jnp.float32
BF16 = jnp.bfloat16


def params(mib):
    return pltpu.CompilerParams(vmem_limit_bytes=mib << 20)


TINY = pl.CostEstimate(flops=1, transcendentals=0, bytes_accessed=1)
LONG = pl.CostEstimate(flops=10**10, transcendentals=0, bytes_accessed=1)


def xshift(a, k):
    pairs = []
    for i in range(XS):
        xl, xh = i // 2, i % 2
        x = (2 * xh + xl + k) % XS
        pairs.append((i, 2 * (x % 2) + x // 2))
    return lax.ppermute(a, ("xl", "xh"), pairs)


def around(a, way):
    up = [(z, (z + way) % ZS) for z in range(ZS)]
    down = [(ZS + z, ZS + (z - way) % ZS) for z in range(ZS)]
    return lax.ppermute(a, ("core", "z"), up + down)


def cshift(a):
    return lax.ppermute(a, "core", [(0, 1), (1, 0)])


def hold(a, *others):
    return lax.optimization_barrier((a, *others))[0]


def in_hbm(a):
    return pltpu.with_memory_space_constraint(a, pltpu.HBM)


def permute_kernel(e_hbm, perm_hbm, x_ref, lead_ref, rest_ref, e_ref, perm_ref, sem):
    rows = e_ref.shape[0]
    half = rows // 2
    order = pltpu.make_async_copy(perm_hbm, perm_ref, sem.at[2])
    order.start()
    copies = []
    for i in range(2):
        part = pl.ds(i * half, half)
        copies.append(pltpu.make_async_copy(e_hbm.at[part, :], e_ref.at[part, :], sem.at[i]))
        copies[-1].start()
    order.wait()
    source = lax.broadcasted_iota(jnp.int32, (COLS, COLS), 0)
    selector = jnp.where(source == perm_ref[...], 1.0, 0.0).astype(BF16)
    for i, copy in enumerate(copies):
        copy.wait()
        part = slice(i * half, (i + 1) * half)
        moved = jnp.dot(e_ref[part, :], selector, preferred_element_type=F32)
        x_ref[:, part] = jnp.transpose(moved[:, :LIVE]).astype(BF16)
        lead_ref[part, :] = moved[:, :LIVE].astype(BF16)
        rest_ref[part, :] = moved[:, LIVE:].astype(BF16)


def permute(eigvecs, perm):
    rows = eigvecs.shape[0]
    return pl.pallas_call(
        permute_kernel,
        in_specs=[HB, HB],
        out_specs=[VM] * 3,
        out_shape=[
            pltpu.VMEM((LIVE, rows), BF16),
            pltpu.VMEM((rows, LIVE), BF16),
            pltpu.VMEM((rows, COLS - LIVE), BF16),
        ],
        scratch_shapes=[
            pltpu.VMEM(eigvecs.shape, BF16),
            pltpu.VMEM(perm.shape, jnp.int32),
            pltpu.SemaphoreType.DMA((3,)),
        ],
        name="permute",
        compiler_params=params(8),
        cost_estimate=TINY,
    )(eigvecs, perm)


def table_kernel(counts_hbm, poles_hbm, weights_hbm, p_ref, f_ref, poles_ref, weights_ref, counts_ref, sem):
    first = pltpu.make_async_copy(poles_hbm, poles_ref, sem.at[0])
    second = pltpu.make_async_copy(weights_hbm, weights_ref, sem.at[1])
    third = pltpu.make_async_copy(counts_hbm, counts_ref, sem.at[2])
    third.start()
    first.start()
    second.start()
    third.wait()
    first.wait()
    second.wait()
    span, keep = COLS // LANES, LIVE // LANES
    at = lax.broadcasted_iota(jnp.int32, (keep, LANES), 0) * LANES
    at = at + lax.broadcasted_iota(jnp.int32, (keep, LANES), 1)
    for block in range(counts_ref.shape[0]):
        rows = slice(keep * block, keep * (block + 1))
        here = slice(span * block, span * block + keep)
        p_ref[rows, :] = poles_ref[here, :]
        f_ref[rows, :] = jnp.where(at < counts_ref[block], weights_ref[here, :], 0.0)


def tables(counts, poles, weights):
    shape = (counts.shape[0] * LIVE // LANES, LANES)
    return pl.pallas_call(
        table_kernel,
        in_specs=[HB, HB, HB],
        out_specs=[VM, VM],
        out_shape=[pltpu.VMEM(shape, F32)] * 2,
        scratch_shapes=[pltpu.VMEM(poles.shape, F32)] * 2
        + [pltpu.SMEM(counts.shape, jnp.int32), pltpu.SemaphoreType.DMA((3,))],
        name="tables",
        compiler_params=params(4),
        cost_estimate=TINY,
    )(counts, poles, weights)


def join_kernel(a_ref, b_ref, o_ref):
    o_ref[:, :COLS] = a_ref[...]
    o_ref[:, COLS:] = b_ref[...]


def join(a, b):
    return pl.pallas_call(
        join_kernel,
        in_specs=[VM, VM],
        out_specs=VM,
        out_shape=pltpu.VMEM((1, 2 * COLS), F32),
        name="join",
        compiler_params=params(4),
        cost_estimate=TINY,
    )(a, b)


def column(row):
    return jnp.transpose(jnp.broadcast_to(row, (8, LIVE)))[:, :1]


def cauchy_kernel(fc, pieces, me_ref, poles_ref, factors_ref, *refs):
    r_refs, c_ref = refs[:-1], refs[-1]
    me = me_ref[0]
    core, z = (me // 16) % 2, (me // 2) % ZS
    step = 1 - 2 * core
    for j in range(XS):
        roots = column(r_refs[j][:, fc * COLS : fc * COLS + LIVE])
        for t in range(LIVE // TILE):
            own = jnp.broadcast_to(roots[t * TILE : (t + 1) * TILE], (TILE, LANES))
            rows = slice(j * LIVE + t * TILE, j * LIVE + (t + 1) * TILE)
            for i, d in enumerate(pieces):
                ring = (z - step * AWAY[d] + ZS) % ZS
                block = me + 2 * (ring - z)
                if d >= 8:
                    block = block + 16 * step
                for h in range(TILES):
                    at = pl.ds(TILES * block + h, 1)
                    value = factors_ref[at, :] / (poles_ref[at, :] - own)
                    lo = (TILES * i + h) * LANES
                    c_ref[rows, lo : lo + LANES] = value.astype(BF16)


def cauchy(fc, pieces, me, poles, factors, roots):
    return pl.pallas_call(
        lambda *refs: cauchy_kernel(fc, pieces, *refs),
        in_specs=[SM] + [VM] * (2 + XS),
        out_specs=VM,
        out_shape=pltpu.VMEM((XS * LIVE, len(pieces) * LIVE), BF16),
        name="cauchy",
        compiler_params=params(8),
        cost_estimate=TINY,
    )(me, poles, factors, *roots)


def norm_kernel(poles_ref, factors_ref, r_ref, rest_ref, n_ref, o_hbm, sem):
    copy = pltpu.make_async_copy(rest_ref, o_hbm.at[:, pl.ds(LIVE, COLS - LIVE)], sem.at[0])
    copy.start()
    roots = column(r_ref[:, :LIVE])
    group = 16
    for t in range(LIVE // TILE):
        own = jnp.broadcast_to(roots[t * TILE : (t + 1) * TILE], (TILE, LANES))

        def step(g, total):
            for u in range(group):
                at = pl.ds(g * group + u, 1)
                value = factors_ref[at, :] / (poles_ref[at, :] - own)
                total = total + value * value
            return total

        total = lax.fori_loop(0, poles_ref.shape[0] // group, step, jnp.zeros((TILE, LANES), F32))
        norm = jnp.sqrt(jnp.sum(total, axis=1, keepdims=True))
        n_ref[t * TILE : (t + 1) * TILE, :] = jnp.broadcast_to(norm, (TILE, LANES))
    copy.wait()


def norms(poles, factors, roots, rest):
    return pl.pallas_call(
        norm_kernel,
        in_specs=[VM] * 4,
        out_specs=[VM, HB],
        out_shape=[
            pltpu.VMEM((LIVE, LANES), F32),
            jax.ShapeDtypeStruct((rest.shape[0], COLS), BF16),
        ],
        scratch_shapes=[pltpu.SemaphoreType.DMA((1,))],
        name="norms",
        compiler_params=params(4),
        cost_estimate=TINY,
    )(poles, factors, roots, rest)


def product(c_ref, j, first, x_refs):
    total = None
    for i, x_ref in enumerate(x_refs):
        lo = (first + i) * LIVE
        part = c_ref[j * LIVE : (j + 1) * LIVE, lo : lo + LIVE]
        piece = jnp.dot(part, x_ref[...], preferred_element_type=F32)
        total = piece if total is None else total + piece
    return total


def stage_kernel(first, count, c_mine, c_other, *refs):
    x_refs, refs = refs[:count], refs[count:]
    sums, outs = refs[:-2], refs[-2:]
    for i, c_ref in enumerate((c_mine, c_other)):
        for j in range(XS):
            rows = slice(j * LIVE, (j + 1) * LIVE)
            total = product(c_ref, j, first, x_refs)
            if sums:
                total = total + sums[i][rows, :]
            outs[i][rows, :] = total.astype(outs[i].dtype)


def stage(first, c_mine, c_other, pieces, sums, last):
    shape = (XS * LIVE, pieces[0].shape[1])
    return pl.pallas_call(
        lambda *refs: stage_kernel(first, len(pieces), *refs),
        in_specs=[VM] * (2 + len(pieces) + len(sums)),
        out_specs=[VM] * 2,
        out_shape=[pltpu.VMEM(shape, F32), pltpu.VMEM(shape, BF16 if last else F32)],
        name="stage",
        compiler_params=params(8),
        cost_estimate=TINY,
    )(c_mine, c_other, *pieces, *sums)


def add_kernel(at, c_ref, *refs):
    x_refs, sum_refs, o_ref = refs[: len(at)], refs[len(at) : -1], refs[-1]
    for j in range(XS):
        rows = slice(j * LIVE, (j + 1) * LIVE)
        total = sum_refs[0][rows, :]
        for sum_ref in sum_refs[1:]:
            total = total + sum_ref[rows, :].astype(F32)
        for i, x_ref in zip(at, x_refs, strict=True):
            total = total + product(c_ref, j, i, (x_ref,))
        o_ref[rows, :] = total


def add(at, c_mine, pieces, sums, estimate):
    return pl.pallas_call(
        lambda *refs: add_kernel(at, *refs),
        in_specs=[VM] * (1 + len(at) + len(sums)),
        out_specs=VM,
        out_shape=pltpu.VMEM(sums[0].shape, F32),
        name="add",
        compiler_params=params(8),
        cost_estimate=estimate,
    )(c_mine, *pieces, *sums)


def total_kernel(c_ref, x_ref, mine_ref, other_ref, own_ref, *out_refs):
    for j, out_ref in enumerate((own_ref, *out_refs)):
        rows = slice(j * LIVE, (j + 1) * LIVE)
        total = product(c_ref, j, 9, (x_ref,))
        total = total + mine_ref[rows, :] + other_ref[rows, :].astype(F32)
        out_ref[...] = total.astype(out_ref.dtype)


def totals(c_mine, sibling, mine, other):
    shape = (LIVE, mine.shape[1])
    return pl.pallas_call(
        total_kernel,
        in_specs=[VM] * 4,
        out_specs=[VM] * XS,
        out_shape=[pltpu.VMEM(shape, F32)] + [pltpu.VMEM(shape, BF16)] * (XS - 1),
        name="totals",
        compiler_params=params(8),
        cost_estimate=TINY,
    )(c_mine, sibling, mine, other)


def finish_kernel(me_ref, counts_ref, own_ref, a_ref, b_ref, c_ref, n_ref, lead_ref, _, o_hbm, buffer, sem):
    within = lax.broadcasted_iota(jnp.int32, (1, LIVE), 1)
    retain = within < counts_ref[me_ref[0]]
    norm = n_ref[:, :1]
    size = buffer.shape[0] // 4
    copies = []
    for i in range(4):
        part = slice(i * size, (i + 1) * size)
        total = own_ref[:, part] + a_ref[:, part].astype(F32)
        total = total + b_ref[:, part].astype(F32) + c_ref[:, part].astype(F32)
        updated = jnp.transpose(total / norm)
        lead = lead_ref[part, :].astype(F32)
        buffer[part, :] = jnp.where(retain, updated, lead).astype(BF16)
        rows = pl.ds(i * size, size)
        copies.append(
            pltpu.make_async_copy(buffer.at[rows, :], o_hbm.at[rows, pl.ds(0, LIVE)], sem.at[i])
        )
        copies[-1].start()
    for copy in copies:
        copy.wait()


def finish(me, counts, own, received, norm, lead, out):
    return pl.pallas_call(
        finish_kernel,
        in_specs=[SM, SM] + [VM] * (XS + 2) + [HB],
        out_specs=HB,
        out_shape=jax.ShapeDtypeStruct(out.shape, BF16),
        scratch_shapes=[pltpu.VMEM(lead.shape, BF16), pltpu.SemaphoreType.DMA((4,))],
        input_output_aliases={4 + XS: 0},
        name="finish",
        compiler_params=params(4),
        cost_estimate=TINY,
    )(me, counts, own, *received, norm, lead, out)


def per_device(eigvecs, perm, counts, poles, weights, roots):
    me = lax.axis_index(("xl", "core", "z", "xh")).astype(jnp.int32).reshape(1)
    roots = roots.reshape(1, COLS)
    other_roots = cshift(roots)

    own, lead, rest = permute(in_hbm(eigvecs), in_hbm(perm.reshape(1, COLS)))
    p3 = around(own, 2)
    p2 = around(own, -1)
    p1 = around(hold(own, p3), 1)
    near = join(roots, hold(other_roots, own))
    far = [xshift(near, k) for k in (-1, -2, 1)]
    table, factors = tables(
        hold(in_hbm(counts), near), in_hbm(poles.reshape(-1, LANES)), in_hbm(weights.reshape(-1, LANES))
    )
    p4 = around(hold(p2, factors, *far), -1)
    p5 = around(hold(p3, *far), 1)
    c_other = cauchy(1, OTHER, me, table, factors, [hold(near, p3), *far])
    c_mine = cauchy(0, MINE, me, table, factors, [hold(near, c_other), *far])
    p6 = around(hold(p4, c_mine), -1)
    sums = stage(0, c_mine, c_other, (own, p2, p3), (), False)
    p7 = around(hold(p5, sums[0]), 1)
    mine, other = stage(3, c_mine, c_other, (p1, p4, p5), sums, True)
    other = cshift(other)
    p6 = hold(p6, mine)
    mine = add((6, 8), c_mine, (p6, cshift(p6)), (mine,), TINY)
    sibling = cshift(p7)
    mine = add((7,), c_mine, (p7,), (mine,), LONG)
    own_sum, *sent = totals(c_mine, sibling, mine, other)
    received = [xshift(sent[i], k) for i, k in ((1, 2), (0, 1), (2, -1))]
    norm, out = norms(table, factors, hold(roots, own_sum), rest)
    return finish(me, counts, own_sum, received, norm, lead, out)


def solution(mesh):
    fine_mesh = Mesh(mesh.devices.reshape(4, 2, 2, 8, 2), ("rows", "xl", "core", "z", "xh"))
    columns = ("xl", "core", "z", "xh")
    return jax.shard_map(
        per_device,
        mesh=fine_mesh,
        in_specs=(P("rows", columns), P(columns), P(), P(), P(), P(columns)),
        out_specs=P("rows", columns),
        check_vma=False,
    )
```

```python
import jax
import jax.numpy as jnp
from jax import lax
from jax.experimental import pallas as pl
from jax.experimental.pallas import tpu as pltpu
from jax.sharding import Mesh
from jax.sharding import PartitionSpec as P

LIVE = 256
COLS = 512
LANES = 128
TILES = LIVE // LANES
ZS = 8
XS = 4
TILE = 128
AWAY = (0, -1, 2, 1, -2, 3, -3, 4, 3, 4)
OTHER = range(6)
MINE = range(10)

VM = pl.BlockSpec(memory_space=pltpu.VMEM)
HB = pl.BlockSpec(memory_space=pltpu.HBM)
SM = pl.BlockSpec(memory_space=pltpu.SMEM)
F32 = jnp.float32
BF16 = jnp.bfloat16


def params(mib):
    return pltpu.CompilerParams(vmem_limit_bytes=mib << 20)


TINY = pl.CostEstimate(flops=1, transcendentals=0, bytes_accessed=1)
LONG = pl.CostEstimate(flops=10**10, transcendentals=0, bytes_accessed=1)


def xshift(a, k):
    pairs = []
    for i in range(XS):
        xl, xh = i // 2, i % 2
        x = (2 * xh + xl + k) % XS
        pairs.append((i, 2 * (x % 2) + x // 2))
    return lax.ppermute(a, ("xl", "xh"), pairs)


def around(a, way):
    up = [(z, (z + way) % ZS) for z in range(ZS)]
    down = [(ZS + z, ZS + (z - way) % ZS) for z in range(ZS)]
    return lax.ppermute(a, ("core", "z"), up + down)


def cshift(a):
    return lax.ppermute(a, "core", [(0, 1), (1, 0)])


def hold(a, *others):
    return lax.optimization_barrier((a, *others))[0]


def in_hbm(a):
    return pltpu.with_memory_space_constraint(a, pltpu.HBM)


def permute_kernel(e_hbm, perm_hbm, x_ref, lead_ref, rest_ref, e_ref, perm_ref, sem):
    rows = e_ref.shape[0]
    half = rows // 2
    order = pltpu.make_async_copy(perm_hbm, perm_ref, sem.at[2])
    order.start()
    copies = []
    for i in range(2):
        part = pl.ds(i * half, half)
        copies.append(pltpu.make_async_copy(e_hbm.at[part, :], e_ref.at[part, :], sem.at[i]))
        copies[-1].start()
    order.wait()
    source = lax.broadcasted_iota(jnp.int32, (COLS, COLS), 0)
    selector = jnp.where(source == perm_ref[...], 1.0, 0.0).astype(BF16)
    for i, copy in enumerate(copies):
        copy.wait()
        part = slice(i * half, (i + 1) * half)
        moved = jnp.dot(e_ref[part, :], selector, preferred_element_type=F32)
        x_ref[:, part] = jnp.transpose(moved[:, :LIVE]).astype(BF16)
        lead_ref[part, :] = moved[:, :LIVE].astype(BF16)
        rest_ref[part, :] = moved[:, LIVE:].astype(BF16)


def permute(eigvecs, perm):
    rows = eigvecs.shape[0]
    return pl.pallas_call(
        permute_kernel,
        in_specs=[HB, HB],
        out_specs=[VM] * 3,
        out_shape=[
            pltpu.VMEM((LIVE, rows), BF16),
            pltpu.VMEM((rows, LIVE), BF16),
            pltpu.VMEM((rows, COLS - LIVE), BF16),
        ],
        scratch_shapes=[
            pltpu.VMEM(eigvecs.shape, BF16),
            pltpu.VMEM(perm.shape, jnp.int32),
            pltpu.SemaphoreType.DMA((3,)),
        ],
        name="permute",
        compiler_params=params(8),
        cost_estimate=TINY,
    )(eigvecs, perm)


def table_kernel(counts_hbm, poles_hbm, weights_hbm, p_ref, f_ref, poles_ref, weights_ref, counts_ref, sem):
    first = pltpu.make_async_copy(poles_hbm, poles_ref, sem.at[0])
    second = pltpu.make_async_copy(weights_hbm, weights_ref, sem.at[1])
    third = pltpu.make_async_copy(counts_hbm, counts_ref, sem.at[2])
    third.start()
    first.start()
    second.start()
    third.wait()
    first.wait()
    second.wait()
    span, keep = COLS // LANES, LIVE // LANES
    at = lax.broadcasted_iota(jnp.int32, (keep, LANES), 0) * LANES
    at = at + lax.broadcasted_iota(jnp.int32, (keep, LANES), 1)
    for block in range(counts_ref.shape[0]):
        rows = slice(keep * block, keep * (block + 1))
        here = slice(span * block, span * block + keep)
        p_ref[rows, :] = poles_ref[here, :]
        f_ref[rows, :] = jnp.where(at < counts_ref[block], weights_ref[here, :], 0.0)


def tables(counts, poles, weights):
    shape = (counts.shape[0] * LIVE // LANES, LANES)
    return pl.pallas_call(
        table_kernel,
        in_specs=[HB, HB, HB],
        out_specs=[VM, VM],
        out_shape=[pltpu.VMEM(shape, F32)] * 2,
        scratch_shapes=[pltpu.VMEM(poles.shape, F32)] * 2
        + [pltpu.SMEM(counts.shape, jnp.int32), pltpu.SemaphoreType.DMA((3,))],
        name="tables",
        compiler_params=params(4),
        cost_estimate=TINY,
    )(counts, poles, weights)


def join_kernel(a_ref, b_ref, o_ref):
    o_ref[:, :COLS] = a_ref[...]
    o_ref[:, COLS:] = b_ref[...]


def join(a, b):
    return pl.pallas_call(
        join_kernel,
        in_specs=[VM, VM],
        out_specs=VM,
        out_shape=pltpu.VMEM((1, 2 * COLS), F32),
        name="join",
        compiler_params=params(4),
        cost_estimate=TINY,
    )(a, b)


def column(row):
    return jnp.transpose(jnp.broadcast_to(row, (8, LIVE)))[:, :1]


def cauchy_kernel(fc, pieces, me_ref, poles_ref, factors_ref, *refs):
    r_refs, c_ref = refs[:-1], refs[-1]
    me = me_ref[0]
    core, z = (me // 16) % 2, (me // 2) % ZS
    step = 1 - 2 * core
    for j in range(XS):
        roots = column(r_refs[j][:, fc * COLS : fc * COLS + LIVE])
        for t in range(LIVE // TILE):
            own = jnp.broadcast_to(roots[t * TILE : (t + 1) * TILE], (TILE, LANES))
            rows = slice(j * LIVE + t * TILE, j * LIVE + (t + 1) * TILE)
            for i, d in enumerate(pieces):
                ring = (z - step * AWAY[d] + ZS) % ZS
                block = me + 2 * (ring - z)
                if d >= 8:
                    block = block + 16 * step
                for h in range(TILES):
                    at = pl.ds(TILES * block + h, 1)
                    value = factors_ref[at, :] / (poles_ref[at, :] - own)
                    lo = (TILES * i + h) * LANES
                    c_ref[rows, lo : lo + LANES] = value.astype(BF16)


def cauchy(fc, pieces, me, poles, factors, roots):
    return pl.pallas_call(
        lambda *refs: cauchy_kernel(fc, pieces, *refs),
        in_specs=[SM] + [VM] * (2 + XS),
        out_specs=VM,
        out_shape=pltpu.VMEM((XS * LIVE, len(pieces) * LIVE), BF16),
        name="cauchy",
        compiler_params=params(8),
        cost_estimate=TINY,
    )(me, poles, factors, *roots)


def norm_kernel(poles_ref, factors_ref, r_ref, rest_ref, n_ref, o_hbm, sem):
    copy = pltpu.make_async_copy(rest_ref, o_hbm.at[:, pl.ds(LIVE, COLS - LIVE)], sem.at[0])
    copy.start()
    roots = column(r_ref[:, :LIVE])
    group = 16
    for t in range(LIVE // TILE):
        own = jnp.broadcast_to(roots[t * TILE : (t + 1) * TILE], (TILE, LANES))

        def step(g, total):
            for u in range(group):
                at = pl.ds(g * group + u, 1)
                value = factors_ref[at, :] / (poles_ref[at, :] - own)
                total = total + value * value
            return total

        total = lax.fori_loop(0, poles_ref.shape[0] // group, step, jnp.zeros((TILE, LANES), F32))
        norm = jnp.sqrt(jnp.sum(total, axis=1, keepdims=True))
        n_ref[t * TILE : (t + 1) * TILE, :] = jnp.broadcast_to(norm, (TILE, LANES))
    copy.wait()


def norms(poles, factors, roots, rest):
    return pl.pallas_call(
        norm_kernel,
        in_specs=[VM] * 4,
        out_specs=[VM, HB],
        out_shape=[
            pltpu.VMEM((LIVE, LANES), F32),
            jax.ShapeDtypeStruct((rest.shape[0], COLS), BF16),
        ],
        scratch_shapes=[pltpu.SemaphoreType.DMA((1,))],
        name="norms",
        compiler_params=params(4),
        cost_estimate=TINY,
    )(poles, factors, roots, rest)


def product(c_ref, j, first, x_refs):
    total = None
    for i, x_ref in enumerate(x_refs):
        lo = (first + i) * LIVE
        part = c_ref[j * LIVE : (j + 1) * LIVE, lo : lo + LIVE]
        piece = jnp.dot(part, x_ref[...], preferred_element_type=F32)
        total = piece if total is None else total + piece
    return total


def stage_kernel(first, count, c_mine, c_other, *refs):
    x_refs, refs = refs[:count], refs[count:]
    sums, outs = refs[:-2], refs[-2:]
    for i, c_ref in enumerate((c_mine, c_other)):
        for j in range(XS):
            rows = slice(j * LIVE, (j + 1) * LIVE)
            total = product(c_ref, j, first, x_refs)
            if sums:
                total = total + sums[i][rows, :]
            outs[i][rows, :] = total.astype(outs[i].dtype)


def stage(first, c_mine, c_other, pieces, sums, last):
    shape = (XS * LIVE, pieces[0].shape[1])
    return pl.pallas_call(
        lambda *refs: stage_kernel(first, len(pieces), *refs),
        in_specs=[VM] * (2 + len(pieces) + len(sums)),
        out_specs=[VM] * 2,
        out_shape=[pltpu.VMEM(shape, F32), pltpu.VMEM(shape, BF16 if last else F32)],
        name="stage",
        compiler_params=params(8),
        cost_estimate=TINY,
    )(c_mine, c_other, *pieces, *sums)


def add_kernel(at, c_ref, *refs):
    x_refs, sum_refs, o_ref = refs[: len(at)], refs[len(at) : -1], refs[-1]
    for j in range(XS):
        rows = slice(j * LIVE, (j + 1) * LIVE)
        total = sum_refs[0][rows, :]
        for sum_ref in sum_refs[1:]:
            total = total + sum_ref[rows, :].astype(F32)
        for i, x_ref in zip(at, x_refs, strict=True):
            total = total + product(c_ref, j, i, (x_ref,))
        o_ref[rows, :] = total


def add(at, c_mine, pieces, sums, estimate):
    return pl.pallas_call(
        lambda *refs: add_kernel(at, *refs),
        in_specs=[VM] * (1 + len(at) + len(sums)),
        out_specs=VM,
        out_shape=pltpu.VMEM(sums[0].shape, F32),
        name="add",
        compiler_params=params(8),
        cost_estimate=estimate,
    )(c_mine, *pieces, *sums)


def total_kernel(c_ref, x_ref, mine_ref, other_ref, own_ref, *out_refs):
    for j, out_ref in enumerate((own_ref, *out_refs)):
        rows = slice(j * LIVE, (j + 1) * LIVE)
        total = product(c_ref, j, 9, (x_ref,))
        total = total + mine_ref[rows, :] + other_ref[rows, :].astype(F32)
        out_ref[...] = total.astype(out_ref.dtype)


def totals(c_mine, sibling, mine, other):
    shape = (LIVE, mine.shape[1])
    return pl.pallas_call(
        total_kernel,
        in_specs=[VM] * 4,
        out_specs=[VM] * XS,
        out_shape=[pltpu.VMEM(shape, F32)] + [pltpu.VMEM(shape, BF16)] * (XS - 1),
        name="totals",
        compiler_params=params(8),
        cost_estimate=TINY,
    )(c_mine, sibling, mine, other)


def finish_kernel(me_ref, counts_ref, own_ref, a_ref, b_ref, c_ref, n_ref, lead_ref, _, o_hbm, buffer, sem):
    within = lax.broadcasted_iota(jnp.int32, (1, LIVE), 1)
    retain = within < counts_ref[me_ref[0]]
    norm = n_ref[:, :1]
    size = buffer.shape[0] // 4
    copies = []
    for i in range(4):
        part = slice(i * size, (i + 1) * size)
        total = own_ref[:, part] + a_ref[:, part].astype(F32)
        total = total + b_ref[:, part].astype(F32) + c_ref[:, part].astype(F32)
        updated = jnp.transpose(total / norm)
        lead = lead_ref[part, :].astype(F32)
        buffer[part, :] = jnp.where(retain, updated, lead).astype(BF16)
        rows = pl.ds(i * size, size)
        copies.append(
            pltpu.make_async_copy(buffer.at[rows, :], o_hbm.at[rows, pl.ds(0, LIVE)], sem.at[i])
        )
        copies[-1].start()
    for copy in copies:
        copy.wait()


def finish(me, counts, own, received, norm, lead, out):
    return pl.pallas_call(
        finish_kernel,
        in_specs=[SM, SM] + [VM] * (XS + 2) + [HB],
        out_specs=HB,
        out_shape=jax.ShapeDtypeStruct(out.shape, BF16),
        scratch_shapes=[pltpu.VMEM(lead.shape, BF16), pltpu.SemaphoreType.DMA((4,))],
        input_output_aliases={4 + XS: 0},
        name="finish",
        compiler_params=params(4),
        cost_estimate=TINY,
    )(me, counts, own, *received, norm, lead, out)


def per_device(eigvecs, perm, counts, poles, weights, roots):
    me = lax.axis_index(("xl", "core", "z", "xh")).astype(jnp.int32).reshape(1)
    roots = roots.reshape(1, COLS)
    other_roots = cshift(roots)

    own, lead, rest = permute(in_hbm(eigvecs), in_hbm(perm.reshape(1, COLS)))
    p3 = around(own, 2)
    p2 = around(own, -1)
    p1 = around(own, 1)
    near = join(roots, hold(other_roots, own))
    far = [xshift(near, k) for k in (-1, -2, 1)]
    table, factors = tables(
        hold(in_hbm(counts), near), in_hbm(poles.reshape(-1, LANES)), in_hbm(weights.reshape(-1, LANES))
    )
    p4 = around(hold(p2, factors, *far), -1)
    p5 = around(hold(p3, *far), 1)
    c_other = cauchy(1, OTHER, me, table, factors, [hold(near, p3), *far])
    c_mine = cauchy(0, MINE, me, table, factors, [hold(near, c_other), *far])
    p6 = around(hold(p4, c_mine), -1)
    sums = stage(0, c_mine, c_other, (own, p2, p3), (), False)
    p7 = around(hold(p5, sums[0]), 1)
    mine, other = stage(3, c_mine, c_other, (p1, p4, p5), sums, True)
    other = cshift(other)
    p6 = hold(p6, mine)
    sibling = cshift(p7)
    mine = add((7,), c_mine, (p7,), (mine,), LONG)
    mine = add((6, 8), c_mine, (p6, cshift(p6)), (mine,), TINY)
    own_sum, *sent = totals(c_mine, sibling, mine, other)
    received = [xshift(sent[i], k) for i, k in ((1, 2), (0, 1), (2, -1))]
    norm, out = norms(table, factors, hold(roots, own_sum), rest)
    return finish(me, counts, own_sum, received, norm, lead, out)


def solution(mesh):
    fine_mesh = Mesh(mesh.devices.reshape(4, 2, 2, 8, 2), ("rows", "xl", "core", "z", "xh"))
    columns = ("xl", "core", "z", "xh")
    return jax.shard_map(
        per_device,
        mesh=fine_mesh,
        in_specs=(P("rows", columns), P(columns), P(), P(), P(), P(columns)),
        out_specs=P("rows", columns),
        check_vma=False,
    )
```

```python
import jax
import jax.numpy as jnp
from jax import lax
from jax.experimental import pallas as pl
from jax.experimental.pallas import tpu as pltpu
from jax.sharding import Mesh
from jax.sharding import PartitionSpec as P

LIVE = 256
COLS = 512
LANES = 128
TILES = LIVE // LANES
ZS = 8
XS = 4
TILE = 128
AWAY = (0, -1, 2, 1, -2, 3, -3, 4, 3, 4)
OTHER = range(6)
MINE = range(10)

VM = pl.BlockSpec(memory_space=pltpu.VMEM)
HB = pl.BlockSpec(memory_space=pltpu.HBM)
SM = pl.BlockSpec(memory_space=pltpu.SMEM)
F32 = jnp.float32
BF16 = jnp.bfloat16


def params(mib):
    return pltpu.CompilerParams(vmem_limit_bytes=mib << 20)


TINY = pl.CostEstimate(flops=1, transcendentals=0, bytes_accessed=1)
LONG = pl.CostEstimate(flops=10**10, transcendentals=0, bytes_accessed=1)


def xshift(a, k):
    pairs = []
    for i in range(XS):
        xl, xh = i // 2, i % 2
        x = (2 * xh + xl + k) % XS
        pairs.append((i, 2 * (x % 2) + x // 2))
    return lax.ppermute(a, ("xl", "xh"), pairs)


def around(a, way):
    up = [(z, (z + way) % ZS) for z in range(ZS)]
    down = [(ZS + z, ZS + (z - way) % ZS) for z in range(ZS)]
    return lax.ppermute(a, ("core", "z"), up + down)


def cshift(a):
    return lax.ppermute(a, "core", [(0, 1), (1, 0)])


def hold(a, *others):
    return lax.optimization_barrier((a, *others))[0]


def in_hbm(a):
    return pltpu.with_memory_space_constraint(a, pltpu.HBM)


def permute_kernel(e_hbm, perm_hbm, x_ref, lead_ref, rest_ref, e_ref, perm_ref, sem):
    rows = e_ref.shape[0]
    half = rows // 2
    order = pltpu.make_async_copy(perm_hbm, perm_ref, sem.at[2])
    order.start()
    copies = []
    for i in range(2):
        part = pl.ds(i * half, half)
        copies.append(pltpu.make_async_copy(e_hbm.at[part, :], e_ref.at[part, :], sem.at[i]))
        copies[-1].start()
    order.wait()
    source = lax.broadcasted_iota(jnp.int32, (COLS, COLS), 0)
    selector = jnp.where(source == perm_ref[...], 1.0, 0.0).astype(BF16)
    for i, copy in enumerate(copies):
        copy.wait()
        part = slice(i * half, (i + 1) * half)
        moved = jnp.dot(e_ref[part, :], selector, preferred_element_type=F32)
        x_ref[:, part] = jnp.transpose(moved[:, :LIVE]).astype(BF16)
        lead_ref[part, :] = moved[:, :LIVE].astype(BF16)
        rest_ref[part, :] = moved[:, LIVE:].astype(BF16)


def permute(eigvecs, perm):
    rows = eigvecs.shape[0]
    return pl.pallas_call(
        permute_kernel,
        in_specs=[HB, HB],
        out_specs=[VM] * 3,
        out_shape=[
            pltpu.VMEM((LIVE, rows), BF16),
            pltpu.VMEM((rows, LIVE), BF16),
            pltpu.VMEM((rows, COLS - LIVE), BF16),
        ],
        scratch_shapes=[
            pltpu.VMEM(eigvecs.shape, BF16),
            pltpu.VMEM(perm.shape, jnp.int32),
            pltpu.SemaphoreType.DMA((3,)),
        ],
        name="permute",
        compiler_params=params(8),
        cost_estimate=TINY,
    )(eigvecs, perm)


def table_kernel(counts_hbm, poles_hbm, weights_hbm, p_ref, f_ref, poles_ref, weights_ref, counts_ref, sem):
    first = pltpu.make_async_copy(poles_hbm, poles_ref, sem.at[0])
    second = pltpu.make_async_copy(weights_hbm, weights_ref, sem.at[1])
    third = pltpu.make_async_copy(counts_hbm, counts_ref, sem.at[2])
    third.start()
    first.start()
    second.start()
    third.wait()
    first.wait()
    second.wait()
    span, keep = COLS // LANES, LIVE // LANES
    at = lax.broadcasted_iota(jnp.int32, (keep, LANES), 0) * LANES
    at = at + lax.broadcasted_iota(jnp.int32, (keep, LANES), 1)
    for block in range(counts_ref.shape[0]):
        rows = slice(keep * block, keep * (block + 1))
        here = slice(span * block, span * block + keep)
        p_ref[rows, :] = poles_ref[here, :]
        f_ref[rows, :] = jnp.where(at < counts_ref[block], weights_ref[here, :], 0.0)


def tables(counts, poles, weights):
    shape = (counts.shape[0] * LIVE // LANES, LANES)
    return pl.pallas_call(
        table_kernel,
        in_specs=[HB, HB, HB],
        out_specs=[VM, VM],
        out_shape=[pltpu.VMEM(shape, F32)] * 2,
        scratch_shapes=[pltpu.VMEM(poles.shape, F32)] * 2
        + [pltpu.SMEM(counts.shape, jnp.int32), pltpu.SemaphoreType.DMA((3,))],
        name="tables",
        compiler_params=params(4),
        cost_estimate=TINY,
    )(counts, poles, weights)


def join_kernel(a_ref, b_ref, o_ref):
    o_ref[:, :COLS] = a_ref[...]
    o_ref[:, COLS:] = b_ref[...]


def join(a, b):
    return pl.pallas_call(
        join_kernel,
        in_specs=[VM, VM],
        out_specs=VM,
        out_shape=pltpu.VMEM((1, 2 * COLS), F32),
        name="join",
        compiler_params=params(4),
        cost_estimate=TINY,
    )(a, b)


def column(row):
    return jnp.transpose(jnp.broadcast_to(row, (8, LIVE)))[:, :1]


def cauchy_kernel(fc, pieces, me_ref, poles_ref, factors_ref, *refs):
    r_refs, c_ref = refs[:-1], refs[-1]
    me = me_ref[0]
    core, z = (me // 16) % 2, (me // 2) % ZS
    step = 1 - 2 * core
    for j in range(XS):
        roots = column(r_refs[j][:, fc * COLS : fc * COLS + LIVE])
        for t in range(LIVE // TILE):
            own = jnp.broadcast_to(roots[t * TILE : (t + 1) * TILE], (TILE, LANES))
            rows = slice(j * LIVE + t * TILE, j * LIVE + (t + 1) * TILE)
            for i, d in enumerate(pieces):
                ring = (z - step * AWAY[d] + ZS) % ZS
                block = me + 2 * (ring - z)
                if d >= 8:
                    block = block + 16 * step
                for h in range(TILES):
                    at = pl.ds(TILES * block + h, 1)
                    value = factors_ref[at, :] / (poles_ref[at, :] - own)
                    lo = (TILES * i + h) * LANES
                    c_ref[rows, lo : lo + LANES] = value.astype(BF16)


def cauchy(fc, pieces, me, poles, factors, roots):
    return pl.pallas_call(
        lambda *refs: cauchy_kernel(fc, pieces, *refs),
        in_specs=[SM] + [VM] * (2 + XS),
        out_specs=VM,
        out_shape=pltpu.VMEM((XS * LIVE, len(pieces) * LIVE), BF16),
        name="cauchy",
        compiler_params=params(8),
        cost_estimate=TINY,
    )(me, poles, factors, *roots)


def norm_kernel(poles_ref, factors_ref, r_ref, rest_ref, n_ref, o_hbm, sem):
    copy = pltpu.make_async_copy(rest_ref, o_hbm.at[:, pl.ds(LIVE, COLS - LIVE)], sem.at[0])
    copy.start()
    roots = column(r_ref[:, :LIVE])
    group = 16
    for t in range(LIVE // TILE):
        own = jnp.broadcast_to(roots[t * TILE : (t + 1) * TILE], (TILE, LANES))

        def step(g, total):
            for u in range(group):
                at = pl.ds(g * group + u, 1)
                value = factors_ref[at, :] / (poles_ref[at, :] - own)
                total = total + value * value
            return total

        total = lax.fori_loop(0, poles_ref.shape[0] // group, step, jnp.zeros((TILE, LANES), F32))
        norm = jnp.sqrt(jnp.sum(total, axis=1, keepdims=True))
        n_ref[t * TILE : (t + 1) * TILE, :] = jnp.broadcast_to(norm, (TILE, LANES))
    copy.wait()


def norms(poles, factors, roots, rest):
    return pl.pallas_call(
        norm_kernel,
        in_specs=[VM] * 4,
        out_specs=[VM, HB],
        out_shape=[
            pltpu.VMEM((LIVE, LANES), F32),
            jax.ShapeDtypeStruct((rest.shape[0], COLS), BF16),
        ],
        scratch_shapes=[pltpu.SemaphoreType.DMA((1,))],
        name="norms",
        compiler_params=params(4),
        cost_estimate=TINY,
    )(poles, factors, roots, rest)


def product(c_ref, j, first, x_refs):
    total = None
    for i, x_ref in enumerate(x_refs):
        lo = (first + i) * LIVE
        part = c_ref[j * LIVE : (j + 1) * LIVE, lo : lo + LIVE]
        piece = jnp.dot(part, x_ref[...], preferred_element_type=F32)
        total = piece if total is None else total + piece
    return total


def stage_kernel(first, count, c_mine, c_other, *refs):
    x_refs, refs = refs[:count], refs[count:]
    sums, outs = refs[:-2], refs[-2:]
    for i, c_ref in enumerate((c_mine, c_other)):
        for j in range(XS):
            rows = slice(j * LIVE, (j + 1) * LIVE)
            total = product(c_ref, j, first, x_refs)
            if sums:
                total = total + sums[i][rows, :]
            outs[i][rows, :] = total.astype(outs[i].dtype)


def stage(first, c_mine, c_other, pieces, sums, last):
    shape = (XS * LIVE, pieces[0].shape[1])
    return pl.pallas_call(
        lambda *refs: stage_kernel(first, len(pieces), *refs),
        in_specs=[VM] * (2 + len(pieces) + len(sums)),
        out_specs=[VM] * 2,
        out_shape=[pltpu.VMEM(shape, F32), pltpu.VMEM(shape, BF16 if last else F32)],
        name="stage",
        compiler_params=params(8),
        cost_estimate=TINY,
    )(c_mine, c_other, *pieces, *sums)


def add_kernel(at, c_ref, *refs):
    x_refs, sum_refs, o_ref = refs[: len(at)], refs[len(at) : -1], refs[-1]
    for j in range(XS):
        rows = slice(j * LIVE, (j + 1) * LIVE)
        total = sum_refs[0][rows, :]
        for sum_ref in sum_refs[1:]:
            total = total + sum_ref[rows, :].astype(F32)
        for i, x_ref in zip(at, x_refs, strict=True):
            total = total + product(c_ref, j, i, (x_ref,))
        o_ref[rows, :] = total


def add(at, c_mine, pieces, sums, estimate):
    return pl.pallas_call(
        lambda *refs: add_kernel(at, *refs),
        in_specs=[VM] * (1 + len(at) + len(sums)),
        out_specs=VM,
        out_shape=pltpu.VMEM(sums[0].shape, F32),
        name="add",
        compiler_params=params(8),
        cost_estimate=estimate,
    )(c_mine, *pieces, *sums)


def total_kernel(c_ref, x_ref, mine_ref, other_ref, own_ref, *out_refs):
    for j, out_ref in enumerate((own_ref, *out_refs)):
        rows = slice(j * LIVE, (j + 1) * LIVE)
        total = product(c_ref, j, 9, (x_ref,))
        total = total + mine_ref[rows, :] + other_ref[rows, :].astype(F32)
        out_ref[...] = total.astype(out_ref.dtype)


def totals(c_mine, sibling, mine, other):
    shape = (LIVE, mine.shape[1])
    return pl.pallas_call(
        total_kernel,
        in_specs=[VM] * 4,
        out_specs=[VM] * XS,
        out_shape=[pltpu.VMEM(shape, F32)] + [pltpu.VMEM(shape, BF16)] * (XS - 1),
        name="totals",
        compiler_params=params(8),
        cost_estimate=TINY,
    )(c_mine, sibling, mine, other)


def finish_kernel(me_ref, counts_ref, own_ref, a_ref, b_ref, c_ref, n_ref, lead_ref, _, o_hbm, buffer, sem):
    within = lax.broadcasted_iota(jnp.int32, (1, LIVE), 1)
    retain = within < counts_ref[me_ref[0]]
    norm = n_ref[:, :1]
    size = buffer.shape[0] // 4
    copies = []
    for i in range(4):
        part = slice(i * size, (i + 1) * size)
        total = own_ref[:, part] + a_ref[:, part].astype(F32)
        total = total + b_ref[:, part].astype(F32) + c_ref[:, part].astype(F32)
        updated = jnp.transpose(total / norm)
        lead = lead_ref[part, :].astype(F32)
        buffer[part, :] = jnp.where(retain, updated, lead).astype(BF16)
        rows = pl.ds(i * size, size)
        copies.append(
            pltpu.make_async_copy(buffer.at[rows, :], o_hbm.at[rows, pl.ds(0, LIVE)], sem.at[i])
        )
        copies[-1].start()
    for copy in copies:
        copy.wait()


def finish(me, counts, own, received, norm, lead, out):
    return pl.pallas_call(
        finish_kernel,
        in_specs=[SM, SM] + [VM] * (XS + 2) + [HB],
        out_specs=HB,
        out_shape=jax.ShapeDtypeStruct(out.shape, BF16),
        scratch_shapes=[pltpu.VMEM(lead.shape, BF16), pltpu.SemaphoreType.DMA((4,))],
        input_output_aliases={4 + XS: 0},
        name="finish",
        compiler_params=params(4),
        cost_estimate=TINY,
    )(me, counts, own, *received, norm, lead, out)


def per_device(eigvecs, perm, counts, poles, weights, roots):
    me = lax.axis_index(("xl", "core", "z", "xh")).astype(jnp.int32).reshape(1)
    roots = roots.reshape(1, COLS)
    other_roots = cshift(roots)

    own, lead, rest = permute(in_hbm(eigvecs), in_hbm(perm.reshape(1, COLS)))
    p3 = around(own, 2)
    p2 = around(own, -1)
    p1 = around(own, 1)
    near = join(roots, hold(other_roots, own))
    far = [xshift(near, k) for k in (-1, -2, 1)]
    table, factors = tables(
        hold(in_hbm(counts), near), in_hbm(poles.reshape(-1, LANES)), in_hbm(weights.reshape(-1, LANES))
    )
    p4 = around(hold(p2, factors, far[0]), -1)
    p5 = around(hold(p3, far[0]), 1)
    c_other = cauchy(1, OTHER, me, table, factors, [hold(near, p3), *far])
    c_mine = cauchy(0, MINE, me, table, factors, [hold(near, c_other), *far])
    p6 = around(hold(p4, *far), -1)
    sums = stage(0, c_mine, c_other, (hold(own, p5), p2, p3), (), False)
    p7 = around(hold(p5, *far), 1)
    mine, other = stage(3, c_mine, c_other, (p1, p4, p5), sums, True)
    other = cshift(other)
    p6 = hold(p6, mine)
    sibling = cshift(p7)
    mine = add((7,), c_mine, (p7,), (mine,), LONG)
    mine = add((6, 8), c_mine, (p6, cshift(p6)), (mine,), TINY)
    own_sum, *sent = totals(c_mine, sibling, mine, other)
    received = [xshift(sent[i], k) for i, k in ((1, 2), (0, 1), (2, -1))]
    norm, out = norms(table, factors, hold(roots, own_sum), rest)
    return finish(me, counts, own_sum, received, norm, lead, out)


def solution(mesh):
    fine_mesh = Mesh(mesh.devices.reshape(4, 2, 2, 8, 2), ("rows", "xl", "core", "z", "xh"))
    columns = ("xl", "core", "z", "xh")
    return jax.shard_map(
        per_device,
        mesh=fine_mesh,
        in_specs=(P("rows", columns), P(columns), P(), P(), P(), P(columns)),
        out_specs=P("rows", columns),
        check_vma=False,
    )
```

```python
import jax
import jax.numpy as jnp
from jax import lax
from jax.experimental import pallas as pl
from jax.experimental.pallas import tpu as pltpu
from jax.sharding import Mesh
from jax.sharding import PartitionSpec as P

LIVE = 256
COLS = 512
LANES = 128
TILES = LIVE // LANES
ZS = 8
XS = 4
TILE = 128
AWAY = (0, -1, 2, 1, -2, 3, -3, 4, 3, 4)
OTHER = range(6)
MINE = range(10)

VM = pl.BlockSpec(memory_space=pltpu.VMEM)
HB = pl.BlockSpec(memory_space=pltpu.HBM)
SM = pl.BlockSpec(memory_space=pltpu.SMEM)
F32 = jnp.float32
BF16 = jnp.bfloat16


def params(mib):
    return pltpu.CompilerParams(vmem_limit_bytes=mib << 20)


TINY = pl.CostEstimate(flops=1, transcendentals=0, bytes_accessed=1)
LONG = pl.CostEstimate(flops=10**10, transcendentals=0, bytes_accessed=1)


def xshift(a, k):
    pairs = []
    for i in range(XS):
        xl, xh = i // 2, i % 2
        x = (2 * xh + xl + k) % XS
        pairs.append((i, 2 * (x % 2) + x // 2))
    return lax.ppermute(a, ("xl", "xh"), pairs)


def around(a, way):
    up = [(z, (z + way) % ZS) for z in range(ZS)]
    down = [(ZS + z, ZS + (z - way) % ZS) for z in range(ZS)]
    return lax.ppermute(a, ("core", "z"), up + down)


def cshift(a):
    return lax.ppermute(a, "core", [(0, 1), (1, 0)])


def hold(a, *others):
    return lax.optimization_barrier((a, *others))[0]


def in_hbm(a):
    return pltpu.with_memory_space_constraint(a, pltpu.HBM)


def permute_kernel(e_hbm, perm_hbm, x_ref, lead_ref, rest_ref, e_ref, perm_ref, sem):
    rows = e_ref.shape[0]
    half = rows // 2
    order = pltpu.make_async_copy(perm_hbm, perm_ref, sem.at[2])
    order.start()
    copies = []
    for i in range(2):
        part = pl.ds(i * half, half)
        copies.append(pltpu.make_async_copy(e_hbm.at[part, :], e_ref.at[part, :], sem.at[i]))
        copies[-1].start()
    order.wait()
    source = lax.broadcasted_iota(jnp.int32, (COLS, COLS), 0)
    selector = jnp.where(source == perm_ref[...], 1.0, 0.0).astype(BF16)
    for i, copy in enumerate(copies):
        copy.wait()
        part = slice(i * half, (i + 1) * half)
        moved = jnp.dot(e_ref[part, :], selector, preferred_element_type=F32)
        x_ref[:, part] = jnp.transpose(moved[:, :LIVE]).astype(BF16)
        lead_ref[part, :] = moved[:, :LIVE].astype(BF16)
        rest_ref[part, :] = moved[:, LIVE:].astype(BF16)


def permute(eigvecs, perm):
    rows = eigvecs.shape[0]
    return pl.pallas_call(
        permute_kernel,
        in_specs=[HB, HB],
        out_specs=[VM] * 3,
        out_shape=[
            pltpu.VMEM((LIVE, rows), BF16),
            pltpu.VMEM((rows, LIVE), BF16),
            pltpu.VMEM((rows, COLS - LIVE), BF16),
        ],
        scratch_shapes=[
            pltpu.VMEM(eigvecs.shape, BF16),
            pltpu.VMEM(perm.shape, jnp.int32),
            pltpu.SemaphoreType.DMA((3,)),
        ],
        name="permute",
        compiler_params=params(8),
        cost_estimate=TINY,
    )(eigvecs, perm)


def table_kernel(counts_hbm, poles_hbm, weights_hbm, p_ref, f_ref, poles_ref, weights_ref, counts_ref, sem):
    first = pltpu.make_async_copy(poles_hbm, poles_ref, sem.at[0])
    second = pltpu.make_async_copy(weights_hbm, weights_ref, sem.at[1])
    third = pltpu.make_async_copy(counts_hbm, counts_ref, sem.at[2])
    third.start()
    first.start()
    second.start()
    third.wait()
    first.wait()
    second.wait()
    span, keep = COLS // LANES, LIVE // LANES
    at = lax.broadcasted_iota(jnp.int32, (keep, LANES), 0) * LANES
    at = at + lax.broadcasted_iota(jnp.int32, (keep, LANES), 1)
    for block in range(counts_ref.shape[0]):
        rows = slice(keep * block, keep * (block + 1))
        here = slice(span * block, span * block + keep)
        p_ref[rows, :] = poles_ref[here, :]
        f_ref[rows, :] = jnp.where(at < counts_ref[block], weights_ref[here, :], 0.0)


def tables(counts, poles, weights):
    shape = (counts.shape[0] * LIVE // LANES, LANES)
    return pl.pallas_call(
        table_kernel,
        in_specs=[HB, HB, HB],
        out_specs=[VM, VM],
        out_shape=[pltpu.VMEM(shape, F32)] * 2,
        scratch_shapes=[pltpu.VMEM(poles.shape, F32)] * 2
        + [pltpu.SMEM(counts.shape, jnp.int32), pltpu.SemaphoreType.DMA((3,))],
        name="tables",
        compiler_params=params(4),
        cost_estimate=TINY,
    )(counts, poles, weights)


def join_kernel(a_ref, b_ref, o_ref):
    o_ref[:, :COLS] = a_ref[...]
    o_ref[:, COLS:] = b_ref[...]


def join(a, b):
    return pl.pallas_call(
        join_kernel,
        in_specs=[VM, VM],
        out_specs=VM,
        out_shape=pltpu.VMEM((1, 2 * COLS), F32),
        name="join",
        compiler_params=params(4),
        cost_estimate=TINY,
    )(a, b)


def column(row):
    return jnp.transpose(jnp.broadcast_to(row, (8, LIVE)))[:, :1]


def cauchy_kernel(fc, pieces, me_ref, poles_ref, factors_ref, *refs):
    r_refs, c_ref = refs[:-1], refs[-1]
    me = me_ref[0]
    core, z = (me // 16) % 2, (me // 2) % ZS
    step = 1 - 2 * core
    for j in range(XS):
        roots = column(r_refs[j][:, fc * COLS : fc * COLS + LIVE])
        for t in range(LIVE // TILE):
            own = jnp.broadcast_to(roots[t * TILE : (t + 1) * TILE], (TILE, LANES))
            rows = slice(j * LIVE + t * TILE, j * LIVE + (t + 1) * TILE)
            for i, d in enumerate(pieces):
                ring = (z - step * AWAY[d] + ZS) % ZS
                block = me + 2 * (ring - z)
                if d >= 8:
                    block = block + 16 * step
                for h in range(TILES):
                    at = pl.ds(TILES * block + h, 1)
                    value = factors_ref[at, :] / (poles_ref[at, :] - own)
                    lo = (TILES * i + h) * LANES
                    c_ref[rows, lo : lo + LANES] = value.astype(BF16)


def cauchy(fc, pieces, me, poles, factors, roots):
    return pl.pallas_call(
        lambda *refs: cauchy_kernel(fc, pieces, *refs),
        in_specs=[SM] + [VM] * (2 + XS),
        out_specs=VM,
        out_shape=pltpu.VMEM((XS * LIVE, len(pieces) * LIVE), BF16),
        name="cauchy",
        compiler_params=params(8),
        cost_estimate=TINY,
    )(me, poles, factors, *roots)


def norm_kernel(poles_ref, factors_ref, r_ref, rest_ref, n_ref, o_hbm, sem):
    copy = pltpu.make_async_copy(rest_ref, o_hbm.at[:, pl.ds(LIVE, COLS - LIVE)], sem.at[0])
    copy.start()
    roots = column(r_ref[:, :LIVE])
    group = 16
    for t in range(LIVE // TILE):
        own = jnp.broadcast_to(roots[t * TILE : (t + 1) * TILE], (TILE, LANES))

        def step(g, total):
            for u in range(group):
                at = pl.ds(g * group + u, 1)
                value = factors_ref[at, :] / (poles_ref[at, :] - own)
                total = total + value * value
            return total

        total = lax.fori_loop(0, poles_ref.shape[0] // group, step, jnp.zeros((TILE, LANES), F32))
        norm = jnp.sqrt(jnp.sum(total, axis=1, keepdims=True))
        n_ref[t * TILE : (t + 1) * TILE, :] = jnp.broadcast_to(norm, (TILE, LANES))
    copy.wait()


def norms(poles, factors, roots, rest):
    return pl.pallas_call(
        norm_kernel,
        in_specs=[VM] * 4,
        out_specs=[VM, HB],
        out_shape=[
            pltpu.VMEM((LIVE, LANES), F32),
            jax.ShapeDtypeStruct((rest.shape[0], COLS), BF16),
        ],
        scratch_shapes=[pltpu.SemaphoreType.DMA((1,))],
        name="norms",
        compiler_params=params(4),
        cost_estimate=TINY,
    )(poles, factors, roots, rest)


def product(c_ref, j, first, x_refs):
    total = None
    for i, x_ref in enumerate(x_refs):
        lo = (first + i) * LIVE
        part = c_ref[j * LIVE : (j + 1) * LIVE, lo : lo + LIVE]
        piece = jnp.dot(part, x_ref[...], preferred_element_type=F32)
        total = piece if total is None else total + piece
    return total


def stage_kernel(first, count, c_mine, c_other, *refs):
    x_refs, refs = refs[:count], refs[count:]
    sums, outs = refs[:-2], refs[-2:]
    for i, c_ref in enumerate((c_mine, c_other)):
        for j in range(XS):
            rows = slice(j * LIVE, (j + 1) * LIVE)
            total = product(c_ref, j, first, x_refs)
            if sums:
                total = total + sums[i][rows, :]
            outs[i][rows, :] = total.astype(outs[i].dtype)


def stage(first, c_mine, c_other, pieces, sums, last):
    shape = (XS * LIVE, pieces[0].shape[1])
    return pl.pallas_call(
        lambda *refs: stage_kernel(first, len(pieces), *refs),
        in_specs=[VM] * (2 + len(pieces) + len(sums)),
        out_specs=[VM] * 2,
        out_shape=[pltpu.VMEM(shape, F32), pltpu.VMEM(shape, BF16 if last else F32)],
        name="stage",
        compiler_params=params(8),
        cost_estimate=TINY,
    )(c_mine, c_other, *pieces, *sums)


def add_kernel(at, c_ref, *refs):
    x_refs, sum_refs, o_ref = refs[: len(at)], refs[len(at) : -1], refs[-1]
    for j in range(XS):
        rows = slice(j * LIVE, (j + 1) * LIVE)
        total = sum_refs[0][rows, :]
        for sum_ref in sum_refs[1:]:
            total = total + sum_ref[rows, :].astype(F32)
        for i, x_ref in zip(at, x_refs, strict=True):
            total = total + product(c_ref, j, i, (x_ref,))
        o_ref[rows, :] = total


def add(at, c_mine, pieces, sums, estimate):
    return pl.pallas_call(
        lambda *refs: add_kernel(at, *refs),
        in_specs=[VM] * (1 + len(at) + len(sums)),
        out_specs=VM,
        out_shape=pltpu.VMEM(sums[0].shape, F32),
        name="add",
        compiler_params=params(8),
        cost_estimate=estimate,
    )(c_mine, *pieces, *sums)


def total_kernel(c_ref, x_ref, mine_ref, other_ref, own_ref, *out_refs):
    for j, out_ref in enumerate((own_ref, *out_refs)):
        rows = slice(j * LIVE, (j + 1) * LIVE)
        total = product(c_ref, j, 9, (x_ref,))
        total = total + mine_ref[rows, :] + other_ref[rows, :].astype(F32)
        out_ref[...] = total.astype(out_ref.dtype)


def totals(c_mine, sibling, mine, other):
    shape = (LIVE, mine.shape[1])
    return pl.pallas_call(
        total_kernel,
        in_specs=[VM] * 4,
        out_specs=[VM] * XS,
        out_shape=[pltpu.VMEM(shape, F32)] + [pltpu.VMEM(shape, BF16)] * (XS - 1),
        name="totals",
        compiler_params=params(8),
        cost_estimate=TINY,
    )(c_mine, sibling, mine, other)


def finish_kernel(me_ref, counts_ref, own_ref, a_ref, b_ref, c_ref, n_ref, lead_ref, _, o_hbm, buffer, sem):
    within = lax.broadcasted_iota(jnp.int32, (1, LIVE), 1)
    retain = within < counts_ref[me_ref[0]]
    norm = n_ref[:, :1]
    size = buffer.shape[0] // 4
    copies = []
    for i in range(4):
        part = slice(i * size, (i + 1) * size)
        total = own_ref[:, part] + a_ref[:, part].astype(F32)
        total = total + b_ref[:, part].astype(F32) + c_ref[:, part].astype(F32)
        updated = jnp.transpose(total / norm)
        lead = lead_ref[part, :].astype(F32)
        buffer[part, :] = jnp.where(retain, updated, lead).astype(BF16)
        rows = pl.ds(i * size, size)
        copies.append(
            pltpu.make_async_copy(buffer.at[rows, :], o_hbm.at[rows, pl.ds(0, LIVE)], sem.at[i])
        )
        copies[-1].start()
    for copy in copies:
        copy.wait()


def finish(me, counts, own, received, norm, lead, out):
    return pl.pallas_call(
        finish_kernel,
        in_specs=[SM, SM] + [VM] * (XS + 2) + [HB],
        out_specs=HB,
        out_shape=jax.ShapeDtypeStruct(out.shape, BF16),
        scratch_shapes=[pltpu.VMEM(lead.shape, BF16), pltpu.SemaphoreType.DMA((4,))],
        input_output_aliases={4 + XS: 0},
        name="finish",
        compiler_params=params(4),
        cost_estimate=TINY,
    )(me, counts, own, *received, norm, lead, out)


def per_device(eigvecs, perm, counts, poles, weights, roots):
    me = lax.axis_index(("xl", "core", "z", "xh")).astype(jnp.int32).reshape(1)
    roots = roots.reshape(1, COLS)
    other_roots = cshift(roots)

    own, lead, rest = permute(in_hbm(eigvecs), in_hbm(perm.reshape(1, COLS)))
    p3 = around(own, 2)
    p2 = around(own, -1)
    p1 = around(own, 1)
    near = join(roots, hold(other_roots, own))
    far = [xshift(near, k) for k in (-1, -2, 1)]
    table, factors = tables(
        hold(in_hbm(counts), near), in_hbm(poles.reshape(-1, LANES)), in_hbm(weights.reshape(-1, LANES))
    )
    p4 = around(hold(p2, factors, *far), -1)
    p5 = around(hold(p3, *far), 1)
    c_other = cauchy(1, OTHER, me, table, factors, [hold(near, p3), *far])
    c_mine = cauchy(0, MINE, me, table, factors, [hold(near, c_other), *far])
    p6 = around(hold(p4, c_mine), -1)
    sums = stage(0, c_mine, c_other, (own, p2, p3), (), False)
    p7 = around(hold(p5, sums[0]), 1)
    mine, other = stage(3, c_mine, c_other, (p1, p4, p5), sums, True)
    other = cshift(other)
    p6 = hold(p6, mine)
    sibling = cshift(p7)
    mine = add((7,), c_mine, (p7,), (mine,), LONG)
    mine = add((6, 8), c_mine, (p6, cshift(p6)), (mine,), TINY)
    own_sum, *sent = totals(c_mine, sibling, mine, other)
    received = [xshift(sent[i], k) for i, k in ((0, 1), (2, -1), (1, 2))]
    norm, out = norms(table, factors, hold(roots, own_sum), rest)
    return finish(me, counts, own_sum, received, norm, lead, out)


def solution(mesh):
    fine_mesh = Mesh(mesh.devices.reshape(4, 2, 2, 8, 2), ("rows", "xl", "core", "z", "xh"))
    columns = ("xl", "core", "z", "xh")
    return jax.shard_map(
        per_device,
        mesh=fine_mesh,
        in_specs=(P("rows", columns), P(columns), P(), P(), P(), P(columns)),
        out_specs=P("rows", columns),
        check_vma=False,
    )
```

```python
import jax
import jax.numpy as jnp
from jax import lax
from jax.experimental import pallas as pl
from jax.experimental.pallas import tpu as pltpu
from jax.sharding import Mesh
from jax.sharding import PartitionSpec as P

LIVE = 256
COLS = 512
LANES = 128
TILES = LIVE // LANES
ZS = 8
XS = 4
TILE = 128
AWAY = (0, -1, 2, 1, -2, 3, -3, 4, 3, 4)
OTHER = range(6)
MINE = range(10)

VM = pl.BlockSpec(memory_space=pltpu.VMEM)
HB = pl.BlockSpec(memory_space=pltpu.HBM)
SM = pl.BlockSpec(memory_space=pltpu.SMEM)
F32 = jnp.float32
BF16 = jnp.bfloat16


def params(mib):
    return pltpu.CompilerParams(vmem_limit_bytes=mib << 20)


TINY = pl.CostEstimate(flops=1, transcendentals=0, bytes_accessed=1)
LONG = pl.CostEstimate(flops=10**10, transcendentals=0, bytes_accessed=1)


def xshift(a, k):
    pairs = []
    for i in range(XS):
        xl, xh = i // 2, i % 2
        x = (2 * xh + xl + k) % XS
        pairs.append((i, 2 * (x % 2) + x // 2))
    return lax.ppermute(a, ("xl", "xh"), pairs)


def around(a, way):
    up = [(z, (z + way) % ZS) for z in range(ZS)]
    down = [(ZS + z, ZS + (z - way) % ZS) for z in range(ZS)]
    return lax.ppermute(a, ("core", "z"), up + down)


def cshift(a):
    return lax.ppermute(a, "core", [(0, 1), (1, 0)])


def hold(a, *others):
    return lax.optimization_barrier((a, *others))[0]


def in_hbm(a):
    return pltpu.with_memory_space_constraint(a, pltpu.HBM)


def permute_kernel(e_hbm, perm_hbm, x_ref, lead_ref, rest_ref, e_ref, perm_ref, sem):
    rows = e_ref.shape[0]
    half = rows // 2
    order = pltpu.make_async_copy(perm_hbm, perm_ref, sem.at[2])
    order.start()
    copies = []
    for i in range(2):
        part = pl.ds(i * half, half)
        copies.append(pltpu.make_async_copy(e_hbm.at[part, :], e_ref.at[part, :], sem.at[i]))
        copies[-1].start()
    order.wait()
    source = lax.broadcasted_iota(jnp.int32, (COLS, COLS), 0)
    selector = jnp.where(source == perm_ref[...], 1.0, 0.0).astype(BF16)
    for i, copy in enumerate(copies):
        copy.wait()
        part = slice(i * half, (i + 1) * half)
        moved = jnp.dot(e_ref[part, :], selector, preferred_element_type=F32)
        x_ref[:, part] = jnp.transpose(moved[:, :LIVE]).astype(BF16)
        lead_ref[part, :] = moved[:, :LIVE].astype(BF16)
        rest_ref[part, :] = moved[:, LIVE:].astype(BF16)


def permute(eigvecs, perm):
    rows = eigvecs.shape[0]
    return pl.pallas_call(
        permute_kernel,
        in_specs=[HB, HB],
        out_specs=[VM] * 3,
        out_shape=[
            pltpu.VMEM((LIVE, rows), BF16),
            pltpu.VMEM((rows, LIVE), BF16),
            pltpu.VMEM((rows, COLS - LIVE), BF16),
        ],
        scratch_shapes=[
            pltpu.VMEM(eigvecs.shape, BF16),
            pltpu.VMEM(perm.shape, jnp.int32),
            pltpu.SemaphoreType.DMA((3,)),
        ],
        name="permute",
        compiler_params=params(8),
        cost_estimate=TINY,
    )(eigvecs, perm)


def table_kernel(counts_hbm, poles_hbm, weights_hbm, p_ref, f_ref, poles_ref, weights_ref, counts_ref, sem):
    first = pltpu.make_async_copy(poles_hbm, poles_ref, sem.at[0])
    second = pltpu.make_async_copy(weights_hbm, weights_ref, sem.at[1])
    third = pltpu.make_async_copy(counts_hbm, counts_ref, sem.at[2])
    third.start()
    first.start()
    second.start()
    third.wait()
    first.wait()
    second.wait()
    span, keep = COLS // LANES, LIVE // LANES
    at = lax.broadcasted_iota(jnp.int32, (keep, LANES), 0) * LANES
    at = at + lax.broadcasted_iota(jnp.int32, (keep, LANES), 1)
    for block in range(counts_ref.shape[0]):
        rows = slice(keep * block, keep * (block + 1))
        here = slice(span * block, span * block + keep)
        p_ref[rows, :] = poles_ref[here, :]
        f_ref[rows, :] = jnp.where(at < counts_ref[block], weights_ref[here, :], 0.0)


def tables(counts, poles, weights):
    shape = (counts.shape[0] * LIVE // LANES, LANES)
    return pl.pallas_call(
        table_kernel,
        in_specs=[HB, HB, HB],
        out_specs=[VM, VM],
        out_shape=[pltpu.VMEM(shape, F32)] * 2,
        scratch_shapes=[pltpu.VMEM(poles.shape, F32)] * 2
        + [pltpu.SMEM(counts.shape, jnp.int32), pltpu.SemaphoreType.DMA((3,))],
        name="tables",
        compiler_params=params(4),
        cost_estimate=TINY,
    )(counts, poles, weights)


def join_kernel(a_ref, b_ref, o_ref):
    o_ref[:, :COLS] = a_ref[...]
    o_ref[:, COLS:] = b_ref[...]


def join(a, b):
    return pl.pallas_call(
        join_kernel,
        in_specs=[VM, VM],
        out_specs=VM,
        out_shape=pltpu.VMEM((1, 2 * COLS), F32),
        name="join",
        compiler_params=params(4),
        cost_estimate=TINY,
    )(a, b)


def column(row):
    return jnp.transpose(jnp.broadcast_to(row, (8, LIVE)))[:, :1]


def cauchy_kernel(fc, pieces, me_ref, poles_ref, factors_ref, *refs):
    r_refs, c_ref = refs[:-1], refs[-1]
    me = me_ref[0]
    core, z = (me // 16) % 2, (me // 2) % ZS
    step = 1 - 2 * core
    for j in range(XS):
        roots = column(r_refs[j][:, fc * COLS : fc * COLS + LIVE])
        for t in range(LIVE // TILE):
            own = jnp.broadcast_to(roots[t * TILE : (t + 1) * TILE], (TILE, LANES))
            rows = slice(j * LIVE + t * TILE, j * LIVE + (t + 1) * TILE)
            for i, d in enumerate(pieces):
                ring = (z - step * AWAY[d] + ZS) % ZS
                block = me + 2 * (ring - z)
                if d >= 8:
                    block = block + 16 * step
                for h in range(TILES):
                    at = pl.ds(TILES * block + h, 1)
                    value = factors_ref[at, :] / (poles_ref[at, :] - own)
                    lo = (TILES * i + h) * LANES
                    c_ref[rows, lo : lo + LANES] = value.astype(BF16)


def cauchy(fc, pieces, me, poles, factors, roots):
    return pl.pallas_call(
        lambda *refs: cauchy_kernel(fc, pieces, *refs),
        in_specs=[SM] + [VM] * (2 + XS),
        out_specs=VM,
        out_shape=pltpu.VMEM((XS * LIVE, len(pieces) * LIVE), BF16),
        name="cauchy",
        compiler_params=params(8),
        cost_estimate=TINY,
    )(me, poles, factors, *roots)


def norm_kernel(me_ref, counts_ref, poles_ref, factors_ref, r_ref, rest_ref, n_ref, live_ref, o_hbm, sem):
    copy = pltpu.make_async_copy(rest_ref, o_hbm.at[:, pl.ds(LIVE, COLS - LIVE)], sem.at[0])
    copy.start()
    within = lax.broadcasted_iota(jnp.int32, (8, LIVE), 1)
    live_ref[...] = jnp.where(within < counts_ref[me_ref[0]], 1.0, 0.0)
    roots = column(r_ref[:, :LIVE])
    group = 16
    for t in range(LIVE // TILE):
        own = jnp.broadcast_to(roots[t * TILE : (t + 1) * TILE], (TILE, LANES))

        def step(g, total):
            for u in range(group):
                at = pl.ds(g * group + u, 1)
                value = factors_ref[at, :] / (poles_ref[at, :] - own)
                total = total + value * value
            return total

        total = lax.fori_loop(0, poles_ref.shape[0] // group, step, jnp.zeros((TILE, LANES), F32))
        norm = jnp.sqrt(jnp.sum(total, axis=1, keepdims=True))
        n_ref[t * TILE : (t + 1) * TILE, :] = jnp.broadcast_to(norm, (TILE, LANES))
    copy.wait()


def norms(me, counts, poles, factors, roots, rest):
    return pl.pallas_call(
        norm_kernel,
        in_specs=[SM, SM] + [VM] * 4,
        out_specs=[VM, VM, HB],
        out_shape=[
            pltpu.VMEM((LIVE, LANES), F32),
            pltpu.VMEM((8, LIVE), F32),
            jax.ShapeDtypeStruct((rest.shape[0], COLS), BF16),
        ],
        scratch_shapes=[pltpu.SemaphoreType.DMA((1,))],
        name="norms",
        compiler_params=params(4),
        cost_estimate=TINY,
    )(me, counts, poles, factors, roots, rest)


def product(c_ref, j, first, x_refs):
    total = None
    for i, x_ref in enumerate(x_refs):
        lo = (first + i) * LIVE
        part = c_ref[j * LIVE : (j + 1) * LIVE, lo : lo + LIVE]
        piece = jnp.dot(part, x_ref[...], preferred_element_type=F32)
        total = piece if total is None else total + piece
    return total


def stage_kernel(first, count, c_mine, c_other, *refs):
    x_refs, refs = refs[:count], refs[count:]
    sums, outs = refs[:-2], refs[-2:]
    for i, c_ref in enumerate((c_mine, c_other)):
        for j in range(XS):
            rows = slice(j * LIVE, (j + 1) * LIVE)
            total = product(c_ref, j, first, x_refs)
            if sums:
                total = total + sums[i][rows, :]
            outs[i][rows, :] = total.astype(outs[i].dtype)


def stage(first, c_mine, c_other, pieces, sums, last):
    shape = (XS * LIVE, pieces[0].shape[1])
    return pl.pallas_call(
        lambda *refs: stage_kernel(first, len(pieces), *refs),
        in_specs=[VM] * (2 + len(pieces) + len(sums)),
        out_specs=[VM] * 2,
        out_shape=[pltpu.VMEM(shape, F32), pltpu.VMEM(shape, BF16 if last else F32)],
        name="stage",
        compiler_params=params(8),
        cost_estimate=TINY,
    )(c_mine, c_other, *pieces, *sums)


def add_kernel(at, c_ref, *refs):
    x_refs, sum_refs, o_ref = refs[: len(at)], refs[len(at) : -1], refs[-1]
    for j in range(XS):
        rows = slice(j * LIVE, (j + 1) * LIVE)
        total = sum_refs[0][rows, :]
        for sum_ref in sum_refs[1:]:
            total = total + sum_ref[rows, :].astype(F32)
        for i, x_ref in zip(at, x_refs, strict=True):
            total = total + product(c_ref, j, i, (x_ref,))
        o_ref[rows, :] = total


def add(at, c_mine, pieces, sums, estimate):
    return pl.pallas_call(
        lambda *refs: add_kernel(at, *refs),
        in_specs=[VM] * (1 + len(at) + len(sums)),
        out_specs=VM,
        out_shape=pltpu.VMEM(sums[0].shape, F32),
        name="add",
        compiler_params=params(8),
        cost_estimate=estimate,
    )(c_mine, *pieces, *sums)


def total_kernel(c_ref, x_ref, mine_ref, other_ref, own_ref, *out_refs):
    for j, out_ref in enumerate((own_ref, *out_refs)):
        rows = slice(j * LIVE, (j + 1) * LIVE)
        total = product(c_ref, j, 9, (x_ref,))
        total = total + mine_ref[rows, :] + other_ref[rows, :].astype(F32)
        out_ref[...] = total.astype(out_ref.dtype)


def totals(c_mine, sibling, mine, other):
    shape = (LIVE, mine.shape[1])
    return pl.pallas_call(
        total_kernel,
        in_specs=[VM] * 4,
        out_specs=[VM] * XS,
        out_shape=[pltpu.VMEM(shape, F32)] + [pltpu.VMEM(shape, BF16)] * (XS - 1),
        name="totals",
        compiler_params=params(8),
        cost_estimate=TINY,
    )(c_mine, sibling, mine, other)


def finish_kernel(own_ref, a_ref, b_ref, c_ref, n_ref, live_ref, lead_ref, _, o_hbm, buffer, sem):
    retain = live_ref[:1, :] > 0.5
    norm = n_ref[:, :1]
    size = buffer.shape[0] // 4
    copies = []
    for i in range(4):
        part = slice(i * size, (i + 1) * size)
        total = own_ref[:, part] + a_ref[:, part].astype(F32)
        total = total + b_ref[:, part].astype(F32) + c_ref[:, part].astype(F32)
        updated = jnp.transpose(total / norm)
        lead = lead_ref[part, :].astype(F32)
        buffer[part, :] = jnp.where(retain, updated, lead).astype(BF16)
        rows = pl.ds(i * size, size)
        copies.append(
            pltpu.make_async_copy(buffer.at[rows, :], o_hbm.at[rows, pl.ds(0, LIVE)], sem.at[i])
        )
        copies[-1].start()
    for copy in copies:
        copy.wait()


def finish(own, received, norm, live, lead, out):
    return pl.pallas_call(
        finish_kernel,
        in_specs=[VM] * (XS + 3) + [HB],
        out_specs=HB,
        out_shape=jax.ShapeDtypeStruct(out.shape, BF16),
        scratch_shapes=[pltpu.VMEM(lead.shape, BF16), pltpu.SemaphoreType.DMA((4,))],
        input_output_aliases={XS + 3: 0},
        name="finish",
        compiler_params=params(4),
        cost_estimate=TINY,
    )(own, *received, norm, live, lead, out)


def per_device(eigvecs, perm, counts, poles, weights, roots):
    me = lax.axis_index(("xl", "core", "z", "xh")).astype(jnp.int32).reshape(1)
    roots = roots.reshape(1, COLS)
    other_roots = cshift(roots)

    own, lead, rest = permute(in_hbm(eigvecs), in_hbm(perm.reshape(1, COLS)))
    p3 = around(own, 2)
    p2 = around(own, -1)
    p1 = around(own, 1)
    near = join(roots, hold(other_roots, own))
    far = [xshift(near, k) for k in (-1, -2, 1)]
    table, factors = tables(
        hold(in_hbm(counts), near), in_hbm(poles.reshape(-1, LANES)), in_hbm(weights.reshape(-1, LANES))
    )
    p4 = around(hold(p2, factors, *far), -1)
    p5 = around(hold(p3, *far), 1)
    c_other = cauchy(1, OTHER, me, table, factors, [hold(near, p3), *far])
    c_mine = cauchy(0, MINE, me, table, factors, [hold(near, c_other), *far])
    p6 = around(hold(p4, c_mine), -1)
    sums = stage(0, c_mine, c_other, (own, p2, p3), (), False)
    p7 = around(hold(p5, sums[0]), 1)
    mine, other = stage(3, c_mine, c_other, (p1, p4, p5), sums, True)
    other = cshift(other)
    p6 = hold(p6, mine)
    sibling = cshift(p7)
    mine = add((7,), c_mine, (p7,), (mine,), LONG)
    mine = add((6, 8), c_mine, (p6, cshift(p6)), (mine,), TINY)
    own_sum, *sent = totals(c_mine, sibling, mine, other)
    received = [xshift(sent[i], k) for i, k in ((0, 1), (2, -1), (1, 2))]
    norm, live, out = norms(me, counts, table, factors, hold(roots, own_sum), rest)
    return finish(own_sum, received, norm, live, lead, out)


def solution(mesh):
    fine_mesh = Mesh(mesh.devices.reshape(4, 2, 2, 8, 2), ("rows", "xl", "core", "z", "xh"))
    columns = ("xl", "core", "z", "xh")
    return jax.shard_map(
        per_device,
        mesh=fine_mesh,
        in_specs=(P("rows", columns), P(columns), P(), P(), P(), P(columns)),
        out_specs=P("rows", columns),
        check_vma=False,
    )
```

```python
import jax
import jax.numpy as jnp
from jax import lax
from jax.experimental import pallas as pl
from jax.experimental.pallas import tpu as pltpu
from jax.sharding import Mesh
from jax.sharding import PartitionSpec as P

LIVE = 256
COLS = 512
LANES = 128
TILES = LIVE // LANES
ZS = 8
XS = 4
TILE = 128
AWAY = (0, -1, 2, 1, -2, 3, -3, 4, 3, 4)
OTHER = range(6)
MINE = range(10)

VM = pl.BlockSpec(memory_space=pltpu.VMEM)
HB = pl.BlockSpec(memory_space=pltpu.HBM)
SM = pl.BlockSpec(memory_space=pltpu.SMEM)
F32 = jnp.float32
BF16 = jnp.bfloat16


def params(mib):
    return pltpu.CompilerParams(vmem_limit_bytes=mib << 20)


TINY = pl.CostEstimate(flops=1, transcendentals=0, bytes_accessed=1)
LONG = pl.CostEstimate(flops=10**10, transcendentals=0, bytes_accessed=1)


def xshift(a, k):
    pairs = []
    for i in range(XS):
        xl, xh = i // 2, i % 2
        x = (2 * xh + xl + k) % XS
        pairs.append((i, 2 * (x % 2) + x // 2))
    return lax.ppermute(a, ("xl", "xh"), pairs)


def around(a, way):
    up = [(z, (z + way) % ZS) for z in range(ZS)]
    down = [(ZS + z, ZS + (z - way) % ZS) for z in range(ZS)]
    return lax.ppermute(a, ("core", "z"), up + down)


def cshift(a):
    return lax.ppermute(a, "core", [(0, 1), (1, 0)])


def hold(a, *others):
    return lax.optimization_barrier((a, *others))[0]


def in_hbm(a):
    return pltpu.with_memory_space_constraint(a, pltpu.HBM)


def permute_kernel(e_hbm, perm_hbm, x_ref, lead_ref, rest_ref, e_ref, perm_ref, sem):
    rows = e_ref.shape[0]
    half = rows // 2
    order = pltpu.make_async_copy(perm_hbm, perm_ref, sem.at[2])
    order.start()
    copies = []
    for i in range(2):
        part = pl.ds(i * half, half)
        copies.append(pltpu.make_async_copy(e_hbm.at[part, :], e_ref.at[part, :], sem.at[i]))
        copies[-1].start()
    order.wait()
    source = lax.broadcasted_iota(jnp.int32, (COLS, COLS), 0)
    selector = jnp.where(source == perm_ref[...], 1.0, 0.0).astype(BF16)
    for i, copy in enumerate(copies):
        copy.wait()
        part = slice(i * half, (i + 1) * half)
        moved = jnp.dot(e_ref[part, :], selector, preferred_element_type=F32)
        x_ref[:, part] = jnp.transpose(moved[:, :LIVE]).astype(BF16)
        lead_ref[part, :] = moved[:, :LIVE].astype(BF16)
        rest_ref[part, :] = moved[:, LIVE:].astype(BF16)


def permute(eigvecs, perm):
    rows = eigvecs.shape[0]
    return pl.pallas_call(
        permute_kernel,
        in_specs=[HB, HB],
        out_specs=[VM] * 3,
        out_shape=[
            pltpu.VMEM((LIVE, rows), BF16),
            pltpu.VMEM((rows, LIVE), BF16),
            pltpu.VMEM((rows, COLS - LIVE), BF16),
        ],
        scratch_shapes=[
            pltpu.VMEM(eigvecs.shape, BF16),
            pltpu.VMEM(perm.shape, jnp.int32),
            pltpu.SemaphoreType.DMA((3,)),
        ],
        name="permute",
        compiler_params=params(8),
        cost_estimate=TINY,
    )(eigvecs, perm)


def table_kernel(counts_hbm, poles_hbm, weights_hbm, p_ref, f_ref, poles_ref, weights_ref, counts_ref, sem):
    first = pltpu.make_async_copy(poles_hbm, poles_ref, sem.at[0])
    second = pltpu.make_async_copy(weights_hbm, weights_ref, sem.at[1])
    third = pltpu.make_async_copy(counts_hbm, counts_ref, sem.at[2])
    third.start()
    first.start()
    second.start()
    third.wait()
    first.wait()
    second.wait()
    span, keep = COLS // LANES, LIVE // LANES
    at = lax.broadcasted_iota(jnp.int32, (keep, LANES), 0) * LANES
    at = at + lax.broadcasted_iota(jnp.int32, (keep, LANES), 1)
    for block in range(counts_ref.shape[0]):
        rows = slice(keep * block, keep * (block + 1))
        here = slice(span * block, span * block + keep)
        p_ref[rows, :] = poles_ref[here, :]
        f_ref[rows, :] = jnp.where(at < counts_ref[block], weights_ref[here, :], 0.0)


def tables(counts, poles, weights):
    shape = (counts.shape[0] * LIVE // LANES, LANES)
    return pl.pallas_call(
        table_kernel,
        in_specs=[HB, HB, HB],
        out_specs=[VM, VM],
        out_shape=[pltpu.VMEM(shape, F32)] * 2,
        scratch_shapes=[pltpu.VMEM(poles.shape, F32)] * 2
        + [pltpu.SMEM(counts.shape, jnp.int32), pltpu.SemaphoreType.DMA((3,))],
        name="tables",
        compiler_params=params(4),
        cost_estimate=TINY,
    )(counts, poles, weights)


def join_kernel(a_ref, b_ref, o_ref):
    o_ref[:, :COLS] = a_ref[...]
    o_ref[:, COLS:] = b_ref[...]


def join(a, b):
    return pl.pallas_call(
        join_kernel,
        in_specs=[VM, VM],
        out_specs=VM,
        out_shape=pltpu.VMEM((1, 2 * COLS), F32),
        name="join",
        compiler_params=params(4),
        cost_estimate=TINY,
    )(a, b)


def column(row):
    return jnp.transpose(jnp.broadcast_to(row, (8, LIVE)))[:, :1]


def cauchy_kernel(fc, pieces, me_ref, poles_ref, factors_ref, *refs):
    r_refs, c_ref = refs[:-1], refs[-1]
    me = me_ref[0]
    core, z = (me // 16) % 2, (me // 2) % ZS
    step = 1 - 2 * core
    for j in range(XS):
        roots = column(r_refs[j][:, fc * COLS : fc * COLS + LIVE])
        for t in range(LIVE // TILE):
            own = jnp.broadcast_to(roots[t * TILE : (t + 1) * TILE], (TILE, LANES))
            rows = slice(j * LIVE + t * TILE, j * LIVE + (t + 1) * TILE)
            for i, d in enumerate(pieces):
                ring = (z - step * AWAY[d] + ZS) % ZS
                block = me + 2 * (ring - z)
                if d >= 8:
                    block = block + 16 * step
                for h in range(TILES):
                    at = pl.ds(TILES * block + h, 1)
                    value = factors_ref[at, :] / (poles_ref[at, :] - own)
                    lo = (TILES * i + h) * LANES
                    c_ref[rows, lo : lo + LANES] = value.astype(BF16)


def cauchy(fc, pieces, me, poles, factors, roots):
    return pl.pallas_call(
        lambda *refs: cauchy_kernel(fc, pieces, *refs),
        in_specs=[SM] + [VM] * (2 + XS),
        out_specs=VM,
        out_shape=pltpu.VMEM((XS * LIVE, len(pieces) * LIVE), BF16),
        name="cauchy",
        compiler_params=params(8),
        cost_estimate=TINY,
    )(me, poles, factors, *roots)


def norm_kernel(me_ref, counts_ref, poles_ref, factors_ref, r_ref, rest_ref, n_ref, live_ref, o_hbm, sem):
    copy = pltpu.make_async_copy(rest_ref, o_hbm.at[:, pl.ds(LIVE, COLS - LIVE)], sem.at[0])
    copy.start()
    within = lax.broadcasted_iota(jnp.int32, (8, LIVE), 1)
    live_ref[...] = jnp.where(within < counts_ref[me_ref[0]], 1.0, 0.0)
    roots = column(r_ref[:, :LIVE])
    group = 16
    for t in range(LIVE // TILE):
        own = jnp.broadcast_to(roots[t * TILE : (t + 1) * TILE], (TILE, LANES))

        def step(g, total):
            for u in range(group):
                at = pl.ds(g * group + u, 1)
                value = factors_ref[at, :] / (poles_ref[at, :] - own)
                total = total + value * value
            return total

        total = lax.fori_loop(0, poles_ref.shape[0] // group, step, jnp.zeros((TILE, LANES), F32))
        norm = jnp.sqrt(jnp.sum(total, axis=1, keepdims=True))
        n_ref[t * TILE : (t + 1) * TILE, :] = jnp.broadcast_to(norm, (TILE, LANES))
    copy.wait()


def norms(me, counts, poles, factors, roots, rest):
    return pl.pallas_call(
        norm_kernel,
        in_specs=[SM, SM] + [VM] * 4,
        out_specs=[VM, VM, HB],
        out_shape=[
            pltpu.VMEM((LIVE, LANES), F32),
            pltpu.VMEM((8, LIVE), F32),
            jax.ShapeDtypeStruct((rest.shape[0], COLS), BF16),
        ],
        scratch_shapes=[pltpu.SemaphoreType.DMA((1,))],
        name="norms",
        compiler_params=params(4),
        cost_estimate=TINY,
    )(me, counts, poles, factors, roots, rest)


def product(c_ref, j, first, x_refs):
    total = None
    for i, x_ref in enumerate(x_refs):
        lo = (first + i) * LIVE
        part = c_ref[j * LIVE : (j + 1) * LIVE, lo : lo + LIVE]
        piece = jnp.dot(part, x_ref[...], preferred_element_type=F32)
        total = piece if total is None else total + piece
    return total


def stage_kernel(first, count, c_mine, c_other, *refs):
    x_refs, refs = refs[:count], refs[count:]
    sums, outs = refs[:-2], refs[-2:]
    for i, c_ref in enumerate((c_mine, c_other)):
        for j in range(XS):
            rows = slice(j * LIVE, (j + 1) * LIVE)
            total = product(c_ref, j, first, x_refs)
            if sums:
                total = total + sums[i][rows, :]
            outs[i][rows, :] = total.astype(outs[i].dtype)


def stage(first, c_mine, c_other, pieces, sums, last):
    shape = (XS * LIVE, pieces[0].shape[1])
    return pl.pallas_call(
        lambda *refs: stage_kernel(first, len(pieces), *refs),
        in_specs=[VM] * (2 + len(pieces) + len(sums)),
        out_specs=[VM] * 2,
        out_shape=[pltpu.VMEM(shape, F32), pltpu.VMEM(shape, BF16 if last else F32)],
        name="stage",
        compiler_params=params(8),
        cost_estimate=TINY,
    )(c_mine, c_other, *pieces, *sums)


def add_kernel(at, c_ref, *refs):
    x_refs, sum_refs, o_ref = refs[: len(at)], refs[len(at) : -1], refs[-1]
    for j in range(XS):
        rows = slice(j * LIVE, (j + 1) * LIVE)
        total = sum_refs[0][rows, :]
        for sum_ref in sum_refs[1:]:
            total = total + sum_ref[rows, :].astype(F32)
        for i, x_ref in zip(at, x_refs, strict=True):
            total = total + product(c_ref, j, i, (x_ref,))
        o_ref[rows, :] = total


def add(at, c_mine, pieces, sums, estimate):
    return pl.pallas_call(
        lambda *refs: add_kernel(at, *refs),
        in_specs=[VM] * (1 + len(at) + len(sums)),
        out_specs=VM,
        out_shape=pltpu.VMEM(sums[0].shape, F32),
        name="add",
        compiler_params=params(8),
        cost_estimate=estimate,
    )(c_mine, *pieces, *sums)


def total_kernel(c_ref, x_ref, mine_ref, other_ref, own_ref, *out_refs):
    for j, out_ref in enumerate((own_ref, *out_refs)):
        rows = slice(j * LIVE, (j + 1) * LIVE)
        total = product(c_ref, j, 9, (x_ref,))
        total = total + mine_ref[rows, :] + other_ref[rows, :].astype(F32)
        out_ref[...] = total.astype(out_ref.dtype)


def totals(c_mine, sibling, mine, other):
    shape = (LIVE, mine.shape[1])
    return pl.pallas_call(
        total_kernel,
        in_specs=[VM] * 4,
        out_specs=[VM] * XS,
        out_shape=[pltpu.VMEM(shape, F32)] + [pltpu.VMEM(shape, BF16)] * (XS - 1),
        name="totals",
        compiler_params=params(8),
        cost_estimate=TINY,
    )(c_mine, sibling, mine, other)


def gather_kernel(own_ref, a_ref, b_ref, n_ref, o_ref):
    o_ref[...] = (own_ref[...] + a_ref[...].astype(F32) + b_ref[...].astype(F32)) / n_ref[:, :1]


def add_near(own, a, b, norm):
    return pl.pallas_call(
        gather_kernel,
        in_specs=[VM] * 4,
        out_specs=VM,
        out_shape=pltpu.VMEM(own.shape, F32),
        name="add_near",
        compiler_params=params(4),
        cost_estimate=TINY,
    )(own, a, b, norm)


def finish_kernel(own_ref, c_ref, n_ref, live_ref, lead_ref, _, o_hbm, buffer, sem):
    retain = live_ref[:1, :] > 0.5
    norm = n_ref[:, :1]
    size = buffer.shape[0] // 4
    copies = []
    for i in range(4):
        part = slice(i * size, (i + 1) * size)
        updated = jnp.transpose(own_ref[:, part] + c_ref[:, part].astype(F32) / norm)
        lead = lead_ref[part, :].astype(F32)
        buffer[part, :] = jnp.where(retain, updated, lead).astype(BF16)
        rows = pl.ds(i * size, size)
        copies.append(
            pltpu.make_async_copy(buffer.at[rows, :], o_hbm.at[rows, pl.ds(0, LIVE)], sem.at[i])
        )
        copies[-1].start()
    for copy in copies:
        copy.wait()


def finish(own, last, norm, live, lead, out):
    return pl.pallas_call(
        finish_kernel,
        in_specs=[VM] * 5 + [HB],
        out_specs=HB,
        out_shape=jax.ShapeDtypeStruct(out.shape, BF16),
        scratch_shapes=[pltpu.VMEM(lead.shape, BF16), pltpu.SemaphoreType.DMA((4,))],
        input_output_aliases={5: 0},
        name="finish",
        compiler_params=params(4),
        cost_estimate=TINY,
    )(own, last, norm, live, lead, out)


def per_device(eigvecs, perm, counts, poles, weights, roots):
    me = lax.axis_index(("xl", "core", "z", "xh")).astype(jnp.int32).reshape(1)
    roots = roots.reshape(1, COLS)
    other_roots = cshift(roots)

    own, lead, rest = permute(in_hbm(eigvecs), in_hbm(perm.reshape(1, COLS)))
    p3 = around(own, 2)
    p2 = around(own, -1)
    p1 = around(own, 1)
    near = join(roots, hold(other_roots, own))
    far = [xshift(near, k) for k in (-1, -2, 1)]
    table, factors = tables(
        hold(in_hbm(counts), near), in_hbm(poles.reshape(-1, LANES)), in_hbm(weights.reshape(-1, LANES))
    )
    p4 = around(hold(p2, factors, *far), -1)
    p5 = around(hold(p3, *far), 1)
    c_other = cauchy(1, OTHER, me, table, factors, [hold(near, p3), *far])
    c_mine = cauchy(0, MINE, me, table, factors, [hold(near, c_other), *far])
    p6 = around(hold(p4, c_mine), -1)
    sums = stage(0, c_mine, c_other, (own, p2, p3), (), False)
    p7 = around(hold(p5, sums[0]), 1)
    mine, other = stage(3, c_mine, c_other, (p1, p4, p5), sums, True)
    other = cshift(other)
    p6 = hold(p6, mine)
    sibling = cshift(p7)
    mine = add((7,), c_mine, (p7,), (mine,), LONG)
    mine = add((6, 8), c_mine, (p6, cshift(p6)), (mine,), TINY)
    own_sum, *sent = totals(c_mine, sibling, mine, other)
    received = [xshift(sent[i], k) for i, k in ((0, 1), (2, -1), (1, 2))]
    norm, live, out = norms(me, counts, table, factors, hold(roots, own_sum), rest)
    own_sum = add_near(own_sum, received[0], received[1], norm)
    return finish(own_sum, received[2], norm, live, lead, out)


def solution(mesh):
    fine_mesh = Mesh(mesh.devices.reshape(4, 2, 2, 8, 2), ("rows", "xl", "core", "z", "xh"))
    columns = ("xl", "core", "z", "xh")
    return jax.shard_map(
        per_device,
        mesh=fine_mesh,
        in_specs=(P("rows", columns), P(columns), P(), P(), P(), P(columns)),
        out_specs=P("rows", columns),
        check_vma=False,
    )
```
